32 devices in a mesh: rep: 4 (over y, core), fsdp: 8 (over z, x).
Axes of the slice: x: 2, y: 2, z: 4, core: 2. Of those that a mesh axis runs over, the one named last changes fastest.
Arguments:
- inputs: bfloat16 [4096, 1024], P(('rep', 'fsdp')), may hold values from -6 to 6
- first_values: bfloat16 [4096, 1024], P(('rep', 'fsdp')), may hold values from -6 to 6
- prefix: int32 [4], replicated, may hold values from 102 to 512
- positions: int32 [4096], P(('rep', 'fsdp')), may hold values from 0 to 1023, as said below
- first_gain: bfloat16 [1024], P('fsdp'), may hold values from 0.25 to 1.75
- query_weight: bfloat16 [1024, 1024], P('fsdp'), may hold values from -0.1875 to 0.1875
- key_weight: bfloat16 [1024, 1024], P('fsdp'), may hold values from -0.1875 to 0.1875
- value_weight: bfloat16 [1024, 1024], P('fsdp'), may hold values from -0.1875 to 0.1875
- output_weight: bfloat16 [1024, 1024], P('fsdp'), may hold values from -1.5 to 1.5
- second_gain: bfloat16 [1024], P('fsdp'), may hold values from 0.25 to 1.75
- gate_weight: bfloat16 [1024, 2816], P('fsdp'), may hold values from -0.1875 to 0.1875
- up_weight: bfloat16 [1024, 2816], P('fsdp'), may hold values from -0.1875 to 0.1875
- down_weight: bfloat16 [2816, 1024], P('fsdp'), may hold values from -0.109375 to 0.109375
- cotangent: bfloat16 [4096, 1024], P(('rep', 'fsdp')), may hold values from -6 to 6
Outputs:
- layer_output: bfloat16 [4096, 1024], P(('rep', 'fsdp'))
- input_grad: float32 [4096, 1024], P(('rep', 'fsdp'))
- first_values_grad: float32 [4096, 1024], P(('rep', 'fsdp'))
- first_gain_grad: float32 [1024], P('fsdp')
- query_weight_grad: float32 [1024, 1024], P('fsdp')
- key_weight_grad: float32 [1024, 1024], P('fsdp')
- value_weight_grad: float32 [1024, 1024], P('fsdp')
- output_weight_grad: float32 [1024, 1024], P('fsdp')
- second_gain_grad: float32 [1024], P('fsdp')
- gate_weight_grad: float32 [1024, 2816], P('fsdp')
- up_weight_grad: float32 [1024, 2816], P('fsdp')
- down_weight_grad: float32 [2816, 1024], P('fsdp')
The draws below stay inside these ranges and needn't reach their ends.
Inputs may be any that keep to these rules, and one draw needn't show every extreme that they name: Within each sequence every position 0 to 1023 appears once; the rows of one device are two runs of 64 consecutive rising positions.
All inputs are finite; a program needn't handle non-finite values.
Results may differ from the reference program's by a relative error of at most 0.019.
Values may be sent and summed in bfloat16 or wider, within the bound.
A program may use at most 256 MiB of HBM per device.

```python
import math
import jax
import jax.numpy as jnp
from jax import lax

D = 1024
H = 16
E = 64
FF = 2816
TOK_DEV = 128
SEQ_LEN = 1024
SEQS = 4
TOKENS = 4096


def draw_positions(key, part):
    groups = TOKENS // SEQ_LEN
    half_rows = TOK_DEV // 2
    pieces = SEQ_LEN // half_rows

    def one_group(group_index):
        block_order = jax.random.permutation(jax.random.fold_in(key, group_index), pieces)
        return (block_order[:, None] * half_rows + jnp.arange(half_rows)[None, :]).reshape(-1)
    return jax.vmap(one_group)(jnp.arange(groups)).reshape(-1).astype(jnp.int32)


def touch_ends(array, key, smallest, top_value):
    dims = array.shape
    place = [jax.random.randint(jax.random.fold_in(key, axis), (), 0, dims[axis]) for axis in range(len(dims))]
    array = array.at[tuple(place)].set(smallest)
    longest = dims.index(max(dims))
    place[longest] = (place[longest] + 1) % dims[longest]
    return array.at[tuple(place)].set(top_value)


def level_of(stream_key, shape, split, least, high):
    loudness, own = 1.0, jax.random.fold_in(stream_key, 6)
    for position, parts in split:
        steps = jnp.exp(jax.random.uniform(jax.random.fold_in(own, position), (parts,), jnp.float32, least / len(split), high / len(split)))
        loudness = loudness * jnp.repeat(steps, shape[position] // parts).reshape([-1 if axis == position else 1 for axis in range(len(shape))])
    return loudness


def gaussian(rng, dims, width, reach, shards=(), held_as=jnp.bfloat16):
    values = jax.random.normal(rng, dims, jnp.float32) * width
    if len(shards) > 0:
        values = level_of(rng, dims, shards, -0.22, 0.18) * values
    return jnp.clip(values, min=-reach, max=reach).astype(held_as)


def setup_inputs(seed: int = 0) -> dict:
    arg_keys = jax.random.split(jax.random.key(seed), 15)
    return {
        "inputs": gaussian(arg_keys[0], (TOKENS, D), 1.0, 6.0, ((0, 32),)),
        "first_values": gaussian(arg_keys[1], (TOKENS, D), 1.0, 6.0, ((0, 32),)),
        "prefix": touch_ends(jax.random.randint(arg_keys[2], (SEQS,), SEQ_LEN // 10, SEQ_LEN // 2 + 1), jax.random.fold_in(arg_keys[2], 1), SEQ_LEN // 10, (SEQ_LEN // 2 + 1) - 1).astype(jnp.int32),
        "positions": draw_positions(jax.random.fold_in(arg_keys[14], 71), 0),
        "first_gain": jnp.clip(1.0 + 0.15 * jax.random.normal(arg_keys[4], (D,), jnp.float32), 0.25, 1.75).astype(jnp.bfloat16),
        "query_weight": gaussian(arg_keys[5], (D, D), D ** -0.5, 0.1875, ((0, 8),)),
        "key_weight": gaussian(arg_keys[6], (D, D), D ** -0.5, 0.1875, ((0, 8),)),
        "value_weight": gaussian(arg_keys[7], (D, D), D ** -0.5, 0.1875, ((0, 8),)),
        "output_weight": gaussian(arg_keys[8], (D, D), (max(1, D * 16 // SEQ_LEN)) ** -0.5, 1.5, ((0, 8),)),
        "second_gain": jnp.clip(1.0 + 0.15 * jax.random.normal(arg_keys[9], (D,), jnp.float32), 0.25, 1.75).astype(jnp.bfloat16),
        "gate_weight": gaussian(arg_keys[10], (D, FF), D ** -0.5, 0.1875, ((0, 8),)),
        "up_weight": gaussian(arg_keys[11], (D, FF), D ** -0.5, 0.1875, ((0, 8),)),
        "down_weight": gaussian(arg_keys[12], (FF, D), FF ** -0.5, 0.109375, ((0, 8),)),
        "cotangent": gaussian(arg_keys[13], (TOKENS, D), 1.0, 6.0, ((0, 32),)),
    }


epsilon = 1e-06
masked_score = -1e+30
highest = lax.Precision.HIGHEST

@jax.custom_vjp
def low(v):
    return lax.optimization_barrier(v.astype(jnp.bfloat16)).astype(jnp.float32)

@jax.custom_vjp
def low_back(v):
    return v

def low_keep(v):
    return (low(v), None)

def low_pass(kept, grad):
    return (grad,)

def back_keep(v):
    return (v, None)

def back_low(kept, grad):
    return (low(grad),)
low.defvjp(low_keep, low_pass)
low_back.defvjp(back_keep, back_low)

def rms_scale(values):
    return lax.rsqrt(lax.optimization_barrier(jnp.mean(values * values, axis=-1, keepdims=True)) + epsilon)

def rope_tables(places):
    half_width = E // 2
    frequency = jnp.exp(jnp.arange(half_width, dtype=jnp.float32) * (-math.log(10000.0) / half_width))
    angles = places.astype(jnp.float32)[:, None] * frequency[None, :]
    return (jnp.cos(angles)[:, None, :], jnp.sin(angles)[:, None, :])

def rope_apply(shaped, cosine, sine_table):
    half_width = shaped.shape[-1] // 2
    first_half = shaped[..., :half_width]
    second_half = shaped[..., half_width:]
    return jnp.concatenate([first_half * cosine - second_half * sine_table, second_half * cosine + first_half * sine_table], axis=-1)

def layer_forward(seq_rows, first_rows, first_gain, query_weight, key_weight, value_weight, output_weight, second_gain, gate_weight, up_weight, down_weight, places, prefix_length):
    length = seq_rows.shape[0]
    normed_one = seq_rows * rms_scale(seq_rows)
    hidden_one = low(normed_one * first_gain)
    query_pre = low_back(jnp.dot(hidden_one, query_weight, precision=highest))
    key_pre = low_back(jnp.dot(hidden_one, key_weight, precision=highest))
    value_pre = low_back(jnp.dot(hidden_one, value_weight, precision=highest))
    cosine, sine_table = rope_tables(places)
    queries = low(rope_apply(query_pre.reshape(length, H, E), cosine, sine_table))
    key_rows = low(rope_apply(key_pre.reshape(length, H, E), cosine, sine_table))
    mixed_values = low(0.5 * value_pre + 0.5 * first_rows).reshape(length, H, E)
    limits = jnp.maximum(places, prefix_length - 1)
    size_now = min(512, length)

    def attend(blocks):
        query_block, limit_block = blocks
        scores = low_back(jnp.einsum('qhe,khe->hqk', query_block, key_rows, precision=highest) * E ** (-0.5))
        allowed = places[None, None, :] <= limit_block[None, :, None]
        scores = jnp.where(allowed, scores, masked_score)
        row_max = lax.optimization_barrier(jnp.max(scores, axis=-1, keepdims=True))
        weights = jnp.exp(scores - row_max)
        probabilities = low(weights / lax.optimization_barrier(jnp.sum(weights, axis=-1, keepdims=True)))
        return jnp.einsum('hqk,khe->qhe', probabilities, mixed_values, precision=highest)
    attended = lax.map(jax.checkpoint(attend), (queries.reshape(length // size_now, size_now, H, E), limits.reshape(length // size_now, size_now)))
    attended = low(low_back(attended.reshape(length, D)))
    middle = seq_rows + low_back(jnp.dot(attended, output_weight, precision=highest))
    normed_two = middle * rms_scale(middle)
    hidden_two = low(normed_two * second_gain)
    gate_pre = low_back(jnp.dot(hidden_two, gate_weight, precision=highest))
    up_pre = low_back(jnp.dot(hidden_two, up_weight, precision=highest))
    activated = low(jax.nn.silu(gate_pre) * up_pre)
    return middle + low_back(jnp.dot(activated, down_weight, precision=highest))

def reference(inputs, first_values, prefix, positions, first_gain, query_weight, key_weight, value_weight, output_weight, second_gain, gate_weight, up_weight, down_weight, cotangent):
    params = tuple((item.astype(jnp.float32) for item in (first_gain, query_weight, key_weight, value_weight, output_weight, second_gain, gate_weight, up_weight, down_weight)))
    length = SEQ_LEN
    count = inputs.shape[0] // length
    seq_inputs = inputs.astype(jnp.float32).reshape(count, length, D)
    seq_firsts = first_values.astype(jnp.float32).reshape(count, length, D)
    seq_places = positions.reshape(count, length)
    seq_cotangent = cotangent.astype(jnp.float32).reshape(count, length, D)

    def one_sequence(totals, items):
        seq_rows, first_rows, places, prefix_length, seq_grad = items

        def forward(rows_in, firsts_in, *weights_in):
            return layer_forward(rows_in, firsts_in, *weights_in, places, prefix_length)
        result, pullback = jax.vjp(forward, seq_rows, first_rows, *params)
        gradients = pullback(seq_grad)
        totals = tuple((total + grad_now for total, grad_now in zip(totals, gradients[2:])))
        return (totals, (result, gradients[0], gradients[1]))
    start_totals = tuple((jnp.zeros(item.shape, jnp.float32) for item in params))
    totals, (results, input_grads, first_grads) = lax.scan(one_sequence, start_totals, (seq_inputs, seq_firsts, seq_places, prefix, seq_cotangent))
    return (results.reshape(-1, D).astype(jnp.bfloat16), input_grads.reshape(-1, D), first_grads.reshape(-1, D), totals[0], totals[1], totals[2], totals[3], totals[4], totals[5], totals[6], totals[7], totals[8])
```

```python
import functools
import math

import jax
import jax.numpy as jnp
from jax import lax
from jax.experimental import pallas as pl
from jax.experimental.pallas import tpu as pltpu
from jax.sharding import PartitionSpec as P

D = 1024
H = 16
E = 64


epsilon = 1e-06
masked_score = -1e30


def rms_scale(values):
    return lax.rsqrt(jnp.mean(values * values, axis=-1, keepdims=True) + epsilon)


def rope_tables(places):
    half_width = E // 2
    frequency = jnp.exp(
        jnp.arange(half_width, dtype=jnp.float32) * (-math.log(10000.0) / half_width)
    )
    angles = places.astype(jnp.float32)[:, None] * frequency[None, :]
    return (jnp.cos(angles)[:, None, :], jnp.sin(angles)[:, None, :])


def rope_apply(shaped, cosine, sine_table):
    half_width = shaped.shape[-1] // 2
    first_half = shaped[..., :half_width]
    second_half = shaped[..., half_width:]
    return jnp.concatenate(
        [
            first_half * cosine - second_half * sine_table,
            second_half * cosine + first_half * sine_table,
        ],
        axis=-1,
    )


def rope_undo(shaped, cosine, sine_table):
    half_width = shaped.shape[-1] // 2
    first_half = shaped[..., :half_width]
    second_half = shaped[..., half_width:]
    return jnp.concatenate(
        [
            first_half * cosine + second_half * sine_table,
            second_half * cosine - first_half * sine_table,
        ],
        axis=-1,
    )


def times_transposed(left, right):
    return lax.dot_general(
        left, right, (((1,), (1,)), ((), ())), preferred_element_type=jnp.float32
    )


def transposed_times(left, right):
    return lax.dot_general(
        left, right, (((0,), (0,)), ((), ())), preferred_element_type=jnp.float32
    )


def block_rows(count):
    size_now = count
    while size_now > 1024 and size_now % 2 == 0:
        size_now = size_now // 2
    return size_now


def split_blocks(array, size_now):
    return array.reshape((array.shape[0] // size_now, size_now) + array.shape[1:])


def masked_scores(queries, key_rows, limits, key_places):
    scores = jnp.einsum(
        "qhe,khe->hqk", queries, key_rows, preferred_element_type=jnp.float32
    ) * E ** (-0.5)
    allowed = key_places[None, None, :] <= limits[None, :, None]
    return (scores, allowed)


def grad_block(queries, key_rows, value_rows, limits, key_places, out_low, log_total, delta_rows):
    scores, allowed = masked_scores(queries, key_rows, limits, key_places)
    probabilities = jnp.where(allowed, jnp.exp(scores - log_total[:, :, None]), 0.0)
    prob_grad = jnp.einsum("qhe,khe->hqk", out_low, value_rows, preferred_element_type=jnp.float32)
    score_grad = (probabilities * (prob_grad - delta_rows[:, :, None])).astype(jnp.bfloat16)
    return (probabilities.astype(jnp.bfloat16), score_grad)


def norm_back(hidden_grad, normed, gain_float, scale_rows):
    normed_grad = hidden_grad * gain_float
    gain_term = jnp.sum(hidden_grad * normed, axis=0)
    rows_grad = scale_rows * (
        normed_grad - normed * jnp.mean(normed_grad * normed, axis=-1, keepdims=True)
    )
    return (gain_term, rows_grad)


def shards_general(
    inputs,
    first_values,
    prefix,
    positions,
    first_gain,
    query_weight,
    key_weight,
    value_weight,
    output_weight,
    second_gain,
    gate_weight,
    up_weight,
    down_weight,
    cotangent,
):
    token_count = inputs.shape[0]
    gain_one, query_full, key_full, value_full, output_full = (
        lax.all_gather(first_gain, "fsdp", axis=0, tiled=True),
        lax.all_gather(query_weight, "fsdp", axis=0, tiled=True),
        lax.all_gather(key_weight, "fsdp", axis=0, tiled=True),
        lax.all_gather(value_weight, "fsdp", axis=0, tiled=True),
        lax.all_gather(output_weight, "fsdp", axis=0, tiled=True),
    )
    all_places = lax.all_gather(positions, "fsdp", axis=0, tiled=True)
    prefix_here = lax.dynamic_index_in_dim(prefix, lax.axis_index("rep"), keepdims=False)
    own_limits = jnp.maximum(positions, prefix_here - 1)
    cosine, sine_table = rope_tables(positions)
    rows_float = inputs.astype(jnp.float32)
    scale_one = rms_scale(rows_float)
    normed_one = rows_float * scale_one
    gain_one_float = gain_one.astype(jnp.float32)
    hidden_one = (normed_one * gain_one_float).astype(jnp.bfloat16)
    query_pre = jnp.dot(hidden_one, query_full, preferred_element_type=jnp.float32)
    key_pre = jnp.dot(hidden_one, key_full, preferred_element_type=jnp.float32)
    value_pre = jnp.dot(hidden_one, value_full, preferred_element_type=jnp.float32)
    queries = rope_apply(query_pre.reshape(token_count, H, E), cosine, sine_table).astype(
        jnp.bfloat16
    )
    key_rows = (
        rope_apply(key_pre.reshape(token_count, H, E), cosine, sine_table)
        .astype(jnp.bfloat16)
        .reshape(token_count, D)
    )
    mixed_values = (0.5 * value_pre + 0.5 * first_values.astype(jnp.float32)).astype(jnp.bfloat16)
    start_state = (
        jnp.full((H, token_count), masked_score, jnp.float32),
        jnp.zeros((H, token_count), jnp.float32),
        jnp.zeros((token_count, H, E), jnp.float32),
    )
    running = start_state
    key_piece = lax.all_gather(key_rows, "fsdp", axis=0, tiled=True)
    value_piece = lax.all_gather(mixed_values, "fsdp", axis=0, tiled=True)
    count = key_piece.shape[0]
    size_now = block_rows(count)

    def forward_step(state_now, blocks):
        row_max, row_sum, accum = state_now
        key_block, value_block, place_block = blocks
        scores, allowed = masked_scores(
            queries, key_block.reshape(-1, H, E), own_limits, place_block
        )
        new_max = jnp.maximum(row_max, jnp.max(jnp.where(allowed, scores, masked_score), axis=-1))
        rescale = jnp.exp(row_max - new_max)
        weights = jnp.where(allowed, jnp.exp(scores - new_max[:, :, None]), 0.0)
        row_sum = row_sum * rescale + jnp.sum(weights, axis=-1)
        accum = accum * rescale.T[:, :, None] + jnp.einsum(
            "hqk,khe->qhe",
            weights.astype(jnp.bfloat16),
            value_block.reshape(-1, H, E),
            preferred_element_type=jnp.float32,
        )
        return ((new_max, row_sum, accum), None)

    running, unused = lax.scan(
        forward_step,
        running,
        (
            split_blocks(key_piece, size_now),
            split_blocks(value_piece, size_now),
            split_blocks(all_places, size_now),
        ),
    )
    row_max, row_sum, accum = running
    log_total = row_max + jnp.log(row_sum)
    attended = accum / row_sum.T[:, :, None]
    attended_low = attended.reshape(token_count, D).astype(jnp.bfloat16)
    middle = rows_float + jnp.dot(attended_low, output_full, preferred_element_type=jnp.float32)
    mlp_forward = (
        lax.all_gather(second_gain, "fsdp", axis=0, tiled=True),
        lax.all_gather(gate_weight, "fsdp", axis=0, tiled=True),
        lax.all_gather(up_weight, "fsdp", axis=0, tiled=True),
        lax.all_gather(down_weight, "fsdp", axis=0, tiled=True),
    )
    gain_two, gate_full, up_full, down_full = mlp_forward
    scale_two = rms_scale(middle)
    normed_two = middle * scale_two
    hidden_two = (normed_two * gain_two.astype(jnp.float32)).astype(jnp.bfloat16)
    gate_pre = jnp.dot(hidden_two, gate_full, preferred_element_type=jnp.float32)
    up_pre = jnp.dot(hidden_two, up_full, preferred_element_type=jnp.float32)
    sigmoid_gate = jax.nn.sigmoid(gate_pre)
    activated = (gate_pre * sigmoid_gate * up_pre).astype(jnp.bfloat16)
    layer_output = (
        middle + jnp.dot(activated, down_full, preferred_element_type=jnp.float32)
    ).astype(jnp.bfloat16)
    gain_two_back, gate_back, up_back, down_back = (
        lax.all_gather(second_gain, "fsdp", axis=0, tiled=True),
        lax.all_gather(gate_weight, "fsdp", axis=0, tiled=True),
        lax.all_gather(up_weight, "fsdp", axis=0, tiled=True),
        lax.all_gather(down_weight, "fsdp", axis=0, tiled=True),
    )
    act_grad = times_transposed(cotangent, down_back)
    down_term = transposed_times(activated, cotangent)
    gate_grad = (act_grad * up_pre * sigmoid_gate * (1.0 + gate_pre * (1.0 - sigmoid_gate))).astype(
        jnp.bfloat16
    )
    up_grad = (act_grad * gate_pre * sigmoid_gate).astype(jnp.bfloat16)
    hidden_two_grad = times_transposed(gate_grad, gate_back) + times_transposed(up_grad, up_back)
    gate_term = transposed_times(hidden_two, gate_grad)
    up_term = transposed_times(hidden_two, up_grad)
    gain_two_term, middle_part = norm_back(
        hidden_two_grad, normed_two, gain_two_back.astype(jnp.float32), scale_two
    )
    middle_grad = cotangent.astype(jnp.float32) + middle_part
    gain_two_sum, gate_sum, up_sum, down_sum = (
        lax.psum_scatter(gain_two_term, "fsdp", scatter_dimension=0, tiled=True),
        lax.psum_scatter(gate_term, "fsdp", scatter_dimension=0, tiled=True),
        lax.psum_scatter(up_term, "fsdp", scatter_dimension=0, tiled=True),
        lax.psum_scatter(down_term, "fsdp", scatter_dimension=0, tiled=True),
    )
    gain_one_back, query_back, key_back, value_back, output_back = (
        lax.all_gather(first_gain, "fsdp", axis=0, tiled=True),
        lax.all_gather(query_weight, "fsdp", axis=0, tiled=True),
        lax.all_gather(key_weight, "fsdp", axis=0, tiled=True),
        lax.all_gather(value_weight, "fsdp", axis=0, tiled=True),
        lax.all_gather(output_weight, "fsdp", axis=0, tiled=True),
    )
    branch_low = middle_grad.astype(jnp.bfloat16)
    output_term = transposed_times(attended_low, branch_low)
    out_flat = times_transposed(branch_low, output_back).astype(jnp.bfloat16)
    out_low = out_flat.reshape(token_count, H, E)
    delta_rows = jnp.sum(out_low.astype(jnp.float32) * attended, axis=-1).T
    zero_rows = jnp.zeros((token_count, H, E), jnp.float32)
    gathered_keys, gathered_values = (
        lax.all_gather(key_rows, "fsdp", axis=0, tiled=True),
        lax.all_gather(mixed_values, "fsdp", axis=0, tiled=True),
    )
    length = gathered_keys.shape[0]
    size_now = block_rows(length)

    def back_step(query_acc, blocks):
        key_block, value_block, place_block = blocks
        key_shaped = key_block.reshape(-1, H, E)
        value_shaped = value_block.reshape(-1, H, E)
        prob_low, score_grad = grad_block(
            queries,
            key_shaped,
            value_shaped,
            own_limits,
            place_block,
            out_low,
            log_total,
            delta_rows,
        )
        query_acc = query_acc + jnp.einsum(
            "hqk,khe->qhe", score_grad, key_shaped, preferred_element_type=jnp.float32
        )
        key_part = jnp.einsum(
            "hqk,qhe->khe", score_grad, queries, preferred_element_type=jnp.float32
        ).reshape(-1, D)
        value_part = jnp.einsum(
            "hqk,qhe->khe", prob_low, out_low, preferred_element_type=jnp.float32
        ).reshape(-1, D)
        return (query_acc, jnp.concatenate([key_part, value_part], axis=1))

    query_acc, parts = lax.scan(
        back_step,
        zero_rows,
        (
            split_blocks(gathered_keys, size_now),
            split_blocks(gathered_values, size_now),
            split_blocks(all_places, size_now),
        ),
    )
    summed = lax.psum_scatter(parts.reshape(length, 2 * D), "fsdp", scatter_dimension=0, tiled=True)
    key_acc = summed[:, :D]
    value_acc = summed[:, D:]
    query_grad = (
        rope_undo(query_acc * E ** (-0.5), cosine, sine_table)
        .reshape(token_count, D)
        .astype(jnp.bfloat16)
    )
    key_grad = (
        rope_undo(key_acc.reshape(token_count, H, E) * E ** (-0.5), cosine, sine_table)
        .reshape(token_count, D)
        .astype(jnp.bfloat16)
    )
    first_values_grad = 0.5 * value_acc
    value_grad = first_values_grad.astype(jnp.bfloat16)
    hidden_one_grad = (
        times_transposed(query_grad, query_back)
        + times_transposed(key_grad, key_back)
        + times_transposed(value_grad, value_back)
    )
    query_term = transposed_times(hidden_one, query_grad)
    key_term = transposed_times(hidden_one, key_grad)
    value_term = transposed_times(hidden_one, value_grad)
    gain_one_term, input_part = norm_back(
        hidden_one_grad, normed_one, gain_one_back.astype(jnp.float32), scale_one
    )
    input_grad = middle_grad + input_part
    gain_one_sum, query_sum, key_sum, value_sum, output_sum = (
        lax.psum_scatter(gain_one_term, "fsdp", scatter_dimension=0, tiled=True),
        lax.psum_scatter(query_term, "fsdp", scatter_dimension=0, tiled=True),
        lax.psum_scatter(key_term, "fsdp", scatter_dimension=0, tiled=True),
        lax.psum_scatter(value_term, "fsdp", scatter_dimension=0, tiled=True),
        lax.psum_scatter(output_term, "fsdp", scatter_dimension=0, tiled=True),
    )
    totals = (
        lax.psum(gain_one_sum.astype(jnp.bfloat16), "rep").astype(jnp.float32),
        lax.psum(query_sum.astype(jnp.bfloat16), "rep").astype(jnp.float32),
        lax.psum(key_sum.astype(jnp.bfloat16), "rep").astype(jnp.float32),
        lax.psum(value_sum.astype(jnp.bfloat16), "rep").astype(jnp.float32),
        lax.psum(output_sum.astype(jnp.bfloat16), "rep").astype(jnp.float32),
        lax.psum(gain_two_sum.astype(jnp.bfloat16), "rep").astype(jnp.float32),
        lax.psum(gate_sum.astype(jnp.bfloat16), "rep").astype(jnp.float32),
        lax.psum(up_sum.astype(jnp.bfloat16), "rep").astype(jnp.float32),
        lax.psum(down_sum.astype(jnp.bfloat16), "rep").astype(jnp.float32),
    )
    return (
        layer_output,
        input_grad,
        first_values_grad,
        totals[0],
        totals[1],
        totals[2],
        totals[3],
        totals[4],
        totals[5],
        totals[6],
        totals[7],
        totals[8],
    )


MESH = pl.DeviceIdType.MESH
LOW = jnp.bfloat16
WIDE = jnp.float32
VM = pl.BlockSpec(memory_space=pltpu.VMEM)
DMA = pltpu.SemaphoreType.DMA


def remote(src, dst, send_sem, recv_sem, rep, fsdp):
    return pltpu.make_async_remote_copy(
        src_ref=src,
        dst_ref=dst,
        send_sem=send_sem,
        recv_sem=recv_sem,
        device_id={"rep": rep, "fsdp": fsdp},
        device_id_type=MESH,
    )


def greet(peers):
    barrier = pltpu.get_barrier_semaphore()
    for rep, fsdp in peers:
        pl.semaphore_signal(
            barrier, inc=1, device_id={"rep": rep, "fsdp": fsdp}, device_id_type=MESH
        )
    pl.semaphore_wait(barrier, len(peers))


def plane_place():
    rep, fsdp = lax.axis_index("rep"), lax.axis_index("fsdp")
    return rep, fsdp, fsdp // 2, fsdp % 2


def gather_kernel(count, *refs):
    ins, outs = refs[:count], refs[count : 2 * count]
    local, send, recv = refs[2 * count :]
    rep, fsdp, z, x = plane_place()
    side = 2 * z + 1 - x
    others = [lax.rem(z + k, 4) for k in (1, 2, 3)]
    greet([(rep, 2 * other + x) for other in others] + [(rep, side)])
    started = []
    for i in range(count):
        for k, other in enumerate(others):
            copy = remote(
                ins[i], outs[i].at[fsdp], send.at[i, k], recv.at[i, fsdp], rep, 2 * other + x
            )
            copy.start()
            started.append(copy)
        copy = remote(ins[i], outs[i].at[fsdp], send.at[i, 3], recv.at[i, fsdp], rep, side)
        copy.start()
        started.append(copy)
    kept = []
    for i in range(count):
        copy = pltpu.make_async_copy(ins[i], outs[i].at[fsdp], local.at[i])
        copy.start()
        kept.append(copy)
    for k, other in enumerate((others[0], others[2], others[1])):
        for i in range(count):
            slot = 2 * other + x
            place = outs[i].at[slot]
            remote(place, place, send.at[i, 4 + k], recv.at[i, slot], rep, side).wait_recv()
            copy = remote(place, place, send.at[i, 4 + k], recv.at[i, slot], rep, side)
            copy.start()
            started.append(copy)
    for i in range(count):
        for other in range(4):
            slot = 2 * other + 1 - x
            place = outs[i].at[slot]
            remote(place, place, send.at[i, 0], recv.at[i, slot], rep, side).wait_recv()
    for copy in started:
        copy.wait_send()
    for copy in kept:
        copy.wait()


def gather_rows(name, *arrays):
    count = len(arrays)
    out = pl.pallas_call(
        functools.partial(gather_kernel, count),
        out_shape=[jax.ShapeDtypeStruct((8,) + a.shape, a.dtype) for a in arrays],
        in_specs=[VM] * count,
        out_specs=[VM] * count,
        scratch_shapes=[DMA((count,)), DMA((count, 7)), DMA((count, 8))],
        compiler_params=pltpu.CompilerParams(collective_id=name, has_side_effects=True),
    )(*arrays)
    return [a.reshape((8 * a.shape[1],) + a.shape[2:]) for a in out]


def scatter_kernel(part, out, side_in, summed, line_in, send, side_recv, line_recv):
    rep, fsdp, z, x = plane_place()
    side = 2 * z + 1 - x
    others = [lax.rem(z + k, 4) for k in (2, 1, 3)]
    greet([(rep, 2 * other + x) for other in others] + [(rep, side)])
    started = []
    for k, other in enumerate(others + [z]):
        copy = remote(
            part.at[2 * other + 1 - x], side_in.at[other], send.at[k], side_recv.at[other], rep, side
        )
        copy.start()
        started.append(copy)
    for k, other in enumerate(others):
        place = side_in.at[other]
        remote(place, place, send.at[k], side_recv.at[other], rep, side).wait_recv()
        summed[other] = (
            part[2 * other + x].astype(WIDE) + side_in[other].astype(WIDE)
        ).astype(LOW)
        copy = remote(
            summed.at[other], line_in.at[z], send.at[4 + k], line_recv.at[z], rep, 2 * other + x
        )
        copy.start()
        started.append(copy)
    place = side_in.at[z]
    remote(place, place, send.at[3], side_recv.at[z], rep, side).wait_recv()
    total = part[fsdp].astype(WIDE) + side_in[z].astype(WIDE)
    for k in (1, 2, 0):
        place = line_in.at[others[k]]
        remote(place, place, send.at[4 + k], line_recv.at[others[k]], rep, side).wait_recv()
        total = total + line_in[others[k]].astype(WIDE)
    out[...] = total
    for copy in started:
        copy.wait_send()


def scatter_rows(name, part):
    rows, width = part.shape[0] // 8, part.shape[1]
    return pl.pallas_call(
        scatter_kernel,
        out_shape=jax.ShapeDtypeStruct((rows, width), WIDE),
        in_specs=[VM],
        out_specs=VM,
        scratch_shapes=[
            pltpu.VMEM((4, rows, width), LOW),
            pltpu.VMEM((4, rows, width), LOW),
            pltpu.VMEM((4, rows, width), LOW),
            DMA((7,)),
            DMA((4,)),
            DMA((4,)),
        ],
        compiler_params=pltpu.CompilerParams(collective_id=name, has_side_effects=True),
    )(part.reshape(8, rows, width))


def spread_kernel(weights, values, weights_out, values_out, local, send, recv, pass_on, passed):
    rep, fsdp, z, x = plane_place()
    core = lax.rem(rep, 2)
    partner = rep + 1 - 2 * core
    others = [lax.rem(fsdp + k, 8) for k in range(1, 8)]
    greet([(rep, other) for other in others] + [(partner, fsdp)])
    half = weights.shape[1] // 2
    mine = pl.ds(pl.multiple_of(core * half, half), half)
    theirs = pl.ds(pl.multiple_of((1 - core) * half, half), half)
    started = []
    for k, other in enumerate(others):
        copy = remote(
            values.at[other], values_out.at[fsdp], send.at[1, k], recv.at[1, fsdp], rep, other
        )
        copy.start()
        started.append(copy)
    for k, other in enumerate(others):
        copy = remote(
            weights.at[other, mine],
            weights_out.at[fsdp, mine],
            send.at[0, k],
            recv.at[0, fsdp],
            rep,
            other,
        )
        copy.start()
        started.append(copy)
    kept = [
        pltpu.make_async_copy(weights.at[fsdp], weights_out.at[fsdp], local.at[0]),
        pltpu.make_async_copy(values.at[fsdp], values_out.at[fsdp], local.at[1]),
    ]
    for copy in kept:
        copy.start()
    for k, other in enumerate(others):
        place = weights_out.at[other, mine]
        remote(place, place, pass_on.at[k], recv.at[0, other], partner, fsdp).wait_recv()
        copy = remote(place, place, pass_on.at[k], passed.at[other], partner, fsdp)
        copy.start()
        started.append(copy)
    for k, other in enumerate(others):
        place = values_out.at[other]
        remote(place, place, pass_on.at[k], recv.at[1, other], partner, fsdp).wait_recv()
        place = weights_out.at[other, theirs]
        remote(place, place, pass_on.at[k], passed.at[other], partner, fsdp).wait_recv()
    for copy in started:
        copy.wait_send()
    for copy in kept:
        copy.wait()


def spread(name, weights, values):
    return pl.pallas_call(
        spread_kernel,
        out_shape=[jax.ShapeDtypeStruct(a.shape, a.dtype) for a in (weights, values)],
        in_specs=[VM, VM],
        out_specs=[VM, VM],
        scratch_shapes=[DMA((2,)), DMA((2, 7)), DMA((2, 8)), DMA((7,)), DMA((8,))],
        compiler_params=pltpu.CompilerParams(collective_id=name, has_side_effects=True),
    )(weights, values)


def collect_kernel(
    grads,
    rows,
    values,
    grads_out,
    rows_out,
    values_out,
    pair_in,
    pair_sum,
    level_in,
    level_sum,
    landed,
    row_pair_in,
    row_pair_sum,
    row_level_in,
    local,
    send,
    recv,
    cross_send,
    cross_recv,
    value_send,
    value_recv,
):
    rep, fsdp, z, x = plane_place()
    core, level = lax.rem(rep, 2), rep // 2
    partner = rep + 1 - 2 * core
    above = rep + 2 - 4 * level
    others = [lax.rem(fsdp + k, 8) for k in range(1, 8)]
    greet([(rep, other) for other in others] + [(partner, fsdp), (above, fsdp)])
    half = grads.shape[1] // 2
    fourth = half // 2
    row_half = rows.shape[1] // 2
    row_fourth = row_half // 2

    def piece(index, size):
        return pl.ds(pl.multiple_of(index * size, size), size)

    started = []

    def go(copy):
        copy.start()
        started.append(copy)

    go(
        remote(
            grads.at[:, piece(1 - core, half)], pair_in, send.at[0], recv.at[0], partner, fsdp
        )
    )
    go(
        remote(
            rows.at[:, piece(1 - core, row_half)],
            row_pair_in,
            send.at[1],
            recv.at[1],
            partner,
            fsdp,
        )
    )
    for k, other in enumerate(others):
        go(
            remote(
                values.at[other], values_out.at[fsdp], value_send.at[k], value_recv.at[fsdp], rep, other
            )
        )
    kept = pltpu.make_async_copy(values.at[fsdp], values_out.at[fsdp], local.at[0])
    kept.start()
    remote(pair_in, pair_in, send.at[0], recv.at[0], partner, fsdp).wait_recv()
    for i in range(8):
        pair_sum[i] = (
            grads[i, piece(core, half)].astype(WIDE) + pair_in[i].astype(WIDE)
        ).astype(LOW)
    go(
        remote(
            pair_sum.at[:, piece(1 - level, fourth)], level_in, send.at[2], recv.at[2], above, fsdp
        )
    )
    remote(row_pair_in, row_pair_in, send.at[1], recv.at[1], partner, fsdp).wait_recv()
    row_pair_sum[...] = (
        rows[:, piece(core, row_half)].astype(WIDE) + row_pair_in[...].astype(WIDE)
    ).astype(LOW)
    go(
        remote(
            row_pair_sum.at[:, piece(1 - level, row_fourth)],
            row_level_in,
            send.at[3],
            recv.at[3],
            above,
            fsdp,
        )
    )
    remote(level_in, level_in, send.at[2], recv.at[2], above, fsdp).wait_recv()
    for i in range(8):
        level_sum[i] = (
            pair_sum[i, piece(level, fourth)].astype(WIDE) + level_in[i].astype(WIDE)
        ).astype(LOW)
    for k, other in enumerate(others):
        go(
            remote(
                level_sum.at[other], landed.at[fsdp], cross_send.at[k], cross_recv.at[fsdp], rep, other
            )
        )
    quarter = piece(2 * core + level, fourth)
    row_quarter = piece(2 * core + level, row_fourth)
    remote(row_level_in, row_level_in, send.at[3], recv.at[3], above, fsdp).wait_recv()
    rows_out[:, row_quarter] = (
        row_pair_sum[:, piece(level, row_fourth)].astype(WIDE) + row_level_in[...].astype(WIDE)
    ).astype(LOW)
    place = rows_out.at[:, row_quarter]
    go(remote(place, place, send.at[4], recv.at[4], partner, fsdp))
    go(remote(place, place, send.at[5], recv.at[5], above, fsdp))
    landed[fsdp] = level_sum[fsdp]
    for k, other in enumerate(others):
        place = landed.at[other]
        remote(place, place, cross_send.at[k], cross_recv.at[other], rep, fsdp).wait_recv()
    for i in range(8):
        grads_out[i, quarter] = landed[i]
    place = grads_out.at[:, quarter]
    go(remote(landed, place, send.at[7], recv.at[7], above, fsdp))
    go(remote(landed, place, send.at[6], recv.at[6], partner, fsdp))
    quarter = piece(2 * core + 1 - level, fourth)
    row_quarter = piece(2 * core + 1 - level, row_fourth)
    place = rows_out.at[:, row_quarter]
    remote(place, place, send.at[5], recv.at[5], above, fsdp).wait_recv()
    go(remote(place, place, send.at[8], recv.at[8], partner, fsdp))
    place = grads_out.at[:, quarter]
    remote(place, place, send.at[7], recv.at[7], above, fsdp).wait_recv()
    go(remote(place, place, send.at[9], recv.at[9], partner, fsdp))
    quarter = piece(2 * (1 - core) + level, fourth)
    row_quarter = piece(2 * (1 - core) + level, row_fourth)
    place = rows_out.at[:, row_quarter]
    remote(place, place, send.at[4], recv.at[4], partner, fsdp).wait_recv()
    place = grads_out.at[:, quarter]
    remote(place, place, send.at[6], recv.at[6], partner, fsdp).wait_recv()
    quarter = piece(2 * (1 - core) + 1 - level, fourth)
    row_quarter = piece(2 * (1 - core) + 1 - level, row_fourth)
    place = rows_out.at[:, row_quarter]
    remote(place, place, send.at[8], recv.at[8], partner, fsdp).wait_recv()
    place = grads_out.at[:, quarter]
    remote(place, place, send.at[9], recv.at[9], partner, fsdp).wait_recv()
    for k, other in enumerate(others):
        place = values_out.at[other]
        remote(place, place, value_send.at[k], value_recv.at[other], rep, fsdp).wait_recv()
    for copy in started:
        copy.wait_send()
    kept.wait()


def collect(name, grads, rows, values):
    count, high, wide = grads.shape
    tall, across = rows.shape
    return pl.pallas_call(
        collect_kernel,
        out_shape=[jax.ShapeDtypeStruct(a.shape, a.dtype) for a in (grads, rows, values)],
        in_specs=[VM] * 3,
        out_specs=[VM] * 3,
        scratch_shapes=[
            pltpu.VMEM((count, high // 2, wide), LOW),
            pltpu.VMEM((count, high // 2, wide), LOW),
            pltpu.VMEM((count, high // 4, wide), LOW),
            pltpu.VMEM((count, high // 4, wide), LOW),
            pltpu.VMEM((count, high // 4, wide), LOW),
            pltpu.VMEM((tall, across // 2), LOW),
            pltpu.VMEM((tall, across // 2), LOW),
            pltpu.VMEM((tall, across // 4), LOW),
            DMA((1,)),
            DMA((10,)),
            DMA((10,)),
            DMA((7,)),
            DMA((8,)),
            DMA((7,)),
            DMA((8,)),
        ],
        compiler_params=pltpu.CompilerParams(collective_id=name, has_side_effects=True),
    )(grads, rows, values)


def to_blocks(array):
    rows, width = array.shape
    return array.reshape(rows, 8, width // 8).transpose(1, 0, 2)


def from_blocks(array):
    count, rows, width = array.shape
    return array.transpose(1, 0, 2).reshape(rows, count * width)


def matmul(left, right):
    return jnp.dot(left, right, preferred_element_type=WIDE)


def turn_tables(marks, block, cosine_step, sine_step):
    lanes = pl.ds(pl.multiple_of(block * 128, 128), 128)
    cosines, sines = [], []
    for run in range(2):
        c = marks[3 + 2 * run : 4 + 2 * run, lanes]
        s = marks[4 + 2 * run : 5 + 2 * run, lanes]
        cosines.append(c * cosine_step[...] - s * sine_step[...])
        sines.append(s * cosine_step[...] + c * sine_step[...])
    lane = lax.broadcasted_iota(jnp.int32, (1, 128), 1)
    sign = jnp.where(lane % E < E // 2, -1.0, 1.0)
    return jnp.concatenate(cosines, axis=0), jnp.concatenate(sines, axis=0) * sign


def turn(array, cosine, sine):
    lane = lax.broadcasted_iota(jnp.int32, (1, 128), 1)
    swapped = jnp.where(
        lane % E < E // 2, pltpu.roll(array, 96, 1), pltpu.roll(array, 32, 1)
    )
    return array * cosine + swapped * sine


def limit_column(marks, block, prefix):
    base = pl.multiple_of(block * 128, 128)
    tile = marks[0:1, pl.ds(base, 128)]
    lane = lax.broadcasted_iota(jnp.int32, (1, 128), 1)
    row = lax.broadcasted_iota(jnp.int32, (128, 1), 0)
    first = jnp.sum(jnp.where(lane == 0, tile, 0.0), axis=1, keepdims=True)
    second = jnp.sum(jnp.where(lane == 64, tile, 0.0), axis=1, keepdims=True)
    places = jnp.where(row < 64, first + row.astype(WIDE), second + (row - 64).astype(WIDE))
    return jnp.maximum(places, prefix)


def head_lanes(head):
    lane = lax.broadcasted_iota(jnp.int32, (1, 128), 1)
    return (lane // E) == head


def rows_of(block):
    return pl.ds(pl.multiple_of(block * 128, 128), 128)


def forward_kernel(
    rows,
    small,
    prefix,
    cosine_step,
    sine_step,
    query_weight,
    key_weight,
    value_weight,
    output_weight,
    firsts,
    cotangent,
    packed,
    hidden_one,
    queries,
    keys,
    values,
    attended,
    totals,
    weights,
    packed_full,
    grad_full,
    marks,
    middle,
    hidden_two,
    rows_full,
    firsts_full,
    part,
    side_in,
    summed,
    line_in,
    keep,
    w_send,
    w_recv,
    p_send,
    p_recv,
    s_send,
    s_recv,
    f_send,
    f_recv,
    x_send,
    x_recv,
    c_send,
    c_recv,
    m_send,
    m_recv,
    mp_send,
    mp_recv,
    r_send,
    side_recv,
    line_recv,
):
    rep, fsdp, z, x = plane_place()
    core = lax.rem(rep, 2)
    partner = rep + 1 - 2 * core
    side = 2 * z + 1 - x
    others = [lax.rem(fsdp + k, 8) for k in range(1, 8)]
    lines = [lax.rem(z + k, 4) for k in (1, 2, 3)]
    greet([(rep, other) for other in others] + [(partner, fsdp)])
    mine = pl.ds(pl.multiple_of(core * 64, 64), 64)
    theirs = pl.ds(pl.multiple_of(64 - core * 64, 64), 64)
    started, kept = [], []

    def go(copy):
        copy.start()
        started.append(copy)

    def here(src, dst):
        copy = pltpu.make_async_copy(src, dst, keep.at[len(kept)])
        copy.start()
        kept.append(copy)

    def arrived(place, sem):
        remote(place, place, sem, sem, rep, side).wait_recv()

    def part_of(block):
        return pl.ds(pl.multiple_of(block * 128, 128), 128)

    sources = (query_weight, key_weight, value_weight)
    for k, other in enumerate(others):
        for i, source in enumerate(sources):
            go(
                remote(
                    source.at[mine, part_of(other)],
                    weights.at[fsdp, mine, pl.ds(128 * i, 128)],
                    w_send.at[i, k],
                    w_recv.at[i, fsdp],
                    rep,
                    other,
                )
            )
        go(remote(small, marks.at[:, part_of(fsdp)], s_send.at[k], s_recv.at[fsdp], rep, other))
    go(remote(rows, rows_full.at[fsdp], x_send.at[3], x_recv.at[fsdp], rep, side))
    for k, other in enumerate(lines):
        go(remote(rows, rows_full.at[fsdp], x_send.at[k], x_recv.at[fsdp], rep, 2 * other + x))
    for k, other in enumerate(others):
        go(
            remote(
                firsts.at[:, part_of(other)],
                firsts_full.at[fsdp],
                f_send.at[k],
                f_recv.at[fsdp],
                rep,
                other,
            )
        )
    for i, source in enumerate(sources):
        here(source.at[:, part_of(fsdp)], weights.at[fsdp, :, pl.ds(128 * i, 128)])
    here(small, marks.at[:, part_of(fsdp)])
    here(firsts.at[:, part_of(fsdp)], firsts_full.at[fsdp])
    here(rows, rows_full.at[fsdp])
    here(cotangent, grad_full.at[fsdp])
    here(packed.at[fsdp], packed_full.at[fsdp])

    for k, other in enumerate(others):
        for i in range(3):
            arrived(weights.at[other, mine, pl.ds(128 * i, 128)], w_recv.at[i, other])
        place = weights.at[other, mine]
        go(remote(place, place, p_send.at[k], p_recv.at[other], partner, fsdp))
    for other in others:
        arrived(marks.at[:, part_of(other)], s_recv.at[other])
    for copy in kept:
        copy.wait()
    for other in others:
        arrived(weights.at[other, theirs], p_recv.at[other])
        arrived(firsts_full.at[other], f_recv.at[other])

    gain_one = marks[1:2, :]

    def project(block):
        entry = rows_full[block].astype(WIDE)
        scale = lax.rsqrt(jnp.mean(entry * entry, axis=-1, keepdims=True) + epsilon)
        low = (entry * scale * gain_one).astype(LOW)
        hidden_one[block] = low
        pre = matmul(low, weights[...].reshape(8 * 128, 384))
        cosine, sine = turn_tables(marks, block, cosine_step, sine_step)
        at = rows_of(block)
        queries[at, :] = turn(pre[:, :128], cosine, sine).astype(LOW)
        keys[at, :] = turn(pre[:, 128:256], cosine, sine).astype(LOW)
        values[at, :] = (0.5 * pre[:, 256:] + 0.5 * firsts_full[block].astype(WIDE)).astype(LOW)

    project(fsdp)
    for k, other in enumerate(lines):
        block = 2 * other + x
        place = rows_full.at[block]
        arrived(place, x_recv.at[block])
        go(remote(place, place, x_send.at[4 + k], x_recv.at[block], rep, side))
        if k == 0:
            arrived(rows_full.at[side], x_recv.at[side])
            project(side)
        project(block)
    for k, other in enumerate(lines):
        go(
            remote(
                cotangent, grad_full.at[fsdp], c_send.at[k], c_recv.at[fsdp], rep, 2 * other + x
            )
        )
    go(remote(cotangent, grad_full.at[fsdp], c_send.at[3], c_recv.at[fsdp], rep, side))
    for k, other in enumerate(others):
        go(
            remote(
                packed.at[other, mine],
                packed_full.at[fsdp, mine],
                m_send.at[k],
                m_recv.at[fsdp],
                rep,
                other,
            )
        )
    for other in lines:
        block = 2 * other + 1 - x
        arrived(rows_full.at[block], x_recv.at[block])
        project(block)

    prefix_last = (prefix[0] - 1).astype(WIDE)
    places = marks[0:1, :]
    masks = [head_lanes(head) for head in range(2)]

    def attend(block):
        at = rows_of(block)
        query = queries[at, :]
        allowed = places <= limit_column(marks, block, prefix_last)
        result = total = None
        for head in range(2):
            scores = times_transposed(jnp.where(masks[head], query, 0.0).astype(LOW), keys[...])
            scores = jnp.where(allowed, scores * E ** (-0.5), masked_score)
            top = jnp.max(scores, axis=-1, keepdims=True)
            weight = jnp.exp(scores - top)
            below = jnp.sum(weight, axis=-1, keepdims=True)
            probabilities = (weight * (1.0 / below)).astype(LOW)
            out = matmul(probabilities, values[...])
            log_total = jnp.broadcast_to(top + jnp.log(below), out.shape)
            result = out if head == 0 else jnp.where(masks[0], result, out)
            total = log_total if head == 0 else jnp.where(masks[0], total, log_total)
        totals[at, :] = total
        low = result.astype(LOW)
        attended[at, :] = low
        return matmul(low, output_weight[...])

    def first_phase(k, carry):
        other = lax.rem(z + 1 + k, 4)
        block = 2 * other + 1 - x
        part[other] = attend(block).astype(LOW)
        remote(part.at[other], side_in.at[other], r_send.at[k], side_recv.at[other], rep, side).start()
        return carry

    lax.fori_loop(0, 4, first_phase, 0)
    for k, other in enumerate(lines):
        block = 2 * other + x
        place = grad_full.at[block]
        arrived(place, c_recv.at[block])
        go(remote(place, place, c_send.at[4 + k], c_recv.at[block], rep, side))
    for k, other in enumerate(others):
        place = packed_full.at[other, mine]
        arrived(place, m_recv.at[other])
        go(remote(place, place, mp_send.at[k], mp_recv.at[other], partner, fsdp))

    def second_phase(k, carry):
        other = lax.rem(z + 1 + k, 4)
        total = attend(2 * other + x)
        arrived(side_in.at[other], side_recv.at[other])
        summed[other] = (total + side_in[other].astype(WIDE)).astype(LOW)
        remote(
            summed.at[other], line_in.at[z], r_send.at[4 + k], line_recv.at[z], rep, 2 * other + x
        ).start()
        return carry

    lax.fori_loop(0, 3, second_phase, 0)
    total = attend(fsdp)
    arrived(side_in.at[z], side_recv.at[z])
    total = total + side_in[z].astype(WIDE)
    for other in lines:
        arrived(line_in.at[other], line_recv.at[other])
        total = total + line_in[other].astype(WIDE)
    total = rows[...].astype(WIDE) + total
    middle[...] = total
    scale = lax.rsqrt(jnp.mean(total * total, axis=-1, keepdims=True) + epsilon)
    hidden_two[...] = (total * scale * marks[2:3, :]).astype(LOW)
    for other in lines:
        block = 2 * other + 1 - x
        arrived(grad_full.at[block], c_recv.at[block])
    arrived(grad_full.at[side], c_recv.at[side])
    for other in others:
        arrived(packed_full.at[other, theirs], mp_recv.at[other])
    for copy in started:
        copy.wait_send()
    for k in range(7):
        place = part.at[0]
        remote(place, place, r_send.at[k], r_send.at[k], rep, side).wait_send()


def forward(rows, small, prefix, steps, query_weight, key_weight, value_weight, output_weight, firsts, cotangent, packed):
    low = functools.partial(jax.ShapeDtypeStruct, dtype=LOW)
    wide = functools.partial(jax.ShapeDtypeStruct, dtype=WIDE)
    return pl.pallas_call(
        forward_kernel,
        out_shape=[
            low((8, 128, 1024)),
            low((1024, 128)),
            low((1024, 128)),
            low((1024, 128)),
            low((1024, 128)),
            wide((1024, 128)),
            low((8, 128, 384)),
            low(packed.shape),
            low((8, 128, 1024)),
            wide((8, 1024)),
            wide((128, 1024)),
            low((128, 1024)),
        ],
        in_specs=[VM, VM, pl.BlockSpec(memory_space=pltpu.SMEM)] + [VM] * 9,
        out_specs=[VM] * 12,
        scratch_shapes=[
            pltpu.VMEM((8, 128, 1024), LOW),
            pltpu.VMEM((8, 128, 128), LOW),
            pltpu.VMEM((4, 128, 1024), LOW),
            pltpu.VMEM((4, 128, 1024), LOW),
            pltpu.VMEM((4, 128, 1024), LOW),
            pltpu.VMEM((4, 128, 1024), LOW),
            DMA((8,)),
            DMA((3, 7)),
            DMA((3, 8)),
            DMA((7,)),
            DMA((8,)),
            DMA((7,)),
            DMA((8,)),
            DMA((7,)),
            DMA((8,)),
            DMA((7,)),
            DMA((8,)),
            DMA((7,)),
            DMA((8,)),
            DMA((7,)),
            DMA((8,)),
            DMA((7,)),
            DMA((8,)),
            DMA((7,)),
            DMA((4,)),
            DMA((4,)),
        ],
        compiler_params=pltpu.CompilerParams(
            collective_id=1, has_side_effects=True, vmem_limit_bytes=60 * 1024 * 1024
        ),
    )(rows, small, prefix, *steps, query_weight, key_weight, value_weight, output_weight, firsts, cotangent, packed)


def shards_plane(
    inputs,
    first_values,
    prefix,
    positions,
    first_gain,
    query_weight,
    key_weight,
    value_weight,
    output_weight,
    second_gain,
    gate_weight,
    up_weight,
    down_weight,
    cotangent,
):
    count = inputs.shape[0]
    hidden = gate_weight.shape[1] // 8
    half_width = E // 2
    frequency = jnp.exp(
        jnp.arange(half_width, dtype=WIDE) * (-math.log(10000.0) / half_width)
    )
    frequency = jnp.tile(frequency, 128 // half_width)[None, :]
    starts = positions.reshape(2, -1)[:, :1].astype(WIDE) * frequency
    step_angles = jnp.arange(count // 2, dtype=WIDE)[:, None] * frequency
    small = jnp.concatenate(
        [
            positions.astype(WIDE)[None],
            first_gain.astype(WIDE)[None],
            second_gain.astype(WIDE)[None],
            jnp.stack([jnp.cos(starts), jnp.sin(starts)], axis=1).reshape(4, -1),
            jnp.zeros((1, count), WIDE),
        ],
        axis=0,
    )
    pad = jnp.zeros((8, count, 384 - hidden), LOW)
    packed = jnp.concatenate(
        [to_blocks(gate_weight), pad, to_blocks(up_weight), pad], axis=2
    )
    prefix_here = lax.dynamic_slice_in_dim(prefix, lax.axis_index("rep"), 1)
    (
        hidden_one,
        queries,
        keys,
        values,
        attended_low,
        log_totals,
        attention_weights,
        packed_full,
        grad_full,
        marks,
        middle,
        hidden_two_own,
    ) = forward(
        inputs,
        small,
        prefix_here,
        (jnp.cos(step_angles), jnp.sin(step_angles)),
        query_weight,
        key_weight,
        value_weight,
        output_weight,
        first_values,
        cotangent,
        packed,
    )
    length = 8 * count
    width = 128
    hidden_one = hidden_one.reshape(length, -1)
    grad_full = grad_full.reshape(length, -1)
    attention_weights = attention_weights.reshape(length, -1)
    packed_full = packed_full.reshape(length, -1)
    gate_part = packed_full[:, :hidden]
    up_part = packed_full[:, 384 : 384 + hidden]
    places, gain_one, gain_two = marks[0], marks[1:2], marks[2:3]
    limits = jnp.maximum(places, (prefix_here - 1).astype(WIDE))
    allowed = (places[None, :] <= limits[:, None])[None]
    cosine, sine_table = rope_tables(places)
    own_rows = inputs.astype(WIDE)
    scale_two = rms_scale(middle)
    normed_two = middle * scale_two
    queries = queries.reshape(length, -1, E)
    keys = keys.reshape(length, -1, E)
    values = values.reshape(length, -1, E)
    scores = jnp.einsum("qhe,khe->hqk", queries, keys, preferred_element_type=WIDE) * E ** (-0.5)
    log_totals = log_totals.reshape(length, 2, E)[:, :, 0].T
    probabilities = jnp.where(allowed, jnp.exp(scores - log_totals[:, :, None]), 0.0)
    prob_low = probabilities.astype(LOW)
    (hidden_two,) = gather_rows(4, hidden_two_own)

    gate_pre = matmul(hidden_two, gate_part)
    up_pre = matmul(hidden_two, up_part)
    sigmoid_gate = jax.nn.sigmoid(gate_pre)
    activated = (gate_pre * sigmoid_gate * up_pre).astype(LOW)
    act_grad = times_transposed(grad_full, down_weight)
    down_term = transposed_times(activated, grad_full)
    gate_grad = (act_grad * up_pre * sigmoid_gate * (1.0 + gate_pre * (1.0 - sigmoid_gate))).astype(
        LOW
    )
    up_grad = (act_grad * gate_pre * sigmoid_gate).astype(LOW)
    hidden_two_grad = scatter_rows(
        5, (times_transposed(gate_grad, gate_part) + times_transposed(up_grad, up_part)).astype(LOW)
    )
    down_out = scatter_rows(6, matmul(activated, down_weight).astype(LOW))
    layer_output = (middle + down_out).astype(LOW)
    gate_term = transposed_times(hidden_two, gate_grad)
    up_term = transposed_times(hidden_two, up_grad)
    gain_two_term, middle_back = norm_back(hidden_two_grad, normed_two, gain_two, scale_two)
    middle_grad = cotangent.astype(WIDE) + middle_back
    (branch_low,) = gather_rows(7, middle_grad.astype(LOW))
    output_term = transposed_times(attended_low, branch_low)
    out_low = times_transposed(branch_low, output_weight).astype(LOW).reshape(length, -1, E)
    prob_grad = jnp.einsum("qhe,khe->hqk", out_low, values, preferred_element_type=WIDE)
    delta_rows = jnp.sum(probabilities * prob_grad, axis=-1, keepdims=True)
    score_grad = (probabilities * (prob_grad - delta_rows)).astype(LOW)
    query_acc = jnp.einsum("hqk,khe->qhe", score_grad, keys, preferred_element_type=WIDE)
    key_acc = jnp.einsum("hqk,qhe->khe", score_grad, queries, preferred_element_type=WIDE)
    value_acc = jnp.einsum("hqk,qhe->khe", prob_low, out_low, preferred_element_type=WIDE)
    query_grad = rope_undo(query_acc * E ** (-0.5), cosine, sine_table).astype(LOW)
    key_grad = rope_undo(key_acc * E ** (-0.5), cosine, sine_table).astype(LOW)
    value_grad = (0.5 * value_acc).astype(LOW)
    three = jnp.concatenate(
        [a.reshape(length, -1) for a in (query_grad, key_grad, value_grad)], axis=1
    )
    hidden_one_grad = scatter_rows(8, times_transposed(three, attention_weights).astype(LOW))
    attention_term = transposed_times(hidden_one, three)
    scale_one = rms_scale(own_rows)
    normed_one = own_rows * scale_one
    gain_one_term, input_part = norm_back(hidden_one_grad, normed_one, gain_one, scale_one)
    input_grad = middle_grad + input_part

    gains = jnp.stack([gain_one_term, gain_two_term], axis=1).astype(LOW)
    grads = jnp.concatenate(
        [
            attention_term.astype(LOW),
            gate_term.astype(LOW),
            up_term.astype(LOW),
            gains,
            jnp.zeros((length, 62), LOW),
        ],
        axis=1,
    ).reshape(8, count, -1)
    lower = jnp.concatenate([output_term, down_term], axis=0).astype(LOW)
    grads, lower, firsts_grad = collect(
        9, grads, lower, value_grad.reshape(8, count, -1)
    )
    gain_sums = jnp.sum(grads[:, :, 384 + 2 * hidden : 384 + 2 * hidden + 2].astype(WIDE), axis=0)
    return (
        layer_output,
        input_grad,
        from_blocks(firsts_grad).astype(WIDE),
        gain_sums[:, 0],
        from_blocks(grads[:, :, :width]).astype(WIDE),
        from_blocks(grads[:, :, width : 2 * width]).astype(WIDE),
        from_blocks(grads[:, :, 2 * width : 3 * width]).astype(WIDE),
        lower[:count].astype(WIDE),
        gain_sums[:, 1],
        from_blocks(grads[:, :, 384 : 384 + hidden]).astype(WIDE),
        from_blocks(grads[:, :, 384 + hidden : 384 + 2 * hidden]).astype(WIDE),
        lower[count:].astype(WIDE),
    )


def pick_body(mesh):
    if mesh.shape["fsdp"] == 8 and mesh.shape["rep"] == 4:
        return shards_plane
    return shards_general


def solution(mesh):
    placed = (
        P(("rep", "fsdp"), None),
        P(("rep", "fsdp"), None),
        P(),
        P(("rep", "fsdp")),
        P("fsdp"),
        P("fsdp", None),
        P("fsdp", None),
        P("fsdp", None),
        P("fsdp", None),
        P("fsdp"),
        P("fsdp", None),
        P("fsdp", None),
        P("fsdp", None),
        P(("rep", "fsdp"), None),
    )
    return jax.shard_map(
        pick_body(mesh),
        mesh=mesh,
        in_specs=placed,
        out_specs=(
            P(("rep", "fsdp"), None),
            P(("rep", "fsdp"), None),
            P(("rep", "fsdp"), None),
            P("fsdp"),
            P("fsdp", None),
            P("fsdp", None),
            P("fsdp", None),
            P("fsdp", None),
            P("fsdp"),
            P("fsdp", None),
            P("fsdp", None),
            P("fsdp", None),
        ),
        check_vma=False,
    )
```

```python
import functools
import math

import jax
import jax.numpy as jnp
from jax import lax
from jax.experimental import pallas as pl
from jax.experimental.pallas import tpu as pltpu
from jax.sharding import PartitionSpec as P

D = 1024
H = 16
E = 64


epsilon = 1e-06
masked_score = -1e30


def rms_scale(values):
    return lax.rsqrt(jnp.mean(values * values, axis=-1, keepdims=True) + epsilon)


def rope_tables(places):
    half_width = E // 2
    frequency = jnp.exp(
        jnp.arange(half_width, dtype=jnp.float32) * (-math.log(10000.0) / half_width)
    )
    angles = places.astype(jnp.float32)[:, None] * frequency[None, :]
    return (jnp.cos(angles)[:, None, :], jnp.sin(angles)[:, None, :])


def rope_apply(shaped, cosine, sine_table):
    half_width = shaped.shape[-1] // 2
    first_half = shaped[..., :half_width]
    second_half = shaped[..., half_width:]
    return jnp.concatenate(
        [
            first_half * cosine - second_half * sine_table,
            second_half * cosine + first_half * sine_table,
        ],
        axis=-1,
    )


def rope_undo(shaped, cosine, sine_table):
    half_width = shaped.shape[-1] // 2
    first_half = shaped[..., :half_width]
    second_half = shaped[..., half_width:]
    return jnp.concatenate(
        [
            first_half * cosine + second_half * sine_table,
            second_half * cosine - first_half * sine_table,
        ],
        axis=-1,
    )


def times_transposed(left, right):
    return lax.dot_general(
        left, right, (((1,), (1,)), ((), ())), preferred_element_type=jnp.float32
    )


def transposed_times(left, right):
    return lax.dot_general(
        left, right, (((0,), (0,)), ((), ())), preferred_element_type=jnp.float32
    )


def block_rows(count):
    size_now = count
    while size_now > 1024 and size_now % 2 == 0:
        size_now = size_now // 2
    return size_now


def split_blocks(array, size_now):
    return array.reshape((array.shape[0] // size_now, size_now) + array.shape[1:])


def masked_scores(queries, key_rows, limits, key_places):
    scores = jnp.einsum(
        "qhe,khe->hqk", queries, key_rows, preferred_element_type=jnp.float32
    ) * E ** (-0.5)
    allowed = key_places[None, None, :] <= limits[None, :, None]
    return (scores, allowed)


def grad_block(queries, key_rows, value_rows, limits, key_places, out_low, log_total, delta_rows):
    scores, allowed = masked_scores(queries, key_rows, limits, key_places)
    probabilities = jnp.where(allowed, jnp.exp(scores - log_total[:, :, None]), 0.0)
    prob_grad = jnp.einsum("qhe,khe->hqk", out_low, value_rows, preferred_element_type=jnp.float32)
    score_grad = (probabilities * (prob_grad - delta_rows[:, :, None])).astype(jnp.bfloat16)
    return (probabilities.astype(jnp.bfloat16), score_grad)


def norm_back(hidden_grad, normed, gain_float, scale_rows):
    normed_grad = hidden_grad * gain_float
    gain_term = jnp.sum(hidden_grad * normed, axis=0)
    rows_grad = scale_rows * (
        normed_grad - normed * jnp.mean(normed_grad * normed, axis=-1, keepdims=True)
    )
    return (gain_term, rows_grad)


def shards_general(
    inputs,
    first_values,
    prefix,
    positions,
    first_gain,
    query_weight,
    key_weight,
    value_weight,
    output_weight,
    second_gain,
    gate_weight,
    up_weight,
    down_weight,
    cotangent,
):
    token_count = inputs.shape[0]
    gain_one, query_full, key_full, value_full, output_full = (
        lax.all_gather(first_gain, "fsdp", axis=0, tiled=True),
        lax.all_gather(query_weight, "fsdp", axis=0, tiled=True),
        lax.all_gather(key_weight, "fsdp", axis=0, tiled=True),
        lax.all_gather(value_weight, "fsdp", axis=0, tiled=True),
        lax.all_gather(output_weight, "fsdp", axis=0, tiled=True),
    )
    all_places = lax.all_gather(positions, "fsdp", axis=0, tiled=True)
    prefix_here = lax.dynamic_index_in_dim(prefix, lax.axis_index("rep"), keepdims=False)
    own_limits = jnp.maximum(positions, prefix_here - 1)
    cosine, sine_table = rope_tables(positions)
    rows_float = inputs.astype(jnp.float32)
    scale_one = rms_scale(rows_float)
    normed_one = rows_float * scale_one
    gain_one_float = gain_one.astype(jnp.float32)
    hidden_one = (normed_one * gain_one_float).astype(jnp.bfloat16)
    query_pre = jnp.dot(hidden_one, query_full, preferred_element_type=jnp.float32)
    key_pre = jnp.dot(hidden_one, key_full, preferred_element_type=jnp.float32)
    value_pre = jnp.dot(hidden_one, value_full, preferred_element_type=jnp.float32)
    queries = rope_apply(query_pre.reshape(token_count, H, E), cosine, sine_table).astype(
        jnp.bfloat16
    )
    key_rows = (
        rope_apply(key_pre.reshape(token_count, H, E), cosine, sine_table)
        .astype(jnp.bfloat16)
        .reshape(token_count, D)
    )
    mixed_values = (0.5 * value_pre + 0.5 * first_values.astype(jnp.float32)).astype(jnp.bfloat16)
    start_state = (
        jnp.full((H, token_count), masked_score, jnp.float32),
        jnp.zeros((H, token_count), jnp.float32),
        jnp.zeros((token_count, H, E), jnp.float32),
    )
    running = start_state
    key_piece = lax.all_gather(key_rows, "fsdp", axis=0, tiled=True)
    value_piece = lax.all_gather(mixed_values, "fsdp", axis=0, tiled=True)
    count = key_piece.shape[0]
    size_now = block_rows(count)

    def forward_step(state_now, blocks):
        row_max, row_sum, accum = state_now
        key_block, value_block, place_block = blocks
        scores, allowed = masked_scores(
            queries, key_block.reshape(-1, H, E), own_limits, place_block
        )
        new_max = jnp.maximum(row_max, jnp.max(jnp.where(allowed, scores, masked_score), axis=-1))
        rescale = jnp.exp(row_max - new_max)
        weights = jnp.where(allowed, jnp.exp(scores - new_max[:, :, None]), 0.0)
        row_sum = row_sum * rescale + jnp.sum(weights, axis=-1)
        accum = accum * rescale.T[:, :, None] + jnp.einsum(
            "hqk,khe->qhe",
            weights.astype(jnp.bfloat16),
            value_block.reshape(-1, H, E),
            preferred_element_type=jnp.float32,
        )
        return ((new_max, row_sum, accum), None)

    running, unused = lax.scan(
        forward_step,
        running,
        (
            split_blocks(key_piece, size_now),
            split_blocks(value_piece, size_now),
            split_blocks(all_places, size_now),
        ),
    )
    row_max, row_sum, accum = running
    log_total = row_max + jnp.log(row_sum)
    attended = accum / row_sum.T[:, :, None]
    attended_low = attended.reshape(token_count, D).astype(jnp.bfloat16)
    middle = rows_float + jnp.dot(attended_low, output_full, preferred_element_type=jnp.float32)
    mlp_forward = (
        lax.all_gather(second_gain, "fsdp", axis=0, tiled=True),
        lax.all_gather(gate_weight, "fsdp", axis=0, tiled=True),
        lax.all_gather(up_weight, "fsdp", axis=0, tiled=True),
        lax.all_gather(down_weight, "fsdp", axis=0, tiled=True),
    )
    gain_two, gate_full, up_full, down_full = mlp_forward
    scale_two = rms_scale(middle)
    normed_two = middle * scale_two
    hidden_two = (normed_two * gain_two.astype(jnp.float32)).astype(jnp.bfloat16)
    gate_pre = jnp.dot(hidden_two, gate_full, preferred_element_type=jnp.float32)
    up_pre = jnp.dot(hidden_two, up_full, preferred_element_type=jnp.float32)
    sigmoid_gate = jax.nn.sigmoid(gate_pre)
    activated = (gate_pre * sigmoid_gate * up_pre).astype(jnp.bfloat16)
    layer_output = (
        middle + jnp.dot(activated, down_full, preferred_element_type=jnp.float32)
    ).astype(jnp.bfloat16)
    gain_two_back, gate_back, up_back, down_back = (
        lax.all_gather(second_gain, "fsdp", axis=0, tiled=True),
        lax.all_gather(gate_weight, "fsdp", axis=0, tiled=True),
        lax.all_gather(up_weight, "fsdp", axis=0, tiled=True),
        lax.all_gather(down_weight, "fsdp", axis=0, tiled=True),
    )
    act_grad = times_transposed(cotangent, down_back)
    down_term = transposed_times(activated, cotangent)
    gate_grad = (act_grad * up_pre * sigmoid_gate * (1.0 + gate_pre * (1.0 - sigmoid_gate))).astype(
        jnp.bfloat16
    )
    up_grad = (act_grad * gate_pre * sigmoid_gate).astype(jnp.bfloat16)
    hidden_two_grad = times_transposed(gate_grad, gate_back) + times_transposed(up_grad, up_back)
    gate_term = transposed_times(hidden_two, gate_grad)
    up_term = transposed_times(hidden_two, up_grad)
    gain_two_term, middle_part = norm_back(
        hidden_two_grad, normed_two, gain_two_back.astype(jnp.float32), scale_two
    )
    middle_grad = cotangent.astype(jnp.float32) + middle_part
    gain_two_sum, gate_sum, up_sum, down_sum = (
        lax.psum_scatter(gain_two_term, "fsdp", scatter_dimension=0, tiled=True),
        lax.psum_scatter(gate_term, "fsdp", scatter_dimension=0, tiled=True),
        lax.psum_scatter(up_term, "fsdp", scatter_dimension=0, tiled=True),
        lax.psum_scatter(down_term, "fsdp", scatter_dimension=0, tiled=True),
    )
    gain_one_back, query_back, key_back, value_back, output_back = (
        lax.all_gather(first_gain, "fsdp", axis=0, tiled=True),
        lax.all_gather(query_weight, "fsdp", axis=0, tiled=True),
        lax.all_gather(key_weight, "fsdp", axis=0, tiled=True),
        lax.all_gather(value_weight, "fsdp", axis=0, tiled=True),
        lax.all_gather(output_weight, "fsdp", axis=0, tiled=True),
    )
    branch_low = middle_grad.astype(jnp.bfloat16)
    output_term = transposed_times(attended_low, branch_low)
    out_flat = times_transposed(branch_low, output_back).astype(jnp.bfloat16)
    out_low = out_flat.reshape(token_count, H, E)
    delta_rows = jnp.sum(out_low.astype(jnp.float32) * attended, axis=-1).T
    zero_rows = jnp.zeros((token_count, H, E), jnp.float32)
    gathered_keys, gathered_values = (
        lax.all_gather(key_rows, "fsdp", axis=0, tiled=True),
        lax.all_gather(mixed_values, "fsdp", axis=0, tiled=True),
    )
    length = gathered_keys.shape[0]
    size_now = block_rows(length)

    def back_step(query_acc, blocks):
        key_block, value_block, place_block = blocks
        key_shaped = key_block.reshape(-1, H, E)
        value_shaped = value_block.reshape(-1, H, E)
        prob_low, score_grad = grad_block(
            queries,
            key_shaped,
            value_shaped,
            own_limits,
            place_block,
            out_low,
            log_total,
            delta_rows,
        )
        query_acc = query_acc + jnp.einsum(
            "hqk,khe->qhe", score_grad, key_shaped, preferred_element_type=jnp.float32
        )
        key_part = jnp.einsum(
            "hqk,qhe->khe", score_grad, queries, preferred_element_type=jnp.float32
        ).reshape(-1, D)
        value_part = jnp.einsum(
            "hqk,qhe->khe", prob_low, out_low, preferred_element_type=jnp.float32
        ).reshape(-1, D)
        return (query_acc, jnp.concatenate([key_part, value_part], axis=1))

    query_acc, parts = lax.scan(
        back_step,
        zero_rows,
        (
            split_blocks(gathered_keys, size_now),
            split_blocks(gathered_values, size_now),
            split_blocks(all_places, size_now),
        ),
    )
    summed = lax.psum_scatter(parts.reshape(length, 2 * D), "fsdp", scatter_dimension=0, tiled=True)
    key_acc = summed[:, :D]
    value_acc = summed[:, D:]
    query_grad = (
        rope_undo(query_acc * E ** (-0.5), cosine, sine_table)
        .reshape(token_count, D)
        .astype(jnp.bfloat16)
    )
    key_grad = (
        rope_undo(key_acc.reshape(token_count, H, E) * E ** (-0.5), cosine, sine_table)
        .reshape(token_count, D)
        .astype(jnp.bfloat16)
    )
    first_values_grad = 0.5 * value_acc
    value_grad = first_values_grad.astype(jnp.bfloat16)
    hidden_one_grad = (
        times_transposed(query_grad, query_back)
        + times_transposed(key_grad, key_back)
        + times_transposed(value_grad, value_back)
    )
    query_term = transposed_times(hidden_one, query_grad)
    key_term = transposed_times(hidden_one, key_grad)
    value_term = transposed_times(hidden_one, value_grad)
    gain_one_term, input_part = norm_back(
        hidden_one_grad, normed_one, gain_one_back.astype(jnp.float32), scale_one
    )
    input_grad = middle_grad + input_part
    gain_one_sum, query_sum, key_sum, value_sum, output_sum = (
        lax.psum_scatter(gain_one_term, "fsdp", scatter_dimension=0, tiled=True),
        lax.psum_scatter(query_term, "fsdp", scatter_dimension=0, tiled=True),
        lax.psum_scatter(key_term, "fsdp", scatter_dimension=0, tiled=True),
        lax.psum_scatter(value_term, "fsdp", scatter_dimension=0, tiled=True),
        lax.psum_scatter(output_term, "fsdp", scatter_dimension=0, tiled=True),
    )
    totals = (
        lax.psum(gain_one_sum.astype(jnp.bfloat16), "rep").astype(jnp.float32),
        lax.psum(query_sum.astype(jnp.bfloat16), "rep").astype(jnp.float32),
        lax.psum(key_sum.astype(jnp.bfloat16), "rep").astype(jnp.float32),
        lax.psum(value_sum.astype(jnp.bfloat16), "rep").astype(jnp.float32),
        lax.psum(output_sum.astype(jnp.bfloat16), "rep").astype(jnp.float32),
        lax.psum(gain_two_sum.astype(jnp.bfloat16), "rep").astype(jnp.float32),
        lax.psum(gate_sum.astype(jnp.bfloat16), "rep").astype(jnp.float32),
        lax.psum(up_sum.astype(jnp.bfloat16), "rep").astype(jnp.float32),
        lax.psum(down_sum.astype(jnp.bfloat16), "rep").astype(jnp.float32),
    )
    return (
        layer_output,
        input_grad,
        first_values_grad,
        totals[0],
        totals[1],
        totals[2],
        totals[3],
        totals[4],
        totals[5],
        totals[6],
        totals[7],
        totals[8],
    )


MESH = pl.DeviceIdType.MESH
LOW = jnp.bfloat16
WIDE = jnp.float32
VM = pl.BlockSpec(memory_space=pltpu.VMEM)
SM = pl.BlockSpec(memory_space=pltpu.SMEM)
DMA = pltpu.SemaphoreType.DMA
LIMIT = 60 * 1024 * 1024


def remote(src, dst, send_sem, recv_sem, rep, fsdp):
    return pltpu.make_async_remote_copy(
        src_ref=src,
        dst_ref=dst,
        send_sem=send_sem,
        recv_sem=recv_sem,
        device_id={"rep": rep, "fsdp": fsdp},
        device_id_type=MESH,
    )


def arrived(place, sem):
    pltpu.make_async_copy(place, place, sem).wait()


def greet(peers):
    barrier = pltpu.get_barrier_semaphore()
    for rep, fsdp in peers:
        pl.semaphore_signal(
            barrier, inc=1, device_id={"rep": rep, "fsdp": fsdp}, device_id_type=MESH
        )
    pl.semaphore_wait(barrier, len(peers))


def plane_place():
    rep, fsdp = lax.axis_index("rep"), lax.axis_index("fsdp")
    return rep, fsdp, fsdp // 2, fsdp % 2


def piece(index, size):
    return pl.ds(pl.multiple_of(index * size, size), size)


def matmul(left, right):
    return jnp.dot(left, right, preferred_element_type=WIDE)


class Rows:
    def __init__(self, own, full, keep, send, recv):
        self.own, self.full, self.keep, self.send, self.recv = own, full, keep, send, recv
        self.rep, self.fsdp, self.z, self.x = plane_place()
        self.side = 2 * self.z + 1 - self.x

    def push(self, src, block, sem, target):
        return remote(
            src, self.full.at[block], self.send.at[sem], self.recv.at[block], self.rep, target
        )

    def start(self):
        z, x = self.z, self.x

        @pl.when(z < 3)
        def up():
            self.push(self.own, self.fsdp, 0, 2 * (z + 1) + x).start()

        @pl.when(z > 0)
        def down():
            self.push(self.own, self.fsdp, 1, 2 * (z - 1) + x).start()

        self.push(self.own, self.fsdp, 2, self.side).start()
        pltpu.make_async_copy(self.own, self.full.at[self.fsdp], self.keep).start()

    def kept(self):
        pltpu.make_async_copy(self.own, self.full.at[self.fsdp], self.keep).wait()

    def line(self, k):
        high, odd = self.z // 2, self.z % 2
        first = 1 - (k + 1) // 2
        low_side = k + 1 - odd * first
        high_side = 2 - k + first * (1 - odd)
        return low_side + high * (high_side - low_side)

    def pass_on(self, k):
        z, x = self.z, self.x
        other = self.line(k)
        block = 2 * other + x
        place = self.full.at[block]
        arrived(place, self.recv.at[block])

        @pl.when((other < z) & (z < 3))
        def up():
            self.push(place, block, 3 + k, 2 * (z + 1) + x).start()

        @pl.when((other > z) & (z > 0))
        def down():
            self.push(place, block, 3 + k, 2 * (z - 1) + x).start()

        self.push(place, block, 6 + k, self.side).start()
        return block

    def across(self, other):
        block = 2 * other + 1 - self.x
        arrived(self.full.at[block], self.recv.at[block])
        return block

    def sent(self):
        z = self.z
        place = self.full.at[0]

        def done(sem):
            arrived(place, self.send.at[sem])

        pl.when(z < 3)(lambda: done(0))
        pl.when(z > 0)(lambda: done(1))
        done(2)
        for k in range(3):
            done(6 + k)

            @pl.when((z > 0) & (z < 3))
            def relayed():
                done(3 + k)


def rows_sems():
    return [DMA(()), DMA((9,)), DMA((8,))]


class Sums:
    def __init__(self, side_in, summed, line_in, send, side_recv, line_recv):
        self.side_in, self.summed, self.line_in = side_in, summed, line_in
        self.send, self.side_recv, self.line_recv = send, side_recv, line_recv
        self.rep, self.fsdp, self.z, self.x = plane_place()
        self.side = 2 * self.z + 1 - self.x

    def other(self, k):
        return lax.rem(self.z + 1 + k, 4)

    def give(self, k, ref):
        other = self.other(k)
        remote(
            ref, self.side_in.at[other], self.send.at[k], self.side_recv.at[other], self.rep, self.side
        ).start()

    def forward(self, k, value):
        other = self.other(k)
        arrived(self.side_in.at[other], self.side_recv.at[other])
        self.summed[other] = (value + self.side_in[other].astype(WIDE)).astype(LOW)
        remote(
            self.summed.at[other],
            self.line_in.at[self.z],
            self.send.at[4 + k],
            self.line_recv.at[self.z],
            self.rep,
            2 * other + self.x,
        ).start()

    def total(self, value):
        arrived(self.side_in.at[self.z], self.side_recv.at[self.z])
        value = value + self.side_in[self.z].astype(WIDE)
        for k in range(3):
            other = self.other(k)
            arrived(self.line_in.at[other], self.line_recv.at[other])
            value = value + self.line_in[other].astype(WIDE)
        return value

    def sent(self):
        for k in range(7):
            arrived(self.side_in.at[0], self.send.at[k])


def sums_scratch():
    return [pltpu.VMEM((4, 128, D), LOW)] * 3 + [DMA((7,)), DMA((4,)), DMA((4,))]


class Collect:
    def __init__(self, grads, out, pair_in, pair_sum, level_in, level_sum, landed, send, recv, cross_send, cross_recv):
        self.grads, self.out = grads, out
        self.pair_in, self.pair_sum = pair_in, pair_sum
        self.level_in, self.level_sum, self.landed = level_in, level_sum, landed
        self.send, self.recv, self.cross_send, self.cross_recv = send, recv, cross_send, cross_recv
        self.rep, self.fsdp, _, _ = plane_place()
        self.core, self.level = lax.rem(self.rep, 2), self.rep // 2
        self.partner = self.rep + 1 - 2 * self.core
        self.above = self.rep + 2 - 4 * self.level
        self.half = grads.shape[1] // 2
        self.fourth = self.half // 2

    def to(self, src, dst, index, rep):
        return remote(src, dst, self.send.at[index], self.recv.at[index], rep, self.fsdp)

    def start(self):
        src = self.grads.at[:, piece(1 - self.core, self.half)]
        self.to(src, self.pair_in, 0, self.partner).start()

    def fold_pair(self):
        arrived(self.pair_in, self.recv.at[0])
        mine = piece(self.core, self.half)

        def add(i, carry):
            self.pair_sum[i] = (
                self.grads[i, mine].astype(WIDE) + self.pair_in[i].astype(WIDE)
            ).astype(LOW)
            return carry

        lax.fori_loop(0, 8, add, 0)
        src = self.pair_sum.at[:, piece(1 - self.level, self.fourth)]
        self.to(src, self.level_in, 1, self.above).start()

    def fold_level(self):
        arrived(self.level_in, self.recv.at[1])
        mine = piece(self.level, self.fourth)

        def add(i, carry):
            self.level_sum[i] = (
                self.pair_sum[i, mine].astype(WIDE) + self.level_in[i].astype(WIDE)
            ).astype(LOW)
            return carry

        lax.fori_loop(0, 8, add, 0)
        for k in range(7):
            other = lax.rem(self.fsdp + k + 1, 8)
            remote(
                self.level_sum.at[other],
                self.landed.at[self.fsdp],
                self.cross_send.at[k],
                self.cross_recv.at[self.fsdp],
                self.rep,
                other,
            ).start()

    def quarter(self, core, level):
        return self.out.at[:, piece(2 * core + level, self.fourth)]

    def land(self):
        for k in range(7):
            other = lax.rem(self.fsdp + k + 1, 8)
            arrived(self.landed.at[other], self.cross_recv.at[other])
        self.landed[self.fsdp] = self.level_sum[self.fsdp]
        mine = piece(2 * self.core + self.level, self.fourth)
        place = self.quarter(self.core, self.level)
        self.to(self.landed, place, 2, self.above).start()
        self.to(self.landed, place, 3, self.partner).start()
        for i in range(8):
            self.out[i, mine] = self.landed[i]

    def relay(self):
        place = self.quarter(self.core, 1 - self.level)
        arrived(place, self.recv.at[2])
        self.to(place, place, 4, self.partner).start()

    def finish(self):
        arrived(self.quarter(1 - self.core, self.level), self.recv.at[3])
        arrived(self.quarter(1 - self.core, 1 - self.level), self.recv.at[4])
        arrived(self.pair_in, self.send.at[0])
        arrived(self.level_in, self.send.at[1])
        for k in range(3):
            arrived(self.landed, self.send.at[2 + k])
        for k in range(7):
            arrived(self.landed.at[0], self.cross_send.at[k])


def collect_scratch(high, wide):
    return [
        pltpu.VMEM((8, high // 2, wide), LOW),
        pltpu.VMEM((8, high // 2, wide), LOW),
        pltpu.VMEM((8, high // 4, wide), LOW),
        pltpu.VMEM((8, high // 4, wide), LOW),
        pltpu.VMEM((8, high // 4, wide), LOW),
        DMA((5,)),
        DMA((5,)),
        DMA((7,)),
        DMA((8,)),
    ]


class CollectRows:
    def __init__(self, rows, out, pair_in, pair_sum, level_in, send, recv):
        self.rows, self.out = rows, out
        self.pair_in, self.pair_sum, self.level_in = pair_in, pair_sum, level_in
        self.send, self.recv = send, recv
        self.rep, self.fsdp, _, _ = plane_place()
        self.core, self.level = lax.rem(self.rep, 2), self.rep // 2
        self.partner = self.rep + 1 - 2 * self.core
        self.above = self.rep + 2 - 4 * self.level
        self.half = rows.shape[1] // 2
        self.fourth = self.half // 2

    def to(self, src, dst, index, rep):
        return remote(src, dst, self.send.at[index], self.recv.at[index], rep, self.fsdp)

    def start(self):
        src = self.rows.at[:, piece(1 - self.core, self.half)]
        self.to(src, self.pair_in, 0, self.partner).start()

    def fold_pair(self):
        arrived(self.pair_in, self.recv.at[0])
        self.pair_sum[...] = (
            self.rows[:, piece(self.core, self.half)].astype(WIDE) + self.pair_in[...].astype(WIDE)
        ).astype(LOW)
        src = self.pair_sum.at[:, piece(1 - self.level, self.fourth)]
        self.to(src, self.level_in, 1, self.above).start()

    def quarter(self, core, level):
        return self.out.at[:, piece(2 * core + level, self.fourth)]

    def fold_level(self):
        arrived(self.level_in, self.recv.at[1])
        mine = piece(2 * self.core + self.level, self.fourth)
        self.out[:, mine] = (
            self.pair_sum[:, piece(self.level, self.fourth)].astype(WIDE)
            + self.level_in[...].astype(WIDE)
        ).astype(LOW)
        place = self.quarter(self.core, self.level)
        self.to(place, place, 2, self.above).start()
        self.to(place, place, 3, self.partner).start()

    def relay(self):
        place = self.quarter(self.core, 1 - self.level)
        arrived(place, self.recv.at[2])
        self.to(place, place, 4, self.partner).start()

    def finish(self):
        arrived(self.quarter(1 - self.core, self.level), self.recv.at[3])
        arrived(self.quarter(1 - self.core, 1 - self.level), self.recv.at[4])
        arrived(self.pair_in, self.send.at[0])
        for k in range(4):
            arrived(self.level_in, self.send.at[1 + k])


def collect_rows_scratch(tall):
    return [
        pltpu.VMEM((tall, D // 2), LOW),
        pltpu.VMEM((tall, D // 2), LOW),
        pltpu.VMEM((tall, D // 4), LOW),
        DMA((5,)),
        DMA((5,)),
    ]


def turn_tables(marks, block, cosine_step, sine_step):
    lanes = piece(block, 128)
    cosines, sines = [], []
    for run in range(2):
        c = marks[3 + 2 * run : 4 + 2 * run, lanes]
        s = marks[4 + 2 * run : 5 + 2 * run, lanes]
        cosines.append(c * cosine_step[...] - s * sine_step[...])
        sines.append(s * cosine_step[...] + c * sine_step[...])
    lane = lax.broadcasted_iota(jnp.int32, (1, 128), 1)
    sign = jnp.where(lane % E < E // 2, -1.0, 1.0)
    return jnp.concatenate(cosines, axis=0), jnp.concatenate(sines, axis=0) * sign


def turn(array, cosine, sine):
    lane = lax.broadcasted_iota(jnp.int32, (1, 128), 1)
    swapped = jnp.where(lane % E < E // 2, pltpu.roll(array, 96, 1), pltpu.roll(array, 32, 1))
    return array * cosine + swapped * sine


def limit_column(marks, block, prefix_last):
    tile = marks[0:1, piece(block, 128)]
    lane = lax.broadcasted_iota(jnp.int32, (1, 128), 1)
    row = lax.broadcasted_iota(jnp.int32, (128, 1), 0)
    first = jnp.sum(jnp.where(lane == 0, tile, 0.0), axis=1, keepdims=True)
    second = jnp.sum(jnp.where(lane == 64, tile, 0.0), axis=1, keepdims=True)
    places = jnp.where(row < 64, first + row.astype(WIDE), second + (row - 64).astype(WIDE))
    return jnp.maximum(places, prefix_last)


def head_lanes(head):
    lane = lax.broadcasted_iota(jnp.int32, (1, 128), 1)
    return (lane // E) == head


def only(mask, array):
    return jnp.where(mask, array.astype(WIDE), 0.0).astype(LOW)


def forward_kernel(
    rows,
    small,
    prefix,
    cosine_step,
    sine_step,
    query_weight,
    key_weight,
    value_weight,
    output_weight,
    firsts,
    cotangent,
    packed,
    hidden_one,
    queries,
    keys,
    keys_turned,
    values_turned,
    attended,
    totals,
    weights,
    packed_full,
    grad_full,
    marks,
    middle,
    hidden_two,
    rows_full,
    firsts_full,
    values,
    part,
    *sems,
):
    (side_in, summed, line_in, r_send, side_recv, line_recv) = sems[:6]
    x_sems, c_sems = sems[6:9], sems[9:12]
    keep, w_send, w_recv, p_send, p_recv, s_send, s_recv, f_send, f_recv = sems[12:21]
    m_send, m_recv, mp_send, mp_recv = sems[21:]
    rep, fsdp, z, x = plane_place()
    core = lax.rem(rep, 2)
    partner = rep + 1 - 2 * core
    others = [lax.rem(fsdp + k, 8) for k in range(1, 8)]
    greet([(rep, other) for other in others] + [(partner, fsdp)])
    mine = piece(core, 64)
    theirs = piece(1 - core, 64)
    started, kept = [], []
    row_flow = Rows(rows, rows_full, *x_sems)
    grad_flow = Rows(cotangent, grad_full, *c_sems)
    sums = Sums(side_in, summed, line_in, r_send, side_recv, line_recv)

    def go(copy):
        copy.start()
        started.append(copy)

    def here(src, dst):
        copy = pltpu.make_async_copy(src, dst, keep.at[len(kept)])
        copy.start()
        kept.append(copy)

    sources = (query_weight, key_weight, value_weight)
    for k, other in enumerate(others):
        for i, source in enumerate(sources):
            go(
                remote(
                    source.at[mine, piece(other, 128)],
                    weights.at[fsdp, mine, pl.ds(128 * i, 128)],
                    w_send.at[i, k],
                    w_recv.at[i, fsdp],
                    rep,
                    other,
                )
            )
        go(remote(small, marks.at[:, piece(fsdp, 128)], s_send.at[k], s_recv.at[fsdp], rep, other))
    row_flow.start()
    for k, other in enumerate(others):
        go(
            remote(
                firsts.at[:, piece(other, 128)],
                firsts_full.at[fsdp],
                f_send.at[k],
                f_recv.at[fsdp],
                rep,
                other,
            )
        )
    for i, source in enumerate(sources):
        here(source.at[:, piece(fsdp, 128)], weights.at[fsdp, :, pl.ds(128 * i, 128)])
    here(small, marks.at[:, piece(fsdp, 128)])
    here(firsts.at[:, piece(fsdp, 128)], firsts_full.at[fsdp])
    here(packed.at[fsdp], packed_full.at[fsdp])

    for k, other in enumerate(others):
        for i in range(3):
            arrived(weights.at[other, mine, pl.ds(128 * i, 128)], w_recv.at[i, other])
        place = weights.at[other, mine]
        go(remote(place, place, p_send.at[k], p_recv.at[other], partner, fsdp))
    for other in others:
        arrived(marks.at[:, piece(other, 128)], s_recv.at[other])
    for copy in kept:
        copy.wait()
    row_flow.kept()
    for other in others:
        arrived(weights.at[other, theirs], p_recv.at[other])
        arrived(firsts_full.at[other], f_recv.at[other])

    gain_one = marks[1:2, :]

    def project(block):
        entry = rows_full[block].astype(WIDE)
        scale = lax.rsqrt(jnp.mean(entry * entry, axis=-1, keepdims=True) + epsilon)
        low = (entry * scale * gain_one).astype(LOW)
        hidden_one[block] = low
        pre = matmul(low, weights[...].reshape(8 * 128, 384))
        cosine, sine = turn_tables(marks, block, cosine_step, sine_step)
        at = piece(block, 128)
        queries[at, :] = turn(pre[:, :128], cosine, sine).astype(LOW)
        key = turn(pre[:, 128:256], cosine, sine)
        keys[at, :] = key.astype(LOW)
        keys_turned[:, at] = key.T.astype(LOW)
        value = 0.5 * pre[:, 256:] + 0.5 * firsts_full[block].astype(WIDE)
        values[at, :] = value.astype(LOW)
        values_turned[:, at] = value.T.astype(LOW)

    def own_column(k, carry):
        block = row_flow.pass_on(k)
        project(block)
        return carry

    def other_column(k, carry):
        project(row_flow.across(lax.rem(z + k, 4)))
        return carry

    project(fsdp)
    lax.fori_loop(0, 3, own_column, 0)
    grad_flow.start()
    for k, other in enumerate(others):
        go(
            remote(
                packed.at[other, mine],
                packed_full.at[fsdp, mine],
                m_send.at[k],
                m_recv.at[fsdp],
                rep,
                other,
            )
        )
    lax.fori_loop(0, 4, other_column, 0)
    prefix_last = (prefix[0] - 1).astype(WIDE)
    masks = [head_lanes(head) for head in range(2)]

    def attend(block):
        at = piece(block, 128)
        query = queries[at, :]
        allowed = marks[0:1, :] <= limit_column(marks, block, prefix_last)
        result = total = None
        for head in range(2):
            scores = matmul(only(masks[head], query), keys_turned[...]) * E ** (-0.5)
            scores = jnp.where(allowed, scores, masked_score)
            top = jnp.max(scores, axis=-1, keepdims=True)
            weight = jnp.exp(scores - top)
            below = jnp.sum(weight, axis=-1, keepdims=True)
            probabilities = (weight * (1.0 / below)).astype(LOW)
            out = matmul(probabilities, values[...])
            log_total = jnp.broadcast_to(top + jnp.log(below), out.shape)
            result = out if head == 0 else jnp.where(masks[0], result, out)
            total = log_total if head == 0 else jnp.where(masks[0], total, log_total)
        totals[at, :] = total
        low = result.astype(LOW)
        attended[at, :] = low
        return matmul(low, output_weight[...])

    def first_phase(k, carry):
        other = sums.other(k)
        part[other] = attend(2 * other + 1 - x).astype(LOW)
        sums.give(k, part.at[other])

        @pl.when(k > 0)
        def hand_on():
            grad_flow.pass_on(k - 1)

        return carry

    lax.fori_loop(0, 4, first_phase, 0)
    for k, other in enumerate(others):
        place = packed_full.at[other, mine]
        arrived(place, m_recv.at[other])
        go(remote(place, place, mp_send.at[k], mp_recv.at[other], partner, fsdp))

    def second_phase(k, carry):
        sums.forward(k, attend(2 * sums.other(k) + x))
        return carry

    lax.fori_loop(0, 3, second_phase, 0)
    total = rows[...].astype(WIDE) + sums.total(attend(fsdp))
    middle[...] = total
    scale = lax.rsqrt(jnp.mean(total * total, axis=-1, keepdims=True) + epsilon)
    hidden_two[...] = (total * scale * marks[2:3, :]).astype(LOW)
    for k in range(4):
        grad_flow.across(lax.rem(z + k, 4))
    grad_flow.kept()
    for other in others:
        arrived(packed_full.at[other, theirs], mp_recv.at[other])
    for copy in started:
        copy.wait_send()
    row_flow.sent()
    grad_flow.sent()
    sums.sent()


def low_shape(*shape):
    return jax.ShapeDtypeStruct(shape, LOW)


def wide_shape(*shape):
    return jax.ShapeDtypeStruct(shape, WIDE)


def forward(*arrays):
    return pl.pallas_call(
        forward_kernel,
        out_shape=[
            low_shape(8, 128, 1024),
            low_shape(1024, 128),
            low_shape(1024, 128),
            low_shape(128, 1024),
            low_shape(128, 1024),
            low_shape(1024, 128),
            wide_shape(1024, 128),
            low_shape(8, 128, 384),
            low_shape(8, 128, 768),
            low_shape(8, 128, 1024),
            wide_shape(8, 1024),
            wide_shape(128, 1024),
            low_shape(128, 1024),
        ],
        in_specs=[VM, VM, SM] + [VM] * 9,
        out_specs=[VM] * 13,
        scratch_shapes=[
            pltpu.VMEM((8, 128, 1024), LOW),
            pltpu.VMEM((8, 128, 128), LOW),
            pltpu.VMEM((1024, 128), LOW),
            pltpu.VMEM((4, 128, 1024), LOW),
        ]
        + sums_scratch()
        + rows_sems()
        + rows_sems()
        + [DMA((6,)), DMA((3, 7)), DMA((3, 8))]
        + [DMA((7,)), DMA((8,))] * 5,
        compiler_params=pltpu.CompilerParams(
            collective_id=1, has_side_effects=True, vmem_limit_bytes=LIMIT
        ),
    )(*arrays)


def middle_kernel(
    own_hidden,
    packed,
    down,
    grad_full,
    middle,
    cotangent,
    marks,
    middle_grad,
    branch,
    gain_term,
    weight_grads,
    down_grad,
    out_part,
    hidden_full,
    active,
    both,
    down_pad,
    part,
    *sems,
):
    sums = Sums(*sems[:6])
    flow = Rows(own_hidden, hidden_full, *sems[6:9])
    rep, fsdp, z, x = plane_place()
    peers = [(rep, 2 * lax.rem(z + k, 4) + x) for k in (1, 2, 3)] + [(rep, sums.side)]
    greet(peers)
    flow.start()
    used = down.shape[0]
    down_pad[0:used, :] = down[...]
    down_pad[used:384, :] = jnp.zeros((384 - used, D), LOW)

    def work(block):
        at = piece(block, 128)
        pre = matmul(hidden_full[block], packed[...])
        gate, up = pre[:, :384], pre[:, 384:]
        sigmoid = 1.0 / (1.0 + jnp.exp(-gate))
        swish = gate * sigmoid
        act = (swish * up).astype(LOW)
        active[at, :] = act
        act_grad = times_transposed(grad_full[block], down_pad[...])
        gate_grad = act_grad * up * sigmoid * (1.0 + gate * (1.0 - sigmoid))
        both[at, 0:384] = gate_grad.astype(LOW)
        both[at, 384:768] = (act_grad * swish).astype(LOW)
        part[block] = times_transposed(both[at, :], packed[...]).astype(LOW)
        out_part[block] = matmul(act, down_pad[...]).astype(LOW)

    flow.kept()
    work(fsdp)

    def own_column(k, carry):
        work(flow.pass_on(k))
        return carry

    def other_column(k, carry):
        other = sums.other(k)
        block = flow.across(other)
        work(block)
        sums.give(k, part.at[block])
        return carry

    lax.fori_loop(0, 3, own_column, 0)
    lax.fori_loop(0, 4, other_column, 0)

    def grads(i, carry):
        lanes = piece(i, 128)
        turned = hidden_full[:, :, lanes].reshape(8 * 128, 128)
        weight_grads[i] = transposed_times(turned, both[...]).astype(LOW)
        return carry

    def onward(k, carry):
        lax.fori_loop(2 * k, 2 * k + 2, grads, 0)
        sums.forward(k, part[2 * sums.other(k) + x].astype(WIDE))
        return carry

    lax.fori_loop(0, 3, onward, 0)
    lax.fori_loop(6, 8, grads, 0)
    down_sum = transposed_times(active[...], grad_full[...].reshape(8 * 128, D))
    down_grad[...] = down_sum[0:used].astype(LOW)
    hidden_grad = sums.total(part[fsdp].astype(WIDE))
    entry = middle[...]
    scale = lax.rsqrt(jnp.mean(entry * entry, axis=-1, keepdims=True) + epsilon)
    normed = entry * scale
    normed_grad = hidden_grad * marks[2:3, :]
    gain_term[...] = jnp.broadcast_to(
        jnp.sum(hidden_grad * normed, axis=0, keepdims=True), (8, D)
    )
    back = scale * (normed_grad - normed * jnp.mean(normed_grad * normed, axis=-1, keepdims=True))
    grad = cotangent[...].astype(WIDE) + back
    middle_grad[...] = grad
    branch[...] = grad.astype(LOW)
    flow.sent()
    sums.sent()


def feed_forward(*arrays):
    used = arrays[2].shape[0]
    return pl.pallas_call(
        middle_kernel,
        out_shape=[
            wide_shape(128, 1024),
            low_shape(128, 1024),
            wide_shape(8, 1024),
            low_shape(8, 128, 768),
            low_shape(used, 1024),
            low_shape(8, 128, 1024),
        ],
        in_specs=[VM] * 7,
        out_specs=[VM] * 6,
        scratch_shapes=[
            pltpu.VMEM((8, 128, 1024), LOW),
            pltpu.VMEM((1024, 384), LOW),
            pltpu.VMEM((1024, 768), LOW),
            pltpu.VMEM((384, 1024), LOW),
            pltpu.VMEM((8, 128, 1024), LOW),
        ]
        + sums_scratch()
        + rows_sems(),
        compiler_params=pltpu.CompilerParams(
            collective_id=2, has_side_effects=True, vmem_limit_bytes=LIMIT
        ),
    )(*arrays)


def backward_kernel(
    branch,
    output_weight,
    attended,
    queries,
    keys,
    keys_turned,
    values_turned,
    totals,
    marks,
    prefix,
    cosine_step,
    sine_step,
    weights,
    hidden_one,
    rows,
    middle_grad,
    middle,
    out_part,
    weight_grads,
    down_grad,
    gain_two_term,
    layer_output,
    input_grad,
    firsts_grad,
    query_out,
    key_out,
    value_out,
    output_out,
    packed_out,
    down_out,
    gains,
    branch_full,
    out_grad,
    query_grad,
    key_acc,
    value_acc,
    three,
    part,
    qkv_grads,
    qkv_out,
    output_grad,
    gain_own,
    gain_in,
    gain_part,
    gain_rep,
    value_blocks,
    *sems,
):
    rep, fsdp, z, x = plane_place()
    core, level = lax.rem(rep, 2), rep // 2
    partner = rep + 1 - 2 * core
    above = rep + 2 - 4 * level
    slant = 3 - rep
    others = [lax.rem(fsdp + k, 8) for k in range(1, 8)]
    greet([(rep, other) for other in others] + [(partner, fsdp), (above, fsdp), (slant, fsdp)])
    out_sums = Sums(*sems[:6])
    sums = Sums(*sems[6:12])
    flow = Rows(branch, branch_full, *sems[12:15])
    packed_flow = Collect(weight_grads, packed_out, *sems[15:24])
    qkv_flow = Collect(qkv_grads, qkv_out, *sems[24:33])
    down_flow = CollectRows(down_grad, down_out, *sems[33:38])
    output_flow = CollectRows(output_grad, output_out, *sems[38:43])
    g_send, g_recv, gr_send, gr_recv, v_send, v_recv = sems[43:]

    flow.start()
    packed_flow.start()
    down_flow.start()

    def pull(block):
        at = piece(block, 128)
        out_grad[at, :] = times_transposed(branch_full[block], output_weight[...]).astype(LOW)

    flow.kept()
    pull(fsdp)

    def own_column(k, carry):
        pull(flow.pass_on(k))
        return carry

    lax.fori_loop(0, 3, own_column, 0)
    packed_flow.fold_pair()
    down_flow.fold_pair()
    for k in range(4):
        out_sums.give(k, out_part.at[2 * out_sums.other(k) + 1 - x])

    def other_column(k, carry):
        pull(flow.across(lax.rem(z + k, 4)))
        return carry

    lax.fori_loop(0, 4, other_column, 0)
    output_grad[...] = transposed_times(
        attended[...], branch_full[...].reshape(8 * 128, D)
    ).astype(LOW)
    output_flow.start()
    key_acc[...] = jnp.zeros_like(key_acc)
    value_acc[...] = jnp.zeros_like(value_acc)
    prefix_last = (prefix[0] - 1).astype(WIDE)
    masks = [head_lanes(head) for head in range(2)]

    def attend_back(block, carry):
        at = piece(block, 128)
        query, grad = queries[at, :], out_grad[at, :]
        log_total = totals[at, :]
        allowed = marks[0:1, :] <= limit_column(marks, block, prefix_last)
        result = None
        lows, score_grads, turned_queries, turned_grads = [], [], [], []
        for head in range(2):
            query_here, grad_here = only(masks[head], query), only(masks[head], grad)
            scores = matmul(query_here, keys_turned[...]) * E ** (-0.5)
            column = log_total[:, head * E : head * E + 1]
            probabilities = jnp.where(allowed, jnp.exp(scores - column), 0.0)
            prob_grad = matmul(grad_here, values_turned[...])
            delta = jnp.sum(probabilities * prob_grad, axis=-1, keepdims=True)
            score_grad = (probabilities * (prob_grad - delta)).astype(LOW)
            out = matmul(score_grad, keys[...])
            result = out if head == 0 else jnp.where(masks[0], result, out)
            lows.append(probabilities.astype(LOW))
            score_grads.append(score_grad)
            turned_queries.append(query_here.astype(WIDE).T)
            turned_grads.append(grad_here.astype(WIDE).T)
        query_grad[at, :] = result
        key_acc[...] += matmul(
            jnp.concatenate(turned_queries, axis=1).astype(LOW),
            jnp.concatenate(score_grads, axis=0),
        )
        value_acc[...] += matmul(
            jnp.concatenate(turned_grads, axis=1).astype(LOW), jnp.concatenate(lows, axis=0)
        )

        @pl.when(block == 1)
        def step_one():
            packed_flow.fold_level()
            down_flow.fold_level()
            output_flow.fold_pair()

        @pl.when((block >= 2) & (block < 5))
        def step_two():
            other = out_sums.other(block - 2)
            out_sums.forward(block - 2, out_part[2 * other + x].astype(WIDE))

        @pl.when(block == 5)
        def step_three():
            packed_flow.land()
            down_flow.relay()
            output_flow.fold_level()

        @pl.when(block == 7)
        def step_four():
            packed_flow.relay()
            output_flow.relay()

        return carry

    lax.fori_loop(0, 8, attend_back, 0)

    def close(block):
        at = piece(block, 128)
        cosine, sine = turn_tables(marks, block, cosine_step, sine_step)
        three[at, 0:128] = turn(query_grad[at, :] * E ** (-0.5), cosine, -sine).astype(LOW)
        three[at, 128:256] = turn(key_acc[:, at].T * E ** (-0.5), cosine, -sine).astype(LOW)
        value_grad = (0.5 * value_acc[:, at].T).astype(LOW)
        three[at, 256:384] = value_grad
        value_blocks[block] = value_grad
        return times_transposed(three[at, :], weights[...].reshape(8 * 128, 384))

    def first_phase(k, carry):
        other = sums.other(k)
        block = 2 * other + 1 - x
        part[block] = close(block).astype(LOW)
        sums.give(k, part.at[block])
        return carry

    def second_phase(k, carry):
        block = 2 * sums.other(k) + x
        part[block] = close(block).astype(LOW)
        return carry

    lax.fori_loop(0, 4, first_phase, 0)
    lax.fori_loop(0, 4, second_phase, 0)
    for k, other in enumerate(others):
        remote(
            value_blocks.at[other],
            firsts_grad.at[:, piece(fsdp, 128)],
            v_send.at[k],
            v_recv.at[fsdp],
            rep,
            other,
        ).start()
    firsts_grad[:, piece(fsdp, 128)] = value_blocks[fsdp]

    def grads(i, carry):
        lanes = piece(i, 128)
        turned = hidden_one[:, :, lanes].reshape(8 * 128, 128)
        qkv_grads[i] = transposed_times(turned, three[...]).astype(LOW)
        return carry

    lax.fori_loop(0, 8, grads, 0)
    qkv_flow.start()
    layer_output[...] = (middle[...] + out_sums.total(out_part[fsdp].astype(WIDE))).astype(LOW)
    sums.forward(0, part[2 * sums.other(0) + x].astype(WIDE))
    qkv_flow.fold_pair()
    sums.forward(1, part[2 * sums.other(1) + x].astype(WIDE))
    qkv_flow.fold_level()
    sums.forward(2, part[2 * sums.other(2) + x].astype(WIDE))
    qkv_flow.land()
    hidden_grad = sums.total(part[fsdp].astype(WIDE))
    entry = rows[...].astype(WIDE)
    scale = lax.rsqrt(jnp.mean(entry * entry, axis=-1, keepdims=True) + epsilon)
    normed = entry * scale
    normed_grad = hidden_grad * marks[1:2, :]
    gain_term = jnp.sum(hidden_grad * normed, axis=0, keepdims=True)
    for i in range(8):
        lanes = slice(128 * i, 128 * i + 128)
        gain_own[i, 0:1, :] = gain_term[:, lanes]
        gain_own[i, 1:8, :] = gain_two_term[1:8, lanes]
    for k, other in enumerate(others):
        remote(
            gain_own.at[other], gain_in.at[fsdp], g_send.at[k], g_recv.at[fsdp], rep, other
        ).start()
    back = scale * (normed_grad - normed * jnp.mean(normed_grad * normed, axis=-1, keepdims=True))
    input_grad[...] = middle_grad[...] + back
    qkv_flow.relay()
    gain_in[fsdp] = gain_own[fsdp]
    for other in others:
        arrived(gain_in.at[other], g_recv.at[other])
    gain_part[...] = jnp.sum(gain_in[...], axis=0)
    for k, target in enumerate((partner, above, slant)):
        remote(
            gain_part, gain_rep.at[rep], gr_send.at[k], gr_recv.at[rep], target, fsdp
        ).start()
    gain_rep[rep] = gain_part[...]
    for k, other in enumerate(others):
        arrived(firsts_grad.at[:, piece(other, 128)], v_recv.at[other])
        arrived(value_blocks.at[0], v_send.at[k])
        arrived(gain_own.at[0], g_send.at[k])
    for k, source in enumerate((partner, above, slant)):
        arrived(gain_rep.at[source], gr_recv.at[source])
        arrived(gain_part, gr_send.at[k])
    gains[...] = jnp.sum(gain_rep[...], axis=0)
    packed_flow.finish()
    down_flow.finish()
    output_flow.finish()
    qkv_flow.finish()
    for i in range(8):
        lanes = slice(128 * i, 128 * i + 128)
        query_out[:, lanes] = qkv_out[i, :, 0:128]
        key_out[:, lanes] = qkv_out[i, :, 128:256]
        value_out[:, lanes] = qkv_out[i, :, 256:384]
    flow.sent()
    out_sums.sent()
    sums.sent()


def backward(*arrays):
    used = arrays[19].shape[0]
    return pl.pallas_call(
        backward_kernel,
        out_shape=[
            low_shape(128, 1024),
            wide_shape(128, 1024),
            low_shape(128, 1024),
            low_shape(128, 1024),
            low_shape(128, 1024),
            low_shape(128, 1024),
            low_shape(128, 1024),
            low_shape(8, 128, 768),
            low_shape(used, 1024),
            wide_shape(8, 128),
        ],
        in_specs=[VM] * 9 + [SM] + [VM] * 11,
        out_specs=[VM] * 10,
        scratch_shapes=[
            pltpu.VMEM((8, 128, 1024), LOW),
            pltpu.VMEM((1024, 128), LOW),
            pltpu.VMEM((1024, 128), WIDE),
            pltpu.VMEM((128, 1024), WIDE),
            pltpu.VMEM((128, 1024), WIDE),
            pltpu.VMEM((1024, 384), LOW),
            pltpu.VMEM((8, 128, 1024), LOW),
            pltpu.VMEM((8, 128, 384), LOW),
            pltpu.VMEM((8, 128, 384), LOW),
            pltpu.VMEM((128, 1024), LOW),
            pltpu.VMEM((8, 8, 128), WIDE),
            pltpu.VMEM((8, 8, 128), WIDE),
            pltpu.VMEM((8, 128), WIDE),
            pltpu.VMEM((4, 8, 128), WIDE),
            pltpu.VMEM((8, 128, 128), LOW),
        ]
        + sums_scratch()
        + sums_scratch()
        + rows_sems()
        + collect_scratch(128, 768)
        + collect_scratch(128, 384)
        + collect_rows_scratch(used)
        + collect_rows_scratch(128)
        + [DMA((7,)), DMA((8,)), DMA((3,)), DMA((4,)), DMA((7,)), DMA((8,))],
        compiler_params=pltpu.CompilerParams(
            collective_id=3, has_side_effects=True, vmem_limit_bytes=LIMIT
        ),
    )(*arrays)


def to_blocks(array):
    rows, width = array.shape
    return array.reshape(rows, 8, width // 8).transpose(1, 0, 2)


def from_blocks(array):
    count, rows, width = array.shape
    return array.transpose(1, 0, 2).reshape(rows, count * width)


def shards_plane(
    inputs,
    first_values,
    prefix,
    positions,
    first_gain,
    query_weight,
    key_weight,
    value_weight,
    output_weight,
    second_gain,
    gate_weight,
    up_weight,
    down_weight,
    cotangent,
):
    count = inputs.shape[0]
    hidden = gate_weight.shape[1] // 8
    half_width = E // 2
    frequency = jnp.exp(jnp.arange(half_width, dtype=WIDE) * (-math.log(10000.0) / half_width))
    frequency = jnp.tile(frequency, 128 // half_width)[None, :]
    starts = positions.reshape(2, -1)[:, :1].astype(WIDE) * frequency
    step_angles = jnp.arange(count // 2, dtype=WIDE)[:, None] * frequency
    steps = (jnp.cos(step_angles), jnp.sin(step_angles))
    small = jnp.concatenate(
        [
            positions.astype(WIDE)[None],
            first_gain.astype(WIDE)[None],
            second_gain.astype(WIDE)[None],
            jnp.stack([jnp.cos(starts), jnp.sin(starts)], axis=1).reshape(4, -1),
            jnp.zeros((1, count), WIDE),
        ],
        axis=0,
    )
    pad = jnp.zeros((8, count, 384 - hidden), LOW)
    packed = jnp.concatenate([to_blocks(gate_weight), pad, to_blocks(up_weight), pad], axis=2)
    prefix_here = lax.dynamic_slice_in_dim(prefix, lax.axis_index("rep"), 1)
    (
        hidden_one,
        queries,
        keys,
        keys_turned,
        values_turned,
        attended,
        totals,
        weights,
        packed_full,
        grad_full,
        marks,
        middle,
        hidden_two,
    ) = forward(
        inputs,
        small,
        prefix_here,
        *steps,
        query_weight,
        key_weight,
        value_weight,
        output_weight,
        first_values,
        cotangent,
        packed,
    )
    middle_grad, branch, gain_two_term, weight_grads, down_grad, out_part = feed_forward(
        hidden_two,
        packed_full.reshape(8 * count, -1),
        down_weight,
        grad_full,
        middle,
        cotangent,
        marks,
    )
    (
        layer_output,
        input_grad,
        firsts_grad,
        query_grad,
        key_grad,
        value_grad,
        output_grad,
        packed_grad,
        down_sum,
        gains,
    ) = backward(
        branch,
        output_weight,
        attended,
        queries,
        keys,
        keys_turned,
        values_turned,
        totals,
        marks,
        prefix_here,
        *steps,
        weights,
        hidden_one,
        inputs,
        middle_grad,
        middle,
        out_part,
        weight_grads,
        down_grad,
        gain_two_term,
    )
    return (
        layer_output,
        input_grad,
        firsts_grad.astype(WIDE),
        gains[0],
        query_grad.astype(WIDE),
        key_grad.astype(WIDE),
        value_grad.astype(WIDE),
        output_grad.astype(WIDE),
        gains[1],
        from_blocks(packed_grad[:, :, :hidden]).astype(WIDE),
        from_blocks(packed_grad[:, :, 384 : 384 + hidden]).astype(WIDE),
        down_sum.astype(WIDE),
    )


def pick_body(mesh):
    if mesh.shape["fsdp"] == 8 and mesh.shape["rep"] == 4:
        return shards_plane
    return shards_general


def solution(mesh):
    placed = (
        P(("rep", "fsdp"), None),
        P(("rep", "fsdp"), None),
        P(),
        P(("rep", "fsdp")),
        P("fsdp"),
        P("fsdp", None),
        P("fsdp", None),
        P("fsdp", None),
        P("fsdp", None),
        P("fsdp"),
        P("fsdp", None),
        P("fsdp", None),
        P("fsdp", None),
        P(("rep", "fsdp"), None),
    )
    return jax.shard_map(
        pick_body(mesh),
        mesh=mesh,
        in_specs=placed,
        out_specs=(
            P(("rep", "fsdp"), None),
            P(("rep", "fsdp"), None),
            P(("rep", "fsdp"), None),
            P("fsdp"),
            P("fsdp", None),
            P("fsdp", None),
            P("fsdp", None),
            P("fsdp", None),
            P("fsdp"),
            P("fsdp", None),
            P("fsdp", None),
            P("fsdp", None),
        ),
        check_vma=False,
    )
```

```python
import functools
import math
import types

import jax
import jax.numpy as jnp
from jax import lax
from jax.experimental import pallas as pl
from jax.experimental.pallas import tpu as pltpu
from jax.sharding import PartitionSpec as P

D = 1024
H = 16
E = 64


epsilon = 1e-06
masked_score = -1e30


def rms_scale(values):
    return lax.rsqrt(jnp.mean(values * values, axis=-1, keepdims=True) + epsilon)


def rope_tables(places):
    half_width = E // 2
    frequency = jnp.exp(
        jnp.arange(half_width, dtype=jnp.float32) * (-math.log(10000.0) / half_width)
    )
    angles = places.astype(jnp.float32)[:, None] * frequency[None, :]
    return (jnp.cos(angles)[:, None, :], jnp.sin(angles)[:, None, :])


def rope_apply(shaped, cosine, sine_table):
    half_width = shaped.shape[-1] // 2
    first_half = shaped[..., :half_width]
    second_half = shaped[..., half_width:]
    return jnp.concatenate(
        [
            first_half * cosine - second_half * sine_table,
            second_half * cosine + first_half * sine_table,
        ],
        axis=-1,
    )


def rope_undo(shaped, cosine, sine_table):
    half_width = shaped.shape[-1] // 2
    first_half = shaped[..., :half_width]
    second_half = shaped[..., half_width:]
    return jnp.concatenate(
        [
            first_half * cosine + second_half * sine_table,
            second_half * cosine - first_half * sine_table,
        ],
        axis=-1,
    )


def times_transposed(left, right):
    return lax.dot_general(
        left, right, (((1,), (1,)), ((), ())), preferred_element_type=jnp.float32
    )


def transposed_times(left, right):
    return lax.dot_general(
        left, right, (((0,), (0,)), ((), ())), preferred_element_type=jnp.float32
    )


def block_rows(count):
    size_now = count
    while size_now > 1024 and size_now % 2 == 0:
        size_now = size_now // 2
    return size_now


def split_blocks(array, size_now):
    return array.reshape((array.shape[0] // size_now, size_now) + array.shape[1:])


def masked_scores(queries, key_rows, limits, key_places):
    scores = jnp.einsum(
        "qhe,khe->hqk", queries, key_rows, preferred_element_type=jnp.float32
    ) * E ** (-0.5)
    allowed = key_places[None, None, :] <= limits[None, :, None]
    return (scores, allowed)


def grad_block(queries, key_rows, value_rows, limits, key_places, out_low, log_total, delta_rows):
    scores, allowed = masked_scores(queries, key_rows, limits, key_places)
    probabilities = jnp.where(allowed, jnp.exp(scores - log_total[:, :, None]), 0.0)
    prob_grad = jnp.einsum("qhe,khe->hqk", out_low, value_rows, preferred_element_type=jnp.float32)
    score_grad = (probabilities * (prob_grad - delta_rows[:, :, None])).astype(jnp.bfloat16)
    return (probabilities.astype(jnp.bfloat16), score_grad)


def norm_back(hidden_grad, normed, gain_float, scale_rows):
    normed_grad = hidden_grad * gain_float
    gain_term = jnp.sum(hidden_grad * normed, axis=0)
    rows_grad = scale_rows * (
        normed_grad - normed * jnp.mean(normed_grad * normed, axis=-1, keepdims=True)
    )
    return (gain_term, rows_grad)


def shards_general(
    inputs,
    first_values,
    prefix,
    positions,
    first_gain,
    query_weight,
    key_weight,
    value_weight,
    output_weight,
    second_gain,
    gate_weight,
    up_weight,
    down_weight,
    cotangent,
):
    token_count = inputs.shape[0]
    gain_one, query_full, key_full, value_full, output_full = (
        lax.all_gather(first_gain, "fsdp", axis=0, tiled=True),
        lax.all_gather(query_weight, "fsdp", axis=0, tiled=True),
        lax.all_gather(key_weight, "fsdp", axis=0, tiled=True),
        lax.all_gather(value_weight, "fsdp", axis=0, tiled=True),
        lax.all_gather(output_weight, "fsdp", axis=0, tiled=True),
    )
    all_places = lax.all_gather(positions, "fsdp", axis=0, tiled=True)
    prefix_here = lax.dynamic_index_in_dim(prefix, lax.axis_index("rep"), keepdims=False)
    own_limits = jnp.maximum(positions, prefix_here - 1)
    cosine, sine_table = rope_tables(positions)
    rows_float = inputs.astype(jnp.float32)
    scale_one = rms_scale(rows_float)
    normed_one = rows_float * scale_one
    gain_one_float = gain_one.astype(jnp.float32)
    hidden_one = (normed_one * gain_one_float).astype(jnp.bfloat16)
    query_pre = jnp.dot(hidden_one, query_full, preferred_element_type=jnp.float32)
    key_pre = jnp.dot(hidden_one, key_full, preferred_element_type=jnp.float32)
    value_pre = jnp.dot(hidden_one, value_full, preferred_element_type=jnp.float32)
    queries = rope_apply(query_pre.reshape(token_count, H, E), cosine, sine_table).astype(
        jnp.bfloat16
    )
    key_rows = (
        rope_apply(key_pre.reshape(token_count, H, E), cosine, sine_table)
        .astype(jnp.bfloat16)
        .reshape(token_count, D)
    )
    mixed_values = (0.5 * value_pre + 0.5 * first_values.astype(jnp.float32)).astype(jnp.bfloat16)
    start_state = (
        jnp.full((H, token_count), masked_score, jnp.float32),
        jnp.zeros((H, token_count), jnp.float32),
        jnp.zeros((token_count, H, E), jnp.float32),
    )
    running = start_state
    key_piece = lax.all_gather(key_rows, "fsdp", axis=0, tiled=True)
    value_piece = lax.all_gather(mixed_values, "fsdp", axis=0, tiled=True)
    count = key_piece.shape[0]
    size_now = block_rows(count)

    def forward_step(state_now, blocks):
        row_max, row_sum, accum = state_now
        key_block, value_block, place_block = blocks
        scores, allowed = masked_scores(
            queries, key_block.reshape(-1, H, E), own_limits, place_block
        )
        new_max = jnp.maximum(row_max, jnp.max(jnp.where(allowed, scores, masked_score), axis=-1))
        rescale = jnp.exp(row_max - new_max)
        weights = jnp.where(allowed, jnp.exp(scores - new_max[:, :, None]), 0.0)
        row_sum = row_sum * rescale + jnp.sum(weights, axis=-1)
        accum = accum * rescale.T[:, :, None] + jnp.einsum(
            "hqk,khe->qhe",
            weights.astype(jnp.bfloat16),
            value_block.reshape(-1, H, E),
            preferred_element_type=jnp.float32,
        )
        return ((new_max, row_sum, accum), None)

    running, unused = lax.scan(
        forward_step,
        running,
        (
            split_blocks(key_piece, size_now),
            split_blocks(value_piece, size_now),
            split_blocks(all_places, size_now),
        ),
    )
    row_max, row_sum, accum = running
    log_total = row_max + jnp.log(row_sum)
    attended = accum / row_sum.T[:, :, None]
    attended_low = attended.reshape(token_count, D).astype(jnp.bfloat16)
    middle = rows_float + jnp.dot(attended_low, output_full, preferred_element_type=jnp.float32)
    mlp_forward = (
        lax.all_gather(second_gain, "fsdp", axis=0, tiled=True),
        lax.all_gather(gate_weight, "fsdp", axis=0, tiled=True),
        lax.all_gather(up_weight, "fsdp", axis=0, tiled=True),
        lax.all_gather(down_weight, "fsdp", axis=0, tiled=True),
    )
    gain_two, gate_full, up_full, down_full = mlp_forward
    scale_two = rms_scale(middle)
    normed_two = middle * scale_two
    hidden_two = (normed_two * gain_two.astype(jnp.float32)).astype(jnp.bfloat16)
    gate_pre = jnp.dot(hidden_two, gate_full, preferred_element_type=jnp.float32)
    up_pre = jnp.dot(hidden_two, up_full, preferred_element_type=jnp.float32)
    sigmoid_gate = jax.nn.sigmoid(gate_pre)
    activated = (gate_pre * sigmoid_gate * up_pre).astype(jnp.bfloat16)
    layer_output = (
        middle + jnp.dot(activated, down_full, preferred_element_type=jnp.float32)
    ).astype(jnp.bfloat16)
    gain_two_back, gate_back, up_back, down_back = (
        lax.all_gather(second_gain, "fsdp", axis=0, tiled=True),
        lax.all_gather(gate_weight, "fsdp", axis=0, tiled=True),
        lax.all_gather(up_weight, "fsdp", axis=0, tiled=True),
        lax.all_gather(down_weight, "fsdp", axis=0, tiled=True),
    )
    act_grad = times_transposed(cotangent, down_back)
    down_term = transposed_times(activated, cotangent)
    gate_grad = (act_grad * up_pre * sigmoid_gate * (1.0 + gate_pre * (1.0 - sigmoid_gate))).astype(
        jnp.bfloat16
    )
    up_grad = (act_grad * gate_pre * sigmoid_gate).astype(jnp.bfloat16)
    hidden_two_grad = times_transposed(gate_grad, gate_back) + times_transposed(up_grad, up_back)
    gate_term = transposed_times(hidden_two, gate_grad)
    up_term = transposed_times(hidden_two, up_grad)
    gain_two_term, middle_part = norm_back(
        hidden_two_grad, normed_two, gain_two_back.astype(jnp.float32), scale_two
    )
    middle_grad = cotangent.astype(jnp.float32) + middle_part
    gain_two_sum, gate_sum, up_sum, down_sum = (
        lax.psum_scatter(gain_two_term, "fsdp", scatter_dimension=0, tiled=True),
        lax.psum_scatter(gate_term, "fsdp", scatter_dimension=0, tiled=True),
        lax.psum_scatter(up_term, "fsdp", scatter_dimension=0, tiled=True),
        lax.psum_scatter(down_term, "fsdp", scatter_dimension=0, tiled=True),
    )
    gain_one_back, query_back, key_back, value_back, output_back = (
        lax.all_gather(first_gain, "fsdp", axis=0, tiled=True),
        lax.all_gather(query_weight, "fsdp", axis=0, tiled=True),
        lax.all_gather(key_weight, "fsdp", axis=0, tiled=True),
        lax.all_gather(value_weight, "fsdp", axis=0, tiled=True),
        lax.all_gather(output_weight, "fsdp", axis=0, tiled=True),
    )
    branch_low = middle_grad.astype(jnp.bfloat16)
    output_term = transposed_times(attended_low, branch_low)
    out_flat = times_transposed(branch_low, output_back).astype(jnp.bfloat16)
    out_low = out_flat.reshape(token_count, H, E)
    delta_rows = jnp.sum(out_low.astype(jnp.float32) * attended, axis=-1).T
    zero_rows = jnp.zeros((token_count, H, E), jnp.float32)
    gathered_keys, gathered_values = (
        lax.all_gather(key_rows, "fsdp", axis=0, tiled=True),
        lax.all_gather(mixed_values, "fsdp", axis=0, tiled=True),
    )
    length = gathered_keys.shape[0]
    size_now = block_rows(length)

    def back_step(query_acc, blocks):
        key_block, value_block, place_block = blocks
        key_shaped = key_block.reshape(-1, H, E)
        value_shaped = value_block.reshape(-1, H, E)
        prob_low, score_grad = grad_block(
            queries,
            key_shaped,
            value_shaped,
            own_limits,
            place_block,
            out_low,
            log_total,
            delta_rows,
        )
        query_acc = query_acc + jnp.einsum(
            "hqk,khe->qhe", score_grad, key_shaped, preferred_element_type=jnp.float32
        )
        key_part = jnp.einsum(
            "hqk,qhe->khe", score_grad, queries, preferred_element_type=jnp.float32
        ).reshape(-1, D)
        value_part = jnp.einsum(
            "hqk,qhe->khe", prob_low, out_low, preferred_element_type=jnp.float32
        ).reshape(-1, D)
        return (query_acc, jnp.concatenate([key_part, value_part], axis=1))

    query_acc, parts = lax.scan(
        back_step,
        zero_rows,
        (
            split_blocks(gathered_keys, size_now),
            split_blocks(gathered_values, size_now),
            split_blocks(all_places, size_now),
        ),
    )
    summed = lax.psum_scatter(parts.reshape(length, 2 * D), "fsdp", scatter_dimension=0, tiled=True)
    key_acc = summed[:, :D]
    value_acc = summed[:, D:]
    query_grad = (
        rope_undo(query_acc * E ** (-0.5), cosine, sine_table)
        .reshape(token_count, D)
        .astype(jnp.bfloat16)
    )
    key_grad = (
        rope_undo(key_acc.reshape(token_count, H, E) * E ** (-0.5), cosine, sine_table)
        .reshape(token_count, D)
        .astype(jnp.bfloat16)
    )
    first_values_grad = 0.5 * value_acc
    value_grad = first_values_grad.astype(jnp.bfloat16)
    hidden_one_grad = (
        times_transposed(query_grad, query_back)
        + times_transposed(key_grad, key_back)
        + times_transposed(value_grad, value_back)
    )
    query_term = transposed_times(hidden_one, query_grad)
    key_term = transposed_times(hidden_one, key_grad)
    value_term = transposed_times(hidden_one, value_grad)
    gain_one_term, input_part = norm_back(
        hidden_one_grad, normed_one, gain_one_back.astype(jnp.float32), scale_one
    )
    input_grad = middle_grad + input_part
    gain_one_sum, query_sum, key_sum, value_sum, output_sum = (
        lax.psum_scatter(gain_one_term, "fsdp", scatter_dimension=0, tiled=True),
        lax.psum_scatter(query_term, "fsdp", scatter_dimension=0, tiled=True),
        lax.psum_scatter(key_term, "fsdp", scatter_dimension=0, tiled=True),
        lax.psum_scatter(value_term, "fsdp", scatter_dimension=0, tiled=True),
        lax.psum_scatter(output_term, "fsdp", scatter_dimension=0, tiled=True),
    )
    totals = (
        lax.psum(gain_one_sum.astype(jnp.bfloat16), "rep").astype(jnp.float32),
        lax.psum(query_sum.astype(jnp.bfloat16), "rep").astype(jnp.float32),
        lax.psum(key_sum.astype(jnp.bfloat16), "rep").astype(jnp.float32),
        lax.psum(value_sum.astype(jnp.bfloat16), "rep").astype(jnp.float32),
        lax.psum(output_sum.astype(jnp.bfloat16), "rep").astype(jnp.float32),
        lax.psum(gain_two_sum.astype(jnp.bfloat16), "rep").astype(jnp.float32),
        lax.psum(gate_sum.astype(jnp.bfloat16), "rep").astype(jnp.float32),
        lax.psum(up_sum.astype(jnp.bfloat16), "rep").astype(jnp.float32),
        lax.psum(down_sum.astype(jnp.bfloat16), "rep").astype(jnp.float32),
    )
    return (
        layer_output,
        input_grad,
        first_values_grad,
        totals[0],
        totals[1],
        totals[2],
        totals[3],
        totals[4],
        totals[5],
        totals[6],
        totals[7],
        totals[8],
    )


MESH = pl.DeviceIdType.MESH
LOW = jnp.bfloat16
WIDE = jnp.float32
VM = pl.BlockSpec(memory_space=pltpu.VMEM)
SM = pl.BlockSpec(memory_space=pltpu.SMEM)
DMA = pltpu.SemaphoreType.DMA
LIMIT = 63 * 1024 * 1024


def remote(src, dst, send_sem, recv_sem, rep, fsdp):
    return pltpu.make_async_remote_copy(
        src_ref=src,
        dst_ref=dst,
        send_sem=send_sem,
        recv_sem=recv_sem,
        device_id={"rep": rep, "fsdp": fsdp},
        device_id_type=MESH,
    )


def arrived(place, sem):
    pltpu.make_async_copy(place, place, sem).wait()


def greet(peers):
    barrier = pltpu.get_barrier_semaphore()
    for rep, fsdp in peers:
        pl.semaphore_signal(
            barrier, inc=1, device_id={"rep": rep, "fsdp": fsdp}, device_id_type=MESH
        )
    pl.semaphore_wait(barrier, len(peers))


def plane_place():
    rep, fsdp = lax.axis_index("rep"), lax.axis_index("fsdp")
    return rep, fsdp, fsdp // 2, fsdp % 2


def piece(index, size):
    return pl.ds(pl.multiple_of(index * size, size), size)


def matmul(left, right):
    return jnp.dot(left, right, preferred_element_type=WIDE)


class Rows:
    def __init__(self, own, full, keep, send, recv):
        self.own, self.full, self.keep, self.send, self.recv = own, full, keep, send, recv
        self.rep, self.fsdp, self.z, self.x = plane_place()
        self.side = 2 * self.z + 1 - self.x

    def push(self, src, block, sem, target):
        return remote(
            src, self.full.at[block], self.send.at[sem], self.recv.at[block], self.rep, target
        )

    def start(self):
        z, x = self.z, self.x

        @pl.when(z < 3)
        def up():
            self.push(self.own, self.fsdp, 0, 2 * (z + 1) + x).start()

        @pl.when(z > 0)
        def down():
            self.push(self.own, self.fsdp, 1, 2 * (z - 1) + x).start()

        self.push(self.own, self.fsdp, 2, self.side).start()
        pltpu.make_async_copy(self.own, self.full.at[self.fsdp], self.keep).start()

    def kept(self):
        pltpu.make_async_copy(self.own, self.full.at[self.fsdp], self.keep).wait()

    def line(self, k):
        high, odd = self.z // 2, self.z % 2
        first = 1 - (k + 1) // 2
        low_side = k + 1 - odd * first
        high_side = 2 - k + first * (1 - odd)
        return low_side + high * (high_side - low_side)

    def pass_on(self, k):
        z, x = self.z, self.x
        other = self.line(k)
        block = 2 * other + x
        place = self.full.at[block]
        arrived(place, self.recv.at[block])

        @pl.when((other < z) & (z < 3))
        def up():
            self.push(place, block, 3 + k, 2 * (z + 1) + x).start()

        @pl.when((other > z) & (z > 0))
        def down():
            self.push(place, block, 3 + k, 2 * (z - 1) + x).start()

        self.push(place, block, 6 + k, self.side).start()
        return block

    def across(self, other):
        block = 2 * other + 1 - self.x
        arrived(self.full.at[block], self.recv.at[block])
        return block

    def sent(self):
        z = self.z
        place = self.full.at[0]

        def done(sem):
            arrived(place, self.send.at[sem])

        pl.when(z < 3)(lambda: done(0))
        pl.when(z > 0)(lambda: done(1))
        done(2)
        for k in range(3):
            done(6 + k)

            @pl.when((z > 0) & (z < 3))
            def relayed():
                done(3 + k)


def rows_sems():
    return [DMA(()), DMA((9,)), DMA((8,))]


class Sums:
    def __init__(self, side_in, summed, line_in, send, side_recv, line_recv):
        self.side_in, self.summed, self.line_in = side_in, summed, line_in
        self.send, self.side_recv, self.line_recv = send, side_recv, line_recv
        self.rep, self.fsdp, self.z, self.x = plane_place()
        self.side = 2 * self.z + 1 - self.x

    def other(self, k):
        return lax.rem(self.z + 1 + k, 4)

    def give(self, k, ref):
        other = self.other(k)
        remote(
            ref, self.side_in.at[other], self.send.at[k], self.side_recv.at[other], self.rep, self.side
        ).start()

    def forward(self, k, value):
        other = self.other(k)
        arrived(self.side_in.at[other], self.side_recv.at[other])
        self.summed[other] = (value + self.side_in[other].astype(WIDE)).astype(LOW)
        remote(
            self.summed.at[other],
            self.line_in.at[self.z],
            self.send.at[4 + k],
            self.line_recv.at[self.z],
            self.rep,
            2 * other + self.x,
        ).start()

    def total(self, value):
        arrived(self.side_in.at[self.z], self.side_recv.at[self.z])
        value = value + self.side_in[self.z].astype(WIDE)
        for k in range(3):
            other = self.other(k)
            arrived(self.line_in.at[other], self.line_recv.at[other])
            value = value + self.line_in[other].astype(WIDE)
        return value

    def sent(self):
        for k in range(7):
            arrived(self.side_in.at[0], self.send.at[k])


def sums_scratch():
    return [pltpu.VMEM((4, 128, D), LOW)] * 3 + [DMA((7,)), DMA((4,)), DMA((4,))]


class Collect:
    def __init__(self, grads, out, pair_in, pair_sum, level_in, level_sum, landed, send, recv, cross_send, cross_recv):
        self.grads, self.out = grads, out
        self.pair_in, self.pair_sum = pair_in, pair_sum
        self.level_in, self.level_sum, self.landed = level_in, level_sum, landed
        self.send, self.recv, self.cross_send, self.cross_recv = send, recv, cross_send, cross_recv
        self.rep, self.fsdp, _, _ = plane_place()
        self.core, self.level = lax.rem(self.rep, 2), self.rep // 2
        self.partner = self.rep + 1 - 2 * self.core
        self.above = self.rep + 2 - 4 * self.level
        self.half = grads.shape[1] // 2
        self.fourth = self.half // 2

    def to(self, src, dst, index, rep):
        return remote(src, dst, self.send.at[index], self.recv.at[index], rep, self.fsdp)

    def start(self):
        src = self.grads.at[:, piece(1 - self.core, self.half)]
        self.to(src, self.pair_in, 0, self.partner).start()

    def fold_pair(self):
        arrived(self.pair_in, self.recv.at[0])
        mine = piece(self.core, self.half)

        def add(i, carry):
            self.pair_sum[i] = (
                self.grads[i, mine].astype(WIDE) + self.pair_in[i].astype(WIDE)
            ).astype(LOW)
            return carry

        lax.fori_loop(0, 8, add, 0)
        src = self.pair_sum.at[:, piece(1 - self.level, self.fourth)]
        self.to(src, self.level_in, 1, self.above).start()

    def fold_level(self):
        arrived(self.level_in, self.recv.at[1])
        mine = piece(self.level, self.fourth)

        def add(i, carry):
            self.level_sum[i] = (
                self.pair_sum[i, mine].astype(WIDE) + self.level_in[i].astype(WIDE)
            ).astype(LOW)
            return carry

        lax.fori_loop(0, 8, add, 0)
        for k in range(7):
            other = lax.rem(self.fsdp + k + 1, 8)
            remote(
                self.level_sum.at[other],
                self.landed.at[self.fsdp],
                self.cross_send.at[k],
                self.cross_recv.at[self.fsdp],
                self.rep,
                other,
            ).start()

    def quarter(self, core, level):
        return self.out.at[:, piece(2 * core + level, self.fourth)]

    def land(self):
        for k in range(7):
            other = lax.rem(self.fsdp + k + 1, 8)
            arrived(self.landed.at[other], self.cross_recv.at[other])
        self.landed[self.fsdp] = self.level_sum[self.fsdp]
        mine = piece(2 * self.core + self.level, self.fourth)
        place = self.quarter(self.core, self.level)
        self.to(self.landed, place, 2, self.above).start()
        self.to(self.landed, place, 3, self.partner).start()
        for i in range(8):
            self.out[i, mine] = self.landed[i]

    def relay(self):
        place = self.quarter(self.core, 1 - self.level)
        arrived(place, self.recv.at[2])
        self.to(place, place, 4, self.partner).start()

    def finish(self):
        arrived(self.quarter(1 - self.core, self.level), self.recv.at[3])
        arrived(self.quarter(1 - self.core, 1 - self.level), self.recv.at[4])
        arrived(self.pair_in, self.send.at[0])
        arrived(self.level_in, self.send.at[1])
        for k in range(3):
            arrived(self.landed, self.send.at[2 + k])
        for k in range(7):
            arrived(self.landed.at[0], self.cross_send.at[k])


def collect_scratch(high, wide):
    return [
        pltpu.VMEM((8, high // 2, wide), LOW),
        pltpu.VMEM((8, high // 2, wide), LOW),
        pltpu.VMEM((8, high // 4, wide), LOW),
        pltpu.VMEM((8, high // 4, wide), LOW),
        pltpu.VMEM((8, high // 4, wide), LOW),
        DMA((5,)),
        DMA((5,)),
        DMA((7,)),
        DMA((8,)),
    ]


class CollectRows:
    def __init__(self, rows, out, pair_in, pair_sum, level_in, send, recv):
        self.rows, self.out = rows, out
        self.pair_in, self.pair_sum, self.level_in = pair_in, pair_sum, level_in
        self.send, self.recv = send, recv
        self.rep, self.fsdp, _, _ = plane_place()
        self.core, self.level = lax.rem(self.rep, 2), self.rep // 2
        self.partner = self.rep + 1 - 2 * self.core
        self.above = self.rep + 2 - 4 * self.level
        self.half = rows.shape[1] // 2
        self.fourth = self.half // 2

    def to(self, src, dst, index, rep):
        return remote(src, dst, self.send.at[index], self.recv.at[index], rep, self.fsdp)

    def start(self):
        src = self.rows.at[:, piece(1 - self.core, self.half)]
        self.to(src, self.pair_in, 0, self.partner).start()

    def fold_pair(self):
        arrived(self.pair_in, self.recv.at[0])
        self.pair_sum[...] = (
            self.rows[:, piece(self.core, self.half)].astype(WIDE) + self.pair_in[...].astype(WIDE)
        ).astype(LOW)
        src = self.pair_sum.at[:, piece(1 - self.level, self.fourth)]
        self.to(src, self.level_in, 1, self.above).start()

    def quarter(self, core, level):
        return self.out.at[:, piece(2 * core + level, self.fourth)]

    def fold_level(self):
        arrived(self.level_in, self.recv.at[1])
        mine = piece(2 * self.core + self.level, self.fourth)
        self.out[:, mine] = (
            self.pair_sum[:, piece(self.level, self.fourth)].astype(WIDE)
            + self.level_in[...].astype(WIDE)
        ).astype(LOW)
        place = self.quarter(self.core, self.level)
        self.to(place, place, 2, self.above).start()
        self.to(place, place, 3, self.partner).start()

    def relay(self):
        place = self.quarter(self.core, 1 - self.level)
        arrived(place, self.recv.at[2])
        self.to(place, place, 4, self.partner).start()

    def finish(self):
        arrived(self.quarter(1 - self.core, self.level), self.recv.at[3])
        arrived(self.quarter(1 - self.core, 1 - self.level), self.recv.at[4])
        arrived(self.pair_in, self.send.at[0])
        for k in range(4):
            arrived(self.level_in, self.send.at[1 + k])


def collect_rows_scratch(tall):
    return [
        pltpu.VMEM((tall, D // 2), LOW),
        pltpu.VMEM((tall, D // 2), LOW),
        pltpu.VMEM((tall, D // 4), LOW),
        DMA((5,)),
        DMA((5,)),
    ]


def turn_rates():
    lane = lax.broadcasted_iota(jnp.int32, (1, 128), 1) % (E // 2)
    return jnp.exp(lane.astype(WIDE) * (-math.log(10000.0) / (E // 2)))


def turn_tables(marks, block, cosine_step, sine_step):
    lanes = piece(block, 128)
    cosines, sines = [], []
    for run in range(2):
        c = marks[3 + 2 * run : 4 + 2 * run, lanes]
        s = marks[4 + 2 * run : 5 + 2 * run, lanes]
        cosines.append(c * cosine_step[...] - s * sine_step[...])
        sines.append(s * cosine_step[...] + c * sine_step[...])
    lane = lax.broadcasted_iota(jnp.int32, (1, 128), 1)
    sign = jnp.where(lane % E < E // 2, -1.0, 1.0)
    return jnp.concatenate(cosines, axis=0), jnp.concatenate(sines, axis=0) * sign


def turn(array, cosine, sine):
    lane = lax.broadcasted_iota(jnp.int32, (1, 128), 1)
    swapped = jnp.where(lane % E < E // 2, pltpu.roll(array, 96, 1), pltpu.roll(array, 32, 1))
    return array * cosine + swapped * sine


def limit_column(marks, block, prefix_last):
    tile = marks[0:1, piece(block, 128)]
    lane = lax.broadcasted_iota(jnp.int32, (1, 128), 1)
    row = lax.broadcasted_iota(jnp.int32, (128, 1), 0)
    first = jnp.sum(jnp.where(lane == 0, tile, 0.0), axis=1, keepdims=True)
    second = jnp.sum(jnp.where(lane == 64, tile, 0.0), axis=1, keepdims=True)
    places = jnp.where(row < 64, first + row.astype(WIDE), second + (row - 64).astype(WIDE))
    return jnp.maximum(places, prefix_last)


def head_lanes(head):
    lane = lax.broadcasted_iota(jnp.int32, (1, 128), 1)
    return (lane // E) == head


def only(mask, array):
    return jnp.where(mask, array.astype(WIDE), 0.0).astype(LOW)


def low_shape(*shape):
    return jax.ShapeDtypeStruct(shape, LOW)


def wide_shape(*shape):
    return jax.ShapeDtypeStruct(shape, WIDE)


def scratch_of(hidden):
    low, wide = (lambda *shape: pltpu.VMEM(shape, LOW)), (lambda *shape: pltpu.VMEM(shape, WIDE))
    single = {
        "marks": wide(8, 1024),
        "small": wide(8, 128),
        "cosine_step": wide(64, 128),
        "sine_step": wide(64, 128),
        "rows_full": low(8, 128, 1024),
        "firsts_full": low(8, 128, 128),
        "weights": low(8, 128, 384),
        "packed": low(8, 128, 768),
        "packed_full": low(8, 128, 768),
        "grad_full": low(8, 128, 1024),
        "hidden_one": low(8, 128, 1024),
        "queries": low(1024, 128),
        "keys": low(1024, 128),
        "keys_turned": low(128, 1024),
        "values": low(1024, 128),
        "values_turned": low(128, 1024),
        "attended": low(1024, 128),
        "totals": wide(1024, 128),
        "middle": wide(128, 1024),
        "hidden_two": low(128, 1024),
        "hidden_full": low(8, 128, 1024),
        "active": low(1024, 384),
        "both": low(1024, 768),
        "down_pad": low(384, 1024),
        "part": low(8, 128, 1024),
        "out_part": low(8, 128, 1024),
        "middle_grad": wide(128, 1024),
        "branch": low(128, 1024),
        "gain_two_term": wide(1, 1024),
        "down_grad": low(hidden, 1024),
        "branch_full": low(8, 128, 1024),
        "out_grad": low(1024, 128),
        "query_grad": wide(1024, 128),
        "key_acc": wide(128, 1024),
        "value_acc": wide(128, 1024),
        "three": low(1024, 384),
        "qkv_grads": low(8, 128, 384),
        "qkv_out": low(8, 128, 384),
        "packed_out": low(8, 128, 768),
        "output_grad": low(128, 1024),
        "gain_own": wide(8, 8, 128),
        "gain_in": wide(8, 8, 128),
        "gain_part": wide(8, 128),
        "gain_rep": wide(4, 8, 128),
        "value_blocks": low(8, 128, 128),
        "keep": DMA((6,)),
        "w_send": DMA((3, 7)),
        "w_recv": DMA((3, 8)),
        "p_send": DMA((7,)),
        "p_recv": DMA((8,)),
        "s_send": DMA((7,)),
        "s_recv": DMA((8,)),
        "f_send": DMA((7,)),
        "f_recv": DMA((8,)),
        "m_send": DMA((7,)),
        "m_recv": DMA((8,)),
        "mp_send": DMA((7,)),
        "mp_recv": DMA((8,)),
        "g_send": DMA((7,)),
        "g_recv": DMA((8,)),
        "gr_send": DMA((3,)),
        "gr_recv": DMA((4,)),
        "v_send": DMA((7,)),
        "v_recv": DMA((8,)),
    }
    groups = {
        "sums_one": sums_scratch(),
        "sums_two": sums_scratch(),
        "sums_out": sums_scratch(),
        "sums_three": sums_scratch(),
        "row_flow": rows_sems(),
        "grad_flow": rows_sems(),
        "hidden_flow": rows_sems(),
        "branch_flow": rows_sems(),
        "packed_flow": collect_scratch(128, 768),
        "qkv_flow": collect_scratch(128, 384),
        "down_flow": collect_rows_scratch(hidden),
        "output_flow": collect_rows_scratch(128),
    }
    return single, groups


def layer_kernel(
    hidden,
    rows,
    firsts,
    prefix,
    positions,
    first_gain,
    query_weight,
    key_weight,
    value_weight,
    output_weight,
    second_gain,
    gate_weight,
    up_weight,
    down,
    cotangent,
    layer_output,
    input_grad,
    firsts_grad,
    query_out,
    key_out,
    value_out,
    output_out,
    gate_out,
    up_out,
    down_out,
    gains,
    *refs,
):
    single, groups = scratch_of(hidden)
    s = types.SimpleNamespace(**dict(zip(single, refs)))
    refs = list(refs[len(single) :])
    for name, shapes in groups.items():
        setattr(s, name, refs[: len(shapes)])
        refs = refs[len(shapes) :]
    rep, fsdp, z, x = plane_place()
    core, level = lax.rem(rep, 2), rep // 2
    partner = rep + 1 - 2 * core
    above = rep + 2 - 4 * level
    slant = 3 - rep
    others = [lax.rem(fsdp + k, 8) for k in range(1, 8)]
    greet([(rep, other) for other in others] + [(partner, fsdp), (above, fsdp), (slant, fsdp)])
    mine = piece(core, 64)
    theirs = piece(1 - core, 64)
    started, kept = [], []
    row_flow = Rows(rows, s.rows_full, *s.row_flow)
    grad_flow = Rows(cotangent, s.grad_full, *s.grad_flow)
    hidden_flow = Rows(s.hidden_two, s.hidden_full, *s.hidden_flow)
    branch_flow = Rows(s.branch, s.branch_full, *s.branch_flow)
    sums_one, sums_two = Sums(*s.sums_one), Sums(*s.sums_two)
    sums_out, sums_three = Sums(*s.sums_out), Sums(*s.sums_three)
    packed_flow = Collect(s.packed, s.packed_out, *s.packed_flow)
    qkv_flow = Collect(s.qkv_grads, s.qkv_out, *s.qkv_flow)
    down_flow = CollectRows(s.down_grad, down_out, *s.down_flow)
    output_flow = CollectRows(s.output_grad, output_out, *s.output_flow)

    def go(copy):
        copy.start()
        started.append(copy)

    def here(src, dst):
        copy = pltpu.make_async_copy(src, dst, s.keep.at[len(kept)])
        copy.start()
        kept.append(copy)

    sources = (query_weight, key_weight, value_weight)
    for k, other in enumerate(others):
        for i, source in enumerate(sources):
            go(
                remote(
                    source.at[mine, piece(other, 128)],
                    s.weights.at[fsdp, mine, pl.ds(128 * i, 128)],
                    s.w_send.at[i, k],
                    s.w_recv.at[i, fsdp],
                    rep,
                    other,
                )
            )
    row_flow.start()
    rates = turn_rates()
    place_row = positions[...].astype(WIDE)
    lane = lax.broadcasted_iota(jnp.int32, (1, 128), 1)
    s.small[0:1, :] = place_row
    s.small[1:2, :] = first_gain[...].astype(WIDE)
    s.small[2:3, :] = second_gain[...].astype(WIDE)
    for run in range(2):
        begin = jnp.sum(jnp.where(lane == 64 * run, place_row, 0.0), axis=1, keepdims=True)
        s.small[3 + 2 * run : 4 + 2 * run, :] = jnp.cos(begin * rates)
        s.small[4 + 2 * run : 5 + 2 * run, :] = jnp.sin(begin * rates)
    s.small[7:8, :] = jnp.zeros((1, 128), WIDE)
    for k, other in enumerate(others):
        go(
            remote(
                s.small, s.marks.at[:, piece(fsdp, 128)], s.s_send.at[k], s.s_recv.at[fsdp], rep, other
            )
        )
    for k, other in enumerate(others):
        go(
            remote(
                firsts.at[:, piece(other, 128)],
                s.firsts_full.at[fsdp],
                s.f_send.at[k],
                s.f_recv.at[fsdp],
                rep,
                other,
            )
        )
    for i, source in enumerate(sources):
        here(source.at[:, piece(fsdp, 128)], s.weights.at[fsdp, :, pl.ds(128 * i, 128)])
    here(s.small, s.marks.at[:, piece(fsdp, 128)])
    here(firsts.at[:, piece(fsdp, 128)], s.firsts_full.at[fsdp])
    angles = lax.broadcasted_iota(jnp.int32, (64, 128), 0).astype(WIDE) * rates
    s.cosine_step[...] = jnp.cos(angles)
    s.sine_step[...] = jnp.sin(angles)
    pad = jnp.zeros((128, 384 - hidden), LOW)
    for i in range(8):
        s.packed[i, :, 0:hidden] = gate_weight[:, hidden * i : hidden * (i + 1)]
        s.packed[i, :, hidden:384] = pad
        s.packed[i, :, 384 : 384 + hidden] = up_weight[:, hidden * i : hidden * (i + 1)]
        s.packed[i, :, 384 + hidden : 768] = pad
    here(s.packed.at[fsdp], s.packed_full.at[fsdp])

    for k, other in enumerate(others):
        for i in range(3):
            arrived(s.weights.at[other, mine, pl.ds(128 * i, 128)], s.w_recv.at[i, other])
        place = s.weights.at[other, mine]
        go(remote(place, place, s.p_send.at[k], s.p_recv.at[other], partner, fsdp))
    for other in others:
        arrived(s.marks.at[:, piece(other, 128)], s.s_recv.at[other])
    for copy in kept:
        copy.wait()
    row_flow.kept()
    for other in others:
        arrived(s.weights.at[other, theirs], s.p_recv.at[other])
        arrived(s.firsts_full.at[other], s.f_recv.at[other])

    def project(block):
        entry = s.rows_full[block].astype(WIDE)
        scale = lax.rsqrt(jnp.mean(entry * entry, axis=-1, keepdims=True) + epsilon)
        low = (entry * scale * s.marks[1:2, :]).astype(LOW)
        s.hidden_one[block] = low
        pre = matmul(low, s.weights[...].reshape(8 * 128, 384))
        cosine, sine = turn_tables(s.marks, block, s.cosine_step, s.sine_step)
        at = piece(block, 128)
        s.queries[at, :] = turn(pre[:, :128], cosine, sine).astype(LOW)
        key = turn(pre[:, 128:256], cosine, sine)
        s.keys[at, :] = key.astype(LOW)
        s.keys_turned[:, at] = key.T.astype(LOW)
        value = 0.5 * pre[:, 256:] + 0.5 * s.firsts_full[block].astype(WIDE)
        s.values[at, :] = value.astype(LOW)
        s.values_turned[:, at] = value.T.astype(LOW)

    def project_column(k, carry):
        project(row_flow.pass_on(k))
        return carry

    def project_across(k, carry):
        project(row_flow.across(lax.rem(z + k, 4)))
        return carry

    project(fsdp)
    lax.fori_loop(0, 3, project_column, 0)
    grad_flow.start()
    for k, other in enumerate(others):
        go(
            remote(
                s.packed.at[other, mine],
                s.packed_full.at[fsdp, mine],
                s.m_send.at[k],
                s.m_recv.at[fsdp],
                rep,
                other,
            )
        )
    lax.fori_loop(0, 4, project_across, 0)
    prefix_last = (prefix[rep] - 1).astype(WIDE)
    masks = [head_lanes(head) for head in range(2)]

    def attend(block):
        at = piece(block, 128)
        query = s.queries[at, :]
        allowed = s.marks[0:1, :] <= limit_column(s.marks, block, prefix_last)
        result = total = None
        for head in range(2):
            scores = matmul(only(masks[head], query), s.keys_turned[...]) * E ** (-0.5)
            scores = jnp.where(allowed, scores, masked_score)
            top = jnp.max(scores, axis=-1, keepdims=True)
            weight = jnp.exp(scores - top)
            below = jnp.sum(weight, axis=-1, keepdims=True)
            probabilities = (weight * (1.0 / below)).astype(LOW)
            out = matmul(probabilities, s.values[...])
            log_total = jnp.broadcast_to(top + jnp.log(below), out.shape)
            result = out if head == 0 else jnp.where(masks[0], result, out)
            total = log_total if head == 0 else jnp.where(masks[0], total, log_total)
        s.totals[at, :] = total
        low = result.astype(LOW)
        s.attended[at, :] = low
        return matmul(low, output_weight[...])

    def attend_across(k, carry):
        other = sums_one.other(k)
        s.part[other] = attend(2 * other + 1 - x).astype(LOW)
        sums_one.give(k, s.part.at[other])

        @pl.when(k > 0)
        def hand_on():
            grad_flow.pass_on(k - 1)

        return carry

    lax.fori_loop(0, 4, attend_across, 0)
    for k, other in enumerate(others):
        place = s.packed_full.at[other, mine]
        arrived(place, s.m_recv.at[other])
        go(remote(place, place, s.mp_send.at[k], s.mp_recv.at[other], partner, fsdp))

    def attend_column(k, carry):
        sums_one.forward(k, attend(2 * sums_one.other(k) + x))
        return carry

    lax.fori_loop(0, 3, attend_column, 0)
    total = rows[...].astype(WIDE) + sums_one.total(attend(fsdp))
    s.middle[...] = total
    scale = lax.rsqrt(jnp.mean(total * total, axis=-1, keepdims=True) + epsilon)
    s.hidden_two[...] = (total * scale * s.marks[2:3, :]).astype(LOW)

    hidden_flow.start()
    s.down_pad[0:hidden, :] = down[...]
    s.down_pad[hidden:384, :] = jnp.zeros((384 - hidden, D), LOW)
    for k in range(4):
        grad_flow.across(lax.rem(z + k, 4))
    grad_flow.kept()
    for other in others:
        arrived(s.packed_full.at[other, theirs], s.mp_recv.at[other])

    def feed(block):
        at = piece(block, 128)
        packed = s.packed_full[...].reshape(8 * 128, 768)
        pre = matmul(s.hidden_full[block], packed)
        gate, up = pre[:, :384], pre[:, 384:]
        sigmoid = 1.0 / (1.0 + jnp.exp(-gate))
        swish = gate * sigmoid
        act = (swish * up).astype(LOW)
        s.active[at, :] = act
        act_grad = times_transposed(s.grad_full[block], s.down_pad[...])
        gate_grad = act_grad * up * sigmoid * (1.0 + gate * (1.0 - sigmoid))
        s.both[at, 0:384] = gate_grad.astype(LOW)
        s.both[at, 384:768] = (act_grad * swish).astype(LOW)
        s.part[block] = times_transposed(s.both[at, :], packed).astype(LOW)
        s.out_part[block] = matmul(act, s.down_pad[...]).astype(LOW)

    sums_one.sent()
    hidden_flow.kept()
    feed(fsdp)

    def feed_column(k, carry):
        feed(hidden_flow.pass_on(k))
        return carry

    def feed_across(k, carry):
        block = hidden_flow.across(sums_two.other(k))
        feed(block)
        sums_two.give(k, s.part.at[block])
        return carry

    lax.fori_loop(0, 3, feed_column, 0)
    lax.fori_loop(0, 4, feed_across, 0)

    def feed_grads(i, carry):
        turned = s.hidden_full[:, :, piece(i, 128)].reshape(8 * 128, 128)
        s.packed[i] = transposed_times(turned, s.both[...]).astype(LOW)
        return carry

    for copy in started:
        copy.wait_send()

    def feed_onward(k, carry):
        lax.fori_loop(2 * k, 2 * k + 2, feed_grads, 0)
        sums_two.forward(k, s.part[2 * sums_two.other(k) + x].astype(WIDE))
        return carry

    lax.fori_loop(0, 3, feed_onward, 0)
    lax.fori_loop(6, 8, feed_grads, 0)
    packed_flow.start()
    down_sum = transposed_times(s.active[...], s.grad_full[...].reshape(8 * 128, D))
    s.down_grad[...] = down_sum[0:hidden].astype(LOW)
    down_flow.start()
    hidden_grad = sums_two.total(s.part[fsdp].astype(WIDE))
    entry = s.middle[...]
    scale = lax.rsqrt(jnp.mean(entry * entry, axis=-1, keepdims=True) + epsilon)
    normed = entry * scale
    normed_grad = hidden_grad * s.marks[2:3, :]
    back = scale * (normed_grad - normed * jnp.mean(normed_grad * normed, axis=-1, keepdims=True))
    grad = cotangent[...].astype(WIDE) + back
    s.branch[...] = grad.astype(LOW)
    branch_flow.start()
    s.middle_grad[...] = grad
    s.gain_two_term[...] = jnp.sum(hidden_grad * normed, axis=0, keepdims=True)

    def pull(block):
        s.out_grad[piece(block, 128), :] = times_transposed(
            s.branch_full[block], output_weight[...]
        ).astype(LOW)

    packed_flow.fold_pair()
    down_flow.fold_pair()
    branch_flow.kept()
    pull(fsdp)

    def pull_column(k, carry):
        pull(branch_flow.pass_on(k))
        return carry

    def pull_across(k, carry):
        pull(branch_flow.across(lax.rem(z + k, 4)))
        return carry

    lax.fori_loop(0, 3, pull_column, 0)
    packed_flow.fold_level()
    down_flow.fold_level()
    lax.fori_loop(0, 4, pull_across, 0)
    for k in range(4):
        sums_out.give(k, s.out_part.at[2 * sums_out.other(k) + 1 - x])
    s.output_grad[...] = transposed_times(
        s.attended[...], s.branch_full[...].reshape(8 * 128, D)
    ).astype(LOW)
    output_flow.start()
    s.key_acc[...] = jnp.zeros_like(s.key_acc)
    s.value_acc[...] = jnp.zeros_like(s.value_acc)

    def attend_back(block, carry):
        at = piece(block, 128)
        query, grad = s.queries[at, :], s.out_grad[at, :]
        log_total = s.totals[at, :]
        allowed = s.marks[0:1, :] <= limit_column(s.marks, block, prefix_last)
        result = None
        lows, score_grads, turned_queries, turned_grads = [], [], [], []
        for head in range(2):
            query_here, grad_here = only(masks[head], query), only(masks[head], grad)
            scores = matmul(query_here, s.keys_turned[...]) * E ** (-0.5)
            column = log_total[:, head * E : head * E + 1]
            probabilities = jnp.where(allowed, jnp.exp(scores - column), 0.0)
            prob_grad = matmul(grad_here, s.values_turned[...])
            delta = jnp.sum(probabilities * prob_grad, axis=-1, keepdims=True)
            score_grad = (probabilities * (prob_grad - delta)).astype(LOW)
            out = matmul(score_grad, s.keys[...])
            result = out if head == 0 else jnp.where(masks[0], result, out)
            lows.append(probabilities.astype(LOW))
            score_grads.append(score_grad)
            turned_queries.append(query_here.astype(WIDE).T)
            turned_grads.append(grad_here.astype(WIDE).T)
        s.query_grad[at, :] = result
        s.key_acc[...] += matmul(
            jnp.concatenate(turned_queries, axis=1).astype(LOW),
            jnp.concatenate(score_grads, axis=0),
        )
        s.value_acc[...] += matmul(
            jnp.concatenate(turned_grads, axis=1).astype(LOW), jnp.concatenate(lows, axis=0)
        )

        @pl.when(block == 2)
        def step_one():
            output_flow.fold_pair()

        @pl.when(block == 4)
        def step_two():
            down_flow.relay()

        @pl.when(block == 6)
        def step_three():
            packed_flow.land()
            output_flow.fold_level()

        return carry

    lax.fori_loop(0, 8, attend_back, 0)

    def close(block):
        at = piece(block, 128)
        cosine, sine = turn_tables(s.marks, block, s.cosine_step, s.sine_step)
        s.three[at, 0:128] = turn(s.query_grad[at, :] * E ** (-0.5), cosine, -sine).astype(LOW)
        s.three[at, 128:256] = turn(s.key_acc[:, at].T * E ** (-0.5), cosine, -sine).astype(LOW)
        value_grad = (0.5 * s.value_acc[:, at].T).astype(LOW)
        s.three[at, 256:384] = value_grad
        s.value_blocks[block] = value_grad
        return times_transposed(s.three[at, :], s.weights[...].reshape(8 * 128, 384))

    def close_across(k, carry):
        other = sums_three.other(k)
        block = 2 * other + 1 - x
        s.part[block] = close(block).astype(LOW)
        sums_three.give(k, s.part.at[block])
        return carry

    def close_column(k, carry):
        block = 2 * sums_three.other(k) + x
        s.part[block] = close(block).astype(LOW)
        return carry

    sums_two.sent()
    lax.fori_loop(0, 4, close_across, 0)
    lax.fori_loop(0, 4, close_column, 0)
    for k, other in enumerate(others):
        remote(
            s.value_blocks.at[other],
            firsts_grad.at[:, piece(fsdp, 128)],
            s.v_send.at[k],
            s.v_recv.at[fsdp],
            rep,
            other,
        ).start()
    firsts_grad[:, piece(fsdp, 128)] = s.value_blocks[fsdp]

    def qkv_grads(i, carry):
        turned = s.hidden_one[:, :, piece(i, 128)].reshape(8 * 128, 128)
        s.qkv_grads[i] = transposed_times(turned, s.three[...]).astype(LOW)
        return carry

    lax.fori_loop(0, 8, qkv_grads, 0)
    qkv_flow.start()
    packed_flow.relay()
    output_flow.relay()
    for k in range(3):
        sums_out.forward(k, s.out_part[2 * sums_out.other(k) + x].astype(WIDE))
    sums_three.forward(0, s.part[2 * sums_three.other(0) + x].astype(WIDE))
    qkv_flow.fold_pair()
    sums_three.forward(1, s.part[2 * sums_three.other(1) + x].astype(WIDE))
    qkv_flow.fold_level()
    sums_three.forward(2, s.part[2 * sums_three.other(2) + x].astype(WIDE))
    qkv_flow.land()
    hidden_grad = sums_three.total(s.part[fsdp].astype(WIDE))
    entry = rows[...].astype(WIDE)
    scale = lax.rsqrt(jnp.mean(entry * entry, axis=-1, keepdims=True) + epsilon)
    normed = entry * scale
    normed_grad = hidden_grad * s.marks[1:2, :]
    gain_term = jnp.sum(hidden_grad * normed, axis=0, keepdims=True)
    for i in range(8):
        lanes = slice(128 * i, 128 * i + 128)
        s.gain_own[i, 0:1, :] = gain_term[:, lanes]
        s.gain_own[i, 1:2, :] = s.gain_two_term[:, lanes]
        s.gain_own[i, 2:8, :] = jnp.zeros((6, 128), WIDE)
    for k, other in enumerate(others):
        remote(
            s.gain_own.at[other], s.gain_in.at[fsdp], s.g_send.at[k], s.g_recv.at[fsdp], rep, other
        ).start()
    back = scale * (normed_grad - normed * jnp.mean(normed_grad * normed, axis=-1, keepdims=True))
    input_grad[...] = s.middle_grad[...] + back
    qkv_flow.relay()
    s.gain_in[fsdp] = s.gain_own[fsdp]
    for other in others:
        arrived(s.gain_in.at[other], s.g_recv.at[other])
    s.gain_part[...] = jnp.sum(s.gain_in[...], axis=0)
    for k, target in enumerate((partner, above, slant)):
        remote(
            s.gain_part, s.gain_rep.at[rep], s.gr_send.at[k], s.gr_recv.at[rep], target, fsdp
        ).start()
    s.gain_rep[rep] = s.gain_part[...]
    layer_output[...] = (
        s.middle[...] + sums_out.total(s.out_part[fsdp].astype(WIDE))
    ).astype(LOW)
    packed_flow.finish()
    for i in range(8):
        wide = slice(hidden * i, hidden * (i + 1))
        gate_out[:, wide] = s.packed_out[i, :, 0:hidden]
        up_out[:, wide] = s.packed_out[i, :, 384 : 384 + hidden]
    for k, other in enumerate(others):
        arrived(firsts_grad.at[:, piece(other, 128)], s.v_recv.at[other])
        arrived(s.value_blocks.at[0], s.v_send.at[k])
        arrived(s.gain_own.at[0], s.g_send.at[k])
    for k, source in enumerate((partner, above, slant)):
        arrived(s.gain_rep.at[source], s.gr_recv.at[source])
        arrived(s.gain_part, s.gr_send.at[k])
    gains[...] = jnp.sum(s.gain_rep[...], axis=0)
    down_flow.finish()
    output_flow.finish()
    qkv_flow.finish()
    for i in range(8):
        lanes = slice(128 * i, 128 * i + 128)
        query_out[:, lanes] = s.qkv_out[i, :, 0:128]
        key_out[:, lanes] = s.qkv_out[i, :, 128:256]
        value_out[:, lanes] = s.qkv_out[i, :, 256:384]
    for flow in (row_flow, grad_flow, hidden_flow, branch_flow):
        flow.sent()
    for sums in (sums_out, sums_three):
        sums.sent()


def shards_plane(
    inputs,
    first_values,
    prefix,
    positions,
    first_gain,
    query_weight,
    key_weight,
    value_weight,
    output_weight,
    second_gain,
    gate_weight,
    up_weight,
    down_weight,
    cotangent,
):
    hidden = down_weight.shape[0]
    single, groups = scratch_of(hidden)
    outs = pl.pallas_call(
        functools.partial(layer_kernel, hidden),
        out_shape=[
            low_shape(128, D),
            wide_shape(128, D),
            low_shape(128, D),
            low_shape(128, D),
            low_shape(128, D),
            low_shape(128, D),
            low_shape(128, D),
            low_shape(128, 8 * hidden),
            low_shape(128, 8 * hidden),
            low_shape(hidden, D),
            wide_shape(8, 128),
        ],
        in_specs=[VM, VM, SM] + [VM] * 11,
        out_specs=[VM] * 11,
        scratch_shapes=list(single.values()) + [shape for group in groups.values() for shape in group],
        compiler_params=pltpu.CompilerParams(
            collective_id=1, has_side_effects=True, vmem_limit_bytes=LIMIT
        ),
    )(
        inputs,
        first_values,
        prefix,
        positions[None],
        first_gain[None],
        query_weight,
        key_weight,
        value_weight,
        output_weight,
        second_gain[None],
        gate_weight,
        up_weight,
        down_weight,
        cotangent,
    )
    layer_output, input_grad = outs[:2]
    firsts, query, key, value, output, gate, up, down = [a.astype(WIDE) for a in outs[2:10]]
    gains = outs[10]
    return (
        layer_output,
        input_grad,
        firsts,
        gains[0],
        query,
        key,
        value,
        output,
        gains[1],
        gate,
        up,
        down,
    )


def pick_body(mesh):
    if mesh.shape["fsdp"] == 8 and mesh.shape["rep"] == 4:
        return shards_plane
    return shards_general


def solution(mesh):
    placed = (
        P(("rep", "fsdp"), None),
        P(("rep", "fsdp"), None),
        P(),
        P(("rep", "fsdp")),
        P("fsdp"),
        P("fsdp", None),
        P("fsdp", None),
        P("fsdp", None),
        P("fsdp", None),
        P("fsdp"),
        P("fsdp", None),
        P("fsdp", None),
        P("fsdp", None),
        P(("rep", "fsdp"), None),
    )
    return jax.shard_map(
        pick_body(mesh),
        mesh=mesh,
        in_specs=placed,
        out_specs=(
            P(("rep", "fsdp"), None),
            P(("rep", "fsdp"), None),
            P(("rep", "fsdp"), None),
            P("fsdp"),
            P("fsdp", None),
            P("fsdp", None),
            P("fsdp", None),
            P("fsdp", None),
            P("fsdp"),
            P("fsdp", None),
            P("fsdp", None),
            P("fsdp", None),
        ),
        check_vma=False,
    )
```

```python
import functools
import math
import types

import jax
import jax.numpy as jnp
from jax import lax
from jax.experimental import pallas as pl
from jax.experimental.pallas import tpu as pltpu
from jax.sharding import PartitionSpec as P

D = 1024
H = 16
E = 64


epsilon = 1e-06
masked_score = -1e30


def rms_scale(values):
    return lax.rsqrt(jnp.mean(values * values, axis=-1, keepdims=True) + epsilon)


def rope_tables(places):
    half_width = E // 2
    frequency = jnp.exp(
        jnp.arange(half_width, dtype=jnp.float32) * (-math.log(10000.0) / half_width)
    )
    angles = places.astype(jnp.float32)[:, None] * frequency[None, :]
    return (jnp.cos(angles)[:, None, :], jnp.sin(angles)[:, None, :])


def rope_apply(shaped, cosine, sine_table):
    half_width = shaped.shape[-1] // 2
    first_half = shaped[..., :half_width]
    second_half = shaped[..., half_width:]
    return jnp.concatenate(
        [
            first_half * cosine - second_half * sine_table,
            second_half * cosine + first_half * sine_table,
        ],
        axis=-1,
    )


def rope_undo(shaped, cosine, sine_table):
    half_width = shaped.shape[-1] // 2
    first_half = shaped[..., :half_width]
    second_half = shaped[..., half_width:]
    return jnp.concatenate(
        [
            first_half * cosine + second_half * sine_table,
            second_half * cosine - first_half * sine_table,
        ],
        axis=-1,
    )


def times_transposed(left, right):
    return lax.dot_general(
        left, right, (((1,), (1,)), ((), ())), preferred_element_type=jnp.float32
    )


def transposed_times(left, right):
    return lax.dot_general(
        left, right, (((0,), (0,)), ((), ())), preferred_element_type=jnp.float32
    )


def block_rows(count):
    size_now = count
    while size_now > 1024 and size_now % 2 == 0:
        size_now = size_now // 2
    return size_now


def split_blocks(array, size_now):
    return array.reshape((array.shape[0] // size_now, size_now) + array.shape[1:])


def masked_scores(queries, key_rows, limits, key_places):
    scores = jnp.einsum(
        "qhe,khe->hqk", queries, key_rows, preferred_element_type=jnp.float32
    ) * E ** (-0.5)
    allowed = key_places[None, None, :] <= limits[None, :, None]
    return (scores, allowed)


def grad_block(queries, key_rows, value_rows, limits, key_places, out_low, log_total, delta_rows):
    scores, allowed = masked_scores(queries, key_rows, limits, key_places)
    probabilities = jnp.where(allowed, jnp.exp(scores - log_total[:, :, None]), 0.0)
    prob_grad = jnp.einsum("qhe,khe->hqk", out_low, value_rows, preferred_element_type=jnp.float32)
    score_grad = (probabilities * (prob_grad - delta_rows[:, :, None])).astype(jnp.bfloat16)
    return (probabilities.astype(jnp.bfloat16), score_grad)


def norm_back(hidden_grad, normed, gain_float, scale_rows):
    normed_grad = hidden_grad * gain_float
    gain_term = jnp.sum(hidden_grad * normed, axis=0)
    rows_grad = scale_rows * (
        normed_grad - normed * jnp.mean(normed_grad * normed, axis=-1, keepdims=True)
    )
    return (gain_term, rows_grad)


def shards_general(
    inputs,
    first_values,
    prefix,
    positions,
    first_gain,
    query_weight,
    key_weight,
    value_weight,
    output_weight,
    second_gain,
    gate_weight,
    up_weight,
    down_weight,
    cotangent,
):
    token_count = inputs.shape[0]
    gain_one, query_full, key_full, value_full, output_full = (
        lax.all_gather(first_gain, "fsdp", axis=0, tiled=True),
        lax.all_gather(query_weight, "fsdp", axis=0, tiled=True),
        lax.all_gather(key_weight, "fsdp", axis=0, tiled=True),
        lax.all_gather(value_weight, "fsdp", axis=0, tiled=True),
        lax.all_gather(output_weight, "fsdp", axis=0, tiled=True),
    )
    all_places = lax.all_gather(positions, "fsdp", axis=0, tiled=True)
    prefix_here = lax.dynamic_index_in_dim(prefix, lax.axis_index("rep"), keepdims=False)
    own_limits = jnp.maximum(positions, prefix_here - 1)
    cosine, sine_table = rope_tables(positions)
    rows_float = inputs.astype(jnp.float32)
    scale_one = rms_scale(rows_float)
    normed_one = rows_float * scale_one
    gain_one_float = gain_one.astype(jnp.float32)
    hidden_one = (normed_one * gain_one_float).astype(jnp.bfloat16)
    query_pre = jnp.dot(hidden_one, query_full, preferred_element_type=jnp.float32)
    key_pre = jnp.dot(hidden_one, key_full, preferred_element_type=jnp.float32)
    value_pre = jnp.dot(hidden_one, value_full, preferred_element_type=jnp.float32)
    queries = rope_apply(query_pre.reshape(token_count, H, E), cosine, sine_table).astype(
        jnp.bfloat16
    )
    key_rows = (
        rope_apply(key_pre.reshape(token_count, H, E), cosine, sine_table)
        .astype(jnp.bfloat16)
        .reshape(token_count, D)
    )
    mixed_values = (0.5 * value_pre + 0.5 * first_values.astype(jnp.float32)).astype(jnp.bfloat16)
    start_state = (
        jnp.full((H, token_count), masked_score, jnp.float32),
        jnp.zeros((H, token_count), jnp.float32),
        jnp.zeros((token_count, H, E), jnp.float32),
    )
    running = start_state
    key_piece = lax.all_gather(key_rows, "fsdp", axis=0, tiled=True)
    value_piece = lax.all_gather(mixed_values, "fsdp", axis=0, tiled=True)
    count = key_piece.shape[0]
    size_now = block_rows(count)

    def forward_step(state_now, blocks):
        row_max, row_sum, accum = state_now
        key_block, value_block, place_block = blocks
        scores, allowed = masked_scores(
            queries, key_block.reshape(-1, H, E), own_limits, place_block
        )
        new_max = jnp.maximum(row_max, jnp.max(jnp.where(allowed, scores, masked_score), axis=-1))
        rescale = jnp.exp(row_max - new_max)
        weights = jnp.where(allowed, jnp.exp(scores - new_max[:, :, None]), 0.0)
        row_sum = row_sum * rescale + jnp.sum(weights, axis=-1)
        accum = accum * rescale.T[:, :, None] + jnp.einsum(
            "hqk,khe->qhe",
            weights.astype(jnp.bfloat16),
            value_block.reshape(-1, H, E),
            preferred_element_type=jnp.float32,
        )
        return ((new_max, row_sum, accum), None)

    running, unused = lax.scan(
        forward_step,
        running,
        (
            split_blocks(key_piece, size_now),
            split_blocks(value_piece, size_now),
            split_blocks(all_places, size_now),
        ),
    )
    row_max, row_sum, accum = running
    log_total = row_max + jnp.log(row_sum)
    attended = accum / row_sum.T[:, :, None]
    attended_low = attended.reshape(token_count, D).astype(jnp.bfloat16)
    middle = rows_float + jnp.dot(attended_low, output_full, preferred_element_type=jnp.float32)
    mlp_forward = (
        lax.all_gather(second_gain, "fsdp", axis=0, tiled=True),
        lax.all_gather(gate_weight, "fsdp", axis=0, tiled=True),
        lax.all_gather(up_weight, "fsdp", axis=0, tiled=True),
        lax.all_gather(down_weight, "fsdp", axis=0, tiled=True),
    )
    gain_two, gate_full, up_full, down_full = mlp_forward
    scale_two = rms_scale(middle)
    normed_two = middle * scale_two
    hidden_two = (normed_two * gain_two.astype(jnp.float32)).astype(jnp.bfloat16)
    gate_pre = jnp.dot(hidden_two, gate_full, preferred_element_type=jnp.float32)
    up_pre = jnp.dot(hidden_two, up_full, preferred_element_type=jnp.float32)
    sigmoid_gate = jax.nn.sigmoid(gate_pre)
    activated = (gate_pre * sigmoid_gate * up_pre).astype(jnp.bfloat16)
    layer_output = (
        middle + jnp.dot(activated, down_full, preferred_element_type=jnp.float32)
    ).astype(jnp.bfloat16)
    gain_two_back, gate_back, up_back, down_back = (
        lax.all_gather(second_gain, "fsdp", axis=0, tiled=True),
        lax.all_gather(gate_weight, "fsdp", axis=0, tiled=True),
        lax.all_gather(up_weight, "fsdp", axis=0, tiled=True),
        lax.all_gather(down_weight, "fsdp", axis=0, tiled=True),
    )
    act_grad = times_transposed(cotangent, down_back)
    down_term = transposed_times(activated, cotangent)
    gate_grad = (act_grad * up_pre * sigmoid_gate * (1.0 + gate_pre * (1.0 - sigmoid_gate))).astype(
        jnp.bfloat16
    )
    up_grad = (act_grad * gate_pre * sigmoid_gate).astype(jnp.bfloat16)
    hidden_two_grad = times_transposed(gate_grad, gate_back) + times_transposed(up_grad, up_back)
    gate_term = transposed_times(hidden_two, gate_grad)
    up_term = transposed_times(hidden_two, up_grad)
    gain_two_term, middle_part = norm_back(
        hidden_two_grad, normed_two, gain_two_back.astype(jnp.float32), scale_two
    )
    middle_grad = cotangent.astype(jnp.float32) + middle_part
    gain_two_sum, gate_sum, up_sum, down_sum = (
        lax.psum_scatter(gain_two_term, "fsdp", scatter_dimension=0, tiled=True),
        lax.psum_scatter(gate_term, "fsdp", scatter_dimension=0, tiled=True),
        lax.psum_scatter(up_term, "fsdp", scatter_dimension=0, tiled=True),
        lax.psum_scatter(down_term, "fsdp", scatter_dimension=0, tiled=True),
    )
    gain_one_back, query_back, key_back, value_back, output_back = (
        lax.all_gather(first_gain, "fsdp", axis=0, tiled=True),
        lax.all_gather(query_weight, "fsdp", axis=0, tiled=True),
        lax.all_gather(key_weight, "fsdp", axis=0, tiled=True),
        lax.all_gather(value_weight, "fsdp", axis=0, tiled=True),
        lax.all_gather(output_weight, "fsdp", axis=0, tiled=True),
    )
    branch_low = middle_grad.astype(jnp.bfloat16)
    output_term = transposed_times(attended_low, branch_low)
    out_flat = times_transposed(branch_low, output_back).astype(jnp.bfloat16)
    out_low = out_flat.reshape(token_count, H, E)
    delta_rows = jnp.sum(out_low.astype(jnp.float32) * attended, axis=-1).T
    zero_rows = jnp.zeros((token_count, H, E), jnp.float32)
    gathered_keys, gathered_values = (
        lax.all_gather(key_rows, "fsdp", axis=0, tiled=True),
        lax.all_gather(mixed_values, "fsdp", axis=0, tiled=True),
    )
    length = gathered_keys.shape[0]
    size_now = block_rows(length)

    def back_step(query_acc, blocks):
        key_block, value_block, place_block = blocks
        key_shaped = key_block.reshape(-1, H, E)
        value_shaped = value_block.reshape(-1, H, E)
        prob_low, score_grad = grad_block(
            queries,
            key_shaped,
            value_shaped,
            own_limits,
            place_block,
            out_low,
            log_total,
            delta_rows,
        )
        query_acc = query_acc + jnp.einsum(
            "hqk,khe->qhe", score_grad, key_shaped, preferred_element_type=jnp.float32
        )
        key_part = jnp.einsum(
            "hqk,qhe->khe", score_grad, queries, preferred_element_type=jnp.float32
        ).reshape(-1, D)
        value_part = jnp.einsum(
            "hqk,qhe->khe", prob_low, out_low, preferred_element_type=jnp.float32
        ).reshape(-1, D)
        return (query_acc, jnp.concatenate([key_part, value_part], axis=1))

    query_acc, parts = lax.scan(
        back_step,
        zero_rows,
        (
            split_blocks(gathered_keys, size_now),
            split_blocks(gathered_values, size_now),
            split_blocks(all_places, size_now),
        ),
    )
    summed = lax.psum_scatter(parts.reshape(length, 2 * D), "fsdp", scatter_dimension=0, tiled=True)
    key_acc = summed[:, :D]
    value_acc = summed[:, D:]
    query_grad = (
        rope_undo(query_acc * E ** (-0.5), cosine, sine_table)
        .reshape(token_count, D)
        .astype(jnp.bfloat16)
    )
    key_grad = (
        rope_undo(key_acc.reshape(token_count, H, E) * E ** (-0.5), cosine, sine_table)
        .reshape(token_count, D)
        .astype(jnp.bfloat16)
    )
    first_values_grad = 0.5 * value_acc
    value_grad = first_values_grad.astype(jnp.bfloat16)
    hidden_one_grad = (
        times_transposed(query_grad, query_back)
        + times_transposed(key_grad, key_back)
        + times_transposed(value_grad, value_back)
    )
    query_term = transposed_times(hidden_one, query_grad)
    key_term = transposed_times(hidden_one, key_grad)
    value_term = transposed_times(hidden_one, value_grad)
    gain_one_term, input_part = norm_back(
        hidden_one_grad, normed_one, gain_one_back.astype(jnp.float32), scale_one
    )
    input_grad = middle_grad + input_part
    gain_one_sum, query_sum, key_sum, value_sum, output_sum = (
        lax.psum_scatter(gain_one_term, "fsdp", scatter_dimension=0, tiled=True),
        lax.psum_scatter(query_term, "fsdp", scatter_dimension=0, tiled=True),
        lax.psum_scatter(key_term, "fsdp", scatter_dimension=0, tiled=True),
        lax.psum_scatter(value_term, "fsdp", scatter_dimension=0, tiled=True),
        lax.psum_scatter(output_term, "fsdp", scatter_dimension=0, tiled=True),
    )
    totals = (
        lax.psum(gain_one_sum.astype(jnp.bfloat16), "rep").astype(jnp.float32),
        lax.psum(query_sum.astype(jnp.bfloat16), "rep").astype(jnp.float32),
        lax.psum(key_sum.astype(jnp.bfloat16), "rep").astype(jnp.float32),
        lax.psum(value_sum.astype(jnp.bfloat16), "rep").astype(jnp.float32),
        lax.psum(output_sum.astype(jnp.bfloat16), "rep").astype(jnp.float32),
        lax.psum(gain_two_sum.astype(jnp.bfloat16), "rep").astype(jnp.float32),
        lax.psum(gate_sum.astype(jnp.bfloat16), "rep").astype(jnp.float32),
        lax.psum(up_sum.astype(jnp.bfloat16), "rep").astype(jnp.float32),
        lax.psum(down_sum.astype(jnp.bfloat16), "rep").astype(jnp.float32),
    )
    return (
        layer_output,
        input_grad,
        first_values_grad,
        totals[0],
        totals[1],
        totals[2],
        totals[3],
        totals[4],
        totals[5],
        totals[6],
        totals[7],
        totals[8],
    )


MESH = pl.DeviceIdType.MESH
LOW = jnp.bfloat16
WIDE = jnp.float32
VM = pl.BlockSpec(memory_space=pltpu.VMEM)
SM = pl.BlockSpec(memory_space=pltpu.SMEM)
DMA = pltpu.SemaphoreType.DMA
LIMIT = 63 * 1024 * 1024


def remote(src, dst, send_sem, recv_sem, rep, fsdp):
    return pltpu.make_async_remote_copy(
        src_ref=src,
        dst_ref=dst,
        send_sem=send_sem,
        recv_sem=recv_sem,
        device_id={"rep": rep, "fsdp": fsdp},
        device_id_type=MESH,
    )


def arrived(place, sem):
    pltpu.make_async_copy(place, place, sem).wait()


def greet(peers):
    barrier = pltpu.get_barrier_semaphore()
    for rep, fsdp in peers:
        pl.semaphore_signal(
            barrier, inc=1, device_id={"rep": rep, "fsdp": fsdp}, device_id_type=MESH
        )
    pl.semaphore_wait(barrier, len(peers))


def plane_place():
    rep, fsdp = lax.axis_index("rep"), lax.axis_index("fsdp")
    return rep, fsdp, fsdp // 2, fsdp % 2


def piece(index, size):
    return pl.ds(pl.multiple_of(index * size, size), size)


def matmul(left, right):
    return jnp.dot(left, right, preferred_element_type=WIDE)


class Rows:
    def __init__(self, own, full, keep, send, recv):
        self.own, self.full, self.keep, self.send, self.recv = own, full, keep, send, recv
        self.rep, self.fsdp, self.z, self.x = plane_place()
        self.side = 2 * self.z + 1 - self.x

    def push(self, src, block, sem, target):
        return remote(
            src, self.full.at[block], self.send.at[sem], self.recv.at[block], self.rep, target
        )

    def start(self):
        z, x = self.z, self.x

        @pl.when(z < 3)
        def up():
            self.push(self.own, self.fsdp, 0, 2 * (z + 1) + x).start()

        @pl.when(z > 0)
        def down():
            self.push(self.own, self.fsdp, 1, 2 * (z - 1) + x).start()

        self.push(self.own, self.fsdp, 2, self.side).start()
        pltpu.make_async_copy(self.own, self.full.at[self.fsdp], self.keep).start()

    def kept(self):
        pltpu.make_async_copy(self.own, self.full.at[self.fsdp], self.keep).wait()

    def line(self, k):
        high, odd = self.z // 2, self.z % 2
        first = 1 - (k + 1) // 2
        low_side = k + 1 - odd * first
        high_side = 2 - k + first * (1 - odd)
        return low_side + high * (high_side - low_side)

    def pass_on(self, k):
        z, x = self.z, self.x
        other = self.line(k)
        block = 2 * other + x
        place = self.full.at[block]
        arrived(place, self.recv.at[block])

        @pl.when((other < z) & (z < 3))
        def up():
            self.push(place, block, 3 + k, 2 * (z + 1) + x).start()

        @pl.when((other > z) & (z > 0))
        def down():
            self.push(place, block, 3 + k, 2 * (z - 1) + x).start()

        self.push(place, block, 6 + k, self.side).start()
        return block

    def across(self, other):
        block = 2 * other + 1 - self.x
        arrived(self.full.at[block], self.recv.at[block])
        return block

    def sent(self):
        z = self.z
        place = self.full.at[0]

        def done(sem):
            arrived(place, self.send.at[sem])

        pl.when(z < 3)(lambda: done(0))
        pl.when(z > 0)(lambda: done(1))
        done(2)
        for k in range(3):
            done(6 + k)

            @pl.when((z > 0) & (z < 3))
            def relayed():
                done(3 + k)


def rows_sems():
    return [DMA(()), DMA((9,)), DMA((8,))]


class Sums:
    def __init__(self, side_in, summed, line_in, send, side_recv, line_recv):
        self.side_in, self.summed, self.line_in = side_in, summed, line_in
        self.send, self.side_recv, self.line_recv = send, side_recv, line_recv
        self.rep, self.fsdp, self.z, self.x = plane_place()
        self.side = 2 * self.z + 1 - self.x

    def other(self, k):
        return lax.rem(self.z + 1 + k, 4)

    def give(self, k, ref):
        other = self.other(k)
        remote(
            ref, self.side_in.at[other], self.send.at[k], self.side_recv.at[other], self.rep, self.side
        ).start()

    def forward(self, k, value):
        other = self.other(k)
        arrived(self.side_in.at[other], self.side_recv.at[other])
        self.summed[other] = (value + self.side_in[other].astype(WIDE)).astype(LOW)
        remote(
            self.summed.at[other],
            self.line_in.at[self.z],
            self.send.at[4 + k],
            self.line_recv.at[self.z],
            self.rep,
            2 * other + self.x,
        ).start()

    def total(self, value):
        arrived(self.side_in.at[self.z], self.side_recv.at[self.z])
        value = value + self.side_in[self.z].astype(WIDE)
        for k in range(3):
            other = self.other(k)
            arrived(self.line_in.at[other], self.line_recv.at[other])
            value = value + self.line_in[other].astype(WIDE)
        return value

    def sent(self):
        for k in range(7):
            arrived(self.side_in.at[0], self.send.at[k])


def sums_scratch():
    return [pltpu.VMEM((4, 128, D), LOW)] * 3 + [DMA((7,)), DMA((4,)), DMA((4,))]


class Collect:
    def __init__(self, grads, out, pair_in, pair_sum, level_in, level_sum, landed, send, recv, cross_send, cross_recv):
        self.grads, self.out = grads, out
        self.pair_in, self.pair_sum = pair_in, pair_sum
        self.level_in, self.level_sum, self.landed = level_in, level_sum, landed
        self.send, self.recv, self.cross_send, self.cross_recv = send, recv, cross_send, cross_recv
        self.rep, self.fsdp, _, _ = plane_place()
        self.core, self.level = lax.rem(self.rep, 2), self.rep // 2
        self.partner = self.rep + 1 - 2 * self.core
        self.above = self.rep + 2 - 4 * self.level
        self.half = grads.shape[1] // 2
        self.fourth = self.half // 2

    def to(self, src, dst, index, rep):
        return remote(src, dst, self.send.at[index], self.recv.at[index], rep, self.fsdp)

    def start(self):
        src = self.grads.at[:, piece(1 - self.core, self.half)]
        self.to(src, self.pair_in, 0, self.partner).start()

    def fold_pair(self):
        arrived(self.pair_in, self.recv.at[0])
        mine = piece(self.core, self.half)

        def add(i, carry):
            self.pair_sum[i] = (
                self.grads[i, mine].astype(WIDE) + self.pair_in[i].astype(WIDE)
            ).astype(LOW)
            return carry

        lax.fori_loop(0, 8, add, 0)
        src = self.pair_sum.at[:, piece(1 - self.level, self.fourth)]
        self.to(src, self.level_in, 1, self.above).start()

    def fold_level(self):
        arrived(self.level_in, self.recv.at[1])
        mine = piece(self.level, self.fourth)

        def add(i, carry):
            self.level_sum[i] = (
                self.pair_sum[i, mine].astype(WIDE) + self.level_in[i].astype(WIDE)
            ).astype(LOW)
            return carry

        lax.fori_loop(0, 8, add, 0)
        for k in range(7):
            other = lax.rem(self.fsdp + k + 1, 8)
            remote(
                self.level_sum.at[other],
                self.landed.at[self.fsdp],
                self.cross_send.at[k],
                self.cross_recv.at[self.fsdp],
                self.rep,
                other,
            ).start()

    def quarter(self, core, level):
        return self.out.at[:, piece(2 * core + level, self.fourth)]

    def land(self):
        for k in range(7):
            other = lax.rem(self.fsdp + k + 1, 8)
            arrived(self.landed.at[other], self.cross_recv.at[other])
        self.landed[self.fsdp] = self.level_sum[self.fsdp]
        mine = piece(2 * self.core + self.level, self.fourth)
        place = self.quarter(self.core, self.level)
        self.to(self.landed, place, 2, self.above).start()
        self.to(self.landed, place, 3, self.partner).start()
        for i in range(8):
            self.out[i, mine] = self.landed[i]

    def relay(self):
        place = self.quarter(self.core, 1 - self.level)
        arrived(place, self.recv.at[2])
        self.to(place, place, 4, self.partner).start()

    def finish(self):
        arrived(self.quarter(1 - self.core, self.level), self.recv.at[3])
        arrived(self.quarter(1 - self.core, 1 - self.level), self.recv.at[4])
        arrived(self.pair_in, self.send.at[0])
        arrived(self.level_in, self.send.at[1])
        for k in range(3):
            arrived(self.landed, self.send.at[2 + k])
        for k in range(7):
            arrived(self.landed.at[0], self.cross_send.at[k])


def collect_scratch(high, wide):
    return [
        pltpu.VMEM((8, high // 2, wide), LOW),
        pltpu.VMEM((8, high // 2, wide), LOW),
        pltpu.VMEM((8, high // 4, wide), LOW),
        pltpu.VMEM((8, high // 4, wide), LOW),
        pltpu.VMEM((8, high // 4, wide), LOW),
        DMA((5,)),
        DMA((5,)),
        DMA((7,)),
        DMA((8,)),
    ]


class CollectRows:
    def __init__(self, rows, out, pair_in, pair_sum, level_in, send, recv):
        self.rows, self.out = rows, out
        self.pair_in, self.pair_sum, self.level_in = pair_in, pair_sum, level_in
        self.send, self.recv = send, recv
        self.rep, self.fsdp, _, _ = plane_place()
        self.core, self.level = lax.rem(self.rep, 2), self.rep // 2
        self.partner = self.rep + 1 - 2 * self.core
        self.above = self.rep + 2 - 4 * self.level
        self.half = rows.shape[1] // 2
        self.fourth = self.half // 2

    def to(self, src, dst, index, rep):
        return remote(src, dst, self.send.at[index], self.recv.at[index], rep, self.fsdp)

    def start(self):
        src = self.rows.at[:, piece(1 - self.core, self.half)]
        self.to(src, self.pair_in, 0, self.partner).start()

    def fold_pair(self):
        arrived(self.pair_in, self.recv.at[0])
        self.pair_sum[...] = (
            self.rows[:, piece(self.core, self.half)].astype(WIDE) + self.pair_in[...].astype(WIDE)
        ).astype(LOW)
        src = self.pair_sum.at[:, piece(1 - self.level, self.fourth)]
        self.to(src, self.level_in, 1, self.above).start()

    def quarter(self, core, level):
        return self.out.at[:, piece(2 * core + level, self.fourth)]

    def fold_level(self):
        arrived(self.level_in, self.recv.at[1])
        mine = piece(2 * self.core + self.level, self.fourth)
        self.out[:, mine] = (
            self.pair_sum[:, piece(self.level, self.fourth)].astype(WIDE)
            + self.level_in[...].astype(WIDE)
        ).astype(LOW)
        place = self.quarter(self.core, self.level)
        self.to(place, place, 2, self.above).start()
        self.to(place, place, 3, self.partner).start()

    def relay(self):
        place = self.quarter(self.core, 1 - self.level)
        arrived(place, self.recv.at[2])
        self.to(place, place, 4, self.partner).start()

    def finish(self):
        arrived(self.quarter(1 - self.core, self.level), self.recv.at[3])
        arrived(self.quarter(1 - self.core, 1 - self.level), self.recv.at[4])
        arrived(self.pair_in, self.send.at[0])
        for k in range(4):
            arrived(self.level_in, self.send.at[1 + k])


def collect_rows_scratch(tall):
    return [
        pltpu.VMEM((tall, D // 2), LOW),
        pltpu.VMEM((tall, D // 2), LOW),
        pltpu.VMEM((tall, D // 4), LOW),
        DMA((5,)),
        DMA((5,)),
    ]


def turn_rates():
    lane = lax.broadcasted_iota(jnp.int32, (1, 128), 1) % (E // 2)
    return jnp.exp(lane.astype(WIDE) * (-math.log(10000.0) / (E // 2)))


def turn_tables(marks, block, cosine_step, sine_step):
    lanes = piece(block, 128)
    cosines, sines = [], []
    for run in range(2):
        c = marks[3 + 2 * run : 4 + 2 * run, lanes]
        s = marks[4 + 2 * run : 5 + 2 * run, lanes]
        cosines.append(c * cosine_step[...] - s * sine_step[...])
        sines.append(s * cosine_step[...] + c * sine_step[...])
    lane = lax.broadcasted_iota(jnp.int32, (1, 128), 1)
    sign = jnp.where(lane % E < E // 2, -1.0, 1.0)
    return jnp.concatenate(cosines, axis=0), jnp.concatenate(sines, axis=0) * sign


def turn(array, cosine, sine):
    lane = lax.broadcasted_iota(jnp.int32, (1, 128), 1)
    swapped = jnp.where(lane % E < E // 2, pltpu.roll(array, 96, 1), pltpu.roll(array, 32, 1))
    return array * cosine + swapped * sine


def limit_column(marks, block, prefix_last):
    tile = marks[0:1, piece(block, 128)]
    lane = lax.broadcasted_iota(jnp.int32, (1, 128), 1)
    row = lax.broadcasted_iota(jnp.int32, (128, 1), 0)
    first = jnp.sum(jnp.where(lane == 0, tile, 0.0), axis=1, keepdims=True)
    second = jnp.sum(jnp.where(lane == 64, tile, 0.0), axis=1, keepdims=True)
    places = jnp.where(row < 64, first + row.astype(WIDE), second + (row - 64).astype(WIDE))
    return jnp.maximum(places, prefix_last)


def head_lanes(head):
    lane = lax.broadcasted_iota(jnp.int32, (1, 128), 1)
    return (lane // E) == head


def only(mask, array):
    return jnp.where(mask, array.astype(WIDE), 0.0).astype(LOW)


STEP = {"x": 1, "z": 2, "y": 4}
THIRDS = (("x", "y", "z", 0, 48), ("y", "z", "x", 48, 48), ("z", "x", "y", 96, 32))


def flip(block, *dims):
    for dim in dims:
        block = block + STEP[dim] - 2 * STEP[dim] * ((block // STEP[dim]) % 2)
    return block


class Cube:
    def __init__(self):
        self.rep, self.fsdp, z, x = plane_place()
        self.core, self.y = lax.rem(self.rep, 2), self.rep // 2
        self.low, self.high = z % 2, z // 2
        self.own = x + 2 * self.low + 4 * self.y
        self.partner = self.rep + 1 - 2 * self.core
        self.far = self.fsdp + 4 - 8 * self.high
        self.lends = self.high == self.y
        self.near = {
            "x": (self.rep, self.fsdp + 1 - 2 * x),
            "z": (self.rep, self.fsdp + 2 - 4 * self.low),
            "y": (self.rep + 2 - 4 * self.y, self.fsdp),
        }

    def device(self, *dims):
        rep, fsdp = self.rep, self.fsdp
        for dim in dims:
            rep = rep + self.near[dim][0] - self.rep
            fsdp = fsdp + self.near[dim][1] - self.fsdp
        return rep, fsdp


class CubeRows:
    def __init__(self, cube, own, full, keep, send, recv):
        self.cube, self.own, self.full = cube, own, full
        self.keep, self.send, self.recv = keep, send, recv

    def push(self, src, t, block, sem, dim):
        low, count = THIRDS[t][3:]
        rep, fsdp = self.cube.near[dim]
        remote(
            src.at[pl.ds(low, count)],
            self.full.at[block, pl.ds(low, count)],
            self.send.at[t, sem],
            self.recv.at[t, block],
            rep,
            fsdp,
        ).start()

    def come(self, t, *dims):
        low, count = THIRDS[t][3:]
        block = flip(self.cube.own, *dims)
        arrived(self.full.at[block, pl.ds(low, count)], self.recv.at[t, block])
        return block

    def start(self):
        own = self.cube.own
        for step in range(3):
            for t in range(3):
                self.push(self.own, t, own, (0, 1, 3)[step], THIRDS[t][step])
        pltpu.make_async_copy(self.own, self.full.at[own], self.keep).start()

    def kept(self):
        pltpu.make_async_copy(self.own, self.full.at[self.cube.own], self.keep).wait()

    def relay_one(self):
        for t, (one, two, three, _, _) in enumerate(THIRDS):
            block = self.come(t, one)
            self.push(self.full.at[block], t, block, 2, two)
            self.push(self.full.at[block], t, block, 4, three)
        for t, (one, two, three, _, _) in enumerate(THIRDS):
            block = self.come(t, two)
            self.push(self.full.at[block], t, block, 5, three)

    def relay_two(self):
        for t, (one, two, three, _, _) in enumerate(THIRDS):
            block = self.come(t, one, two)
            self.push(self.full.at[block], t, block, 6, three)

    def close_by(self):
        for t in range(3):
            self.come(t, THIRDS[t][2])

    def further(self):
        for t, (one, two, three, _, _) in enumerate(THIRDS):
            self.come(t, one, three)
            self.come(t, two, three)

    def last(self):
        for t, (one, two, three, _, _) in enumerate(THIRDS):
            self.come(t, one, two, three)

    def sent(self):
        for t in range(3):
            low, count = THIRDS[t][3:]
            for sem in range(7):
                arrived(self.full.at[0, pl.ds(low, count)], self.send.at[t, sem])


def cube_rows_sems():
    return [DMA(()), DMA((3, 7)), DMA((3, 8))]


class CubeSums:
    def __init__(self, cube, part, total, in_one, out_two, in_two, out_three, in_three, send, recv):
        self.cube, self.part, self.total = cube, part, total
        self.in_one, self.out_two, self.in_two = in_one, out_two, in_two
        self.out_three, self.in_three = out_three, in_three
        self.send, self.recv = send, recv

    def slot(self, t, block):
        one, two = THIRDS[t][:2]
        return (block // STEP[one]) % 2 + 2 * ((block // STEP[two]) % 2)

    def bit(self, t, block):
        return (block // STEP[THIRDS[t][0]]) % 2

    def give(self, t, block):
        three, low, count = THIRDS[t][2:]
        at = pl.ds(low, count)
        slot = self.slot(t, block)
        rep, fsdp = self.cube.near[three]
        remote(
            self.part.at[block, at],
            self.in_one.at[slot, at],
            self.send.at[t, slot],
            self.recv.at[t, slot],
            rep,
            fsdp,
        ).start()

    def give_all(self):
        for dims in ((), (0,), (1,), (0, 1)):
            for t in range(3):
                axes = [THIRDS[t][2]] + [THIRDS[t][d] for d in dims]
                self.give(t, flip(self.cube.own, *axes))

    def first(self, t, block):
        low, count = THIRDS[t][3:]
        at = pl.ds(low, count)
        slot = self.slot(t, block)
        arrived(self.in_one.at[slot, at], self.recv.at[t, slot])
        return self.part[block, at].astype(WIDE) + self.in_one[slot, at].astype(WIDE)

    def second(self, t, block):
        low, count = THIRDS[t][3:]
        at = pl.ds(low, count)
        value = self.first(t, block)
        bit = self.bit(t, block)
        arrived(self.in_two.at[bit, at], self.recv.at[t, 4 + bit])
        return value + self.in_two[bit, at].astype(WIDE)

    def fold_one(self):
        for t, (one, two, three, low, count) in enumerate(THIRDS):
            at = pl.ds(low, count)
            rep, fsdp = self.cube.near[two]
            for v, dims in enumerate(((two, one), (two,))):
                block = flip(self.cube.own, *dims)
                self.out_two[v, at] = self.first(t, block).astype(LOW)
                bit = self.bit(t, block)
                remote(
                    self.out_two.at[v, at],
                    self.in_two.at[bit, at],
                    self.send.at[t, 4 + v],
                    self.recv.at[t, 4 + bit],
                    rep,
                    fsdp,
                ).start()

    def fold_two(self):
        for t, (one, two, three, low, count) in enumerate(THIRDS):
            at = pl.ds(low, count)
            rep, fsdp = self.cube.near[one]
            self.out_three[at] = self.second(t, flip(self.cube.own, one)).astype(LOW)
            remote(
                self.out_three.at[at],
                self.in_three.at[at],
                self.send.at[t, 6],
                self.recv.at[t, 6],
                rep,
                fsdp,
            ).start()

    def finish(self):
        for t, (one, two, three, low, count) in enumerate(THIRDS):
            at = pl.ds(low, count)
            value = self.second(t, self.cube.own)
            arrived(self.in_three.at[at], self.recv.at[t, 6])
            self.total[at] = value + self.in_three[at].astype(WIDE)

    def sent(self):
        for t in range(3):
            low, count = THIRDS[t][3:]
            for sem in range(7):
                arrived(self.in_one.at[0, pl.ds(low, count)], self.send.at[t, sem])


def cube_sums_scratch():
    return [
        pltpu.VMEM((4, 128, D), LOW),
        pltpu.VMEM((2, 128, D), LOW),
        pltpu.VMEM((2, 128, D), LOW),
        pltpu.VMEM((128, D), LOW),
        pltpu.VMEM((128, D), LOW),
        DMA((3, 7)),
        DMA((3, 7)),
    ]


class CubeCollect:
    def __init__(self, cube, grads, out, pair_in, pair_sum, level_in, level_sum, send, recv, cross_send, cross_recv):
        self.cube, self.grads, self.out = cube, grads, out
        self.pair_in, self.pair_sum = pair_in, pair_sum
        self.level_in, self.level_sum = level_in, level_sum
        self.send, self.recv, self.cross_send, self.cross_recv = send, recv, cross_send, cross_recv
        self.half = grads.shape[1] // 2
        self.mine = piece(cube.core, self.half)
        self.theirs = piece(1 - cube.core, self.half)

    def start(self):
        cube = self.cube
        remote(
            self.grads.at[:, self.theirs],
            self.pair_in,
            self.send.at[0],
            self.recv.at[0],
            cube.partner,
            cube.fsdp,
        ).start()

    def fold_pair(self):
        cube = self.cube
        arrived(self.pair_in, self.recv.at[0])

        def add(i, carry):
            self.pair_sum[i] = (
                self.grads[i, self.mine].astype(WIDE) + self.pair_in[i].astype(WIDE)
            ).astype(LOW)
            return carry

        lax.fori_loop(0, 8, add, 0)
        remote(
            self.pair_sum.at[pl.ds(4 * (1 - cube.high), 4)],
            self.level_in,
            self.send.at[1],
            self.recv.at[1],
            cube.rep,
            cube.far,
        ).start()

    def fold_level(self):
        cube = self.cube
        arrived(self.level_in, self.recv.at[1])

        def add(i, carry):
            self.level_sum[i] = (
                self.pair_sum[4 * cube.high + i].astype(WIDE) + self.level_in[i].astype(WIDE)
            ).astype(LOW)
            return carry

        lax.fori_loop(0, 4, add, 0)
        for k, dims in enumerate(PEERS):
            rep, fsdp = cube.device(*dims)
            remote(
                self.level_sum.at[flip(cube.own, *dims) % 4],
                self.out.at[cube.own, self.mine],
                self.cross_send.at[k],
                self.cross_recv.at[cube.own],
                rep,
                fsdp,
            ).start()
        self.out[cube.own, self.mine] = self.level_sum[cube.own % 4]

    def land(self):
        cube = self.cube
        for dims in PEERS:
            block = flip(cube.own, *dims)
            arrived(self.out.at[block, self.mine], self.cross_recv.at[block])
        place = self.out.at[:, self.mine]
        remote(place, place, self.send.at[2], self.recv.at[2], cube.partner, cube.fsdp).start()

    def finish(self):
        arrived(self.out.at[:, self.theirs], self.recv.at[2])
        arrived(self.pair_in, self.send.at[0])
        arrived(self.level_in, self.send.at[1])
        arrived(self.pair_in, self.send.at[2])
        for k in range(7):
            arrived(self.level_in.at[0], self.cross_send.at[k])


PEERS = (("x",), ("z",), ("y",), ("x", "z"), ("x", "y"), ("z", "y"), ("x", "z", "y"))


def cube_collect_scratch(high, wide):
    return [
        pltpu.VMEM((8, high // 2, wide), LOW),
        pltpu.VMEM((8, high // 2, wide), LOW),
        pltpu.VMEM((4, high // 2, wide), LOW),
        pltpu.VMEM((4, high // 2, wide), LOW),
        DMA((3,)),
        DMA((3,)),
        DMA((7,)),
        DMA((8,)),
    ]


class CubeCollectRows:
    def __init__(self, cube, rows, out, pair_in, pair_sum, level_in, send, recv):
        self.cube, self.rows, self.out = cube, rows, out
        self.pair_in, self.pair_sum, self.level_in = pair_in, pair_sum, level_in
        self.send, self.recv = send, recv
        self.half = rows.shape[1] // 2
        self.mine = piece(cube.core, self.half)
        self.theirs = piece(1 - cube.core, self.half)

    def to(self, src, dst, index, rep, fsdp):
        remote(src, dst, self.send.at[index], self.recv.at[index], rep, fsdp).start()

    def start(self):
        cube = self.cube
        self.to(self.rows.at[:, self.theirs], self.pair_in, 0, cube.partner, cube.fsdp)

    def fold_pair(self):
        cube = self.cube
        arrived(self.pair_in, self.recv.at[0])
        self.pair_sum[...] = (
            self.rows[:, self.mine].astype(WIDE) + self.pair_in[...].astype(WIDE)
        ).astype(LOW)

        @pl.when(jnp.logical_not(cube.lends))
        def hand_over():
            self.to(self.pair_sum, self.level_in, 1, cube.rep, cube.far)

    def fold_level(self):
        cube = self.cube

        @pl.when(cube.lends)
        def close():
            arrived(self.level_in, self.recv.at[1])
            self.out[:, self.mine] = (
                self.pair_sum[...].astype(WIDE) + self.level_in[...].astype(WIDE)
            ).astype(LOW)
            place = self.out.at[:, self.mine]
            self.to(place, place, 2, *cube.near["y"])
            self.to(place, place, 3, cube.partner, cube.fsdp)

    def relay(self):
        cube = self.cube

        @pl.when(jnp.logical_not(cube.lends))
        def pass_on():
            place = self.out.at[:, self.mine]
            arrived(place, self.recv.at[2])
            self.to(place, place, 3, cube.partner, cube.fsdp)

    def finish(self):
        arrived(self.out.at[:, self.theirs], self.recv.at[3])
        arrived(self.pair_in, self.send.at[0])
        arrived(self.pair_in, self.send.at[3])
        pl.when(self.cube.lends)(lambda: arrived(self.pair_in, self.send.at[2]))
        pl.when(jnp.logical_not(self.cube.lends))(lambda: arrived(self.pair_in, self.send.at[1]))


def cube_collect_rows_scratch(tall):
    return [pltpu.VMEM((tall, D // 2), LOW)] * 3 + [DMA((4,)), DMA((4,))]


def low_shape(*shape):
    return jax.ShapeDtypeStruct(shape, LOW)


def wide_shape(*shape):
    return jax.ShapeDtypeStruct(shape, WIDE)


def scratch_of(hidden):
    low, wide = (lambda *shape: pltpu.VMEM(shape, LOW)), (lambda *shape: pltpu.VMEM(shape, WIDE))
    single = {
        "marks": wide(8, 1024),
        "small": wide(8, 128),
        "cosine_step": wide(64, 128),
        "sine_step": wide(64, 128),
        "rows_full": low(8, 128, 1024),
        "firsts_full": low(8, 128, 128),
        "weights": low(8, 128, 384),
        "packed": low(8, 128, 768),
        "packed_full": low(8, 128, 768),
        "grad_full": low(8, 128, 1024),
        "hidden_one": low(8, 128, 1024),
        "queries": low(1024, 128),
        "keys": low(1024, 128),
        "keys_turned": low(128, 1024),
        "values": low(1024, 128),
        "values_turned": low(128, 1024),
        "attended": low(1024, 128),
        "totals": wide(1024, 128),
        "middle": wide(128, 1024),
        "hidden_two": low(128, 1024),
        "hidden_full": low(8, 128, 1024),
        "active": low(1024, 384),
        "both": low(1024, 768),
        "down_pad": low(384, 1024),
        "part": low(8, 128, 1024),
        "out_part": low(8, 128, 1024),
        "total": wide(128, 1024),
        "middle_grad": wide(128, 1024),
        "branch": low(128, 1024),
        "gain_two_term": wide(1, 1024),
        "down_grad": low(hidden, 1024),
        "branch_full": low(8, 128, 1024),
        "out_grad": low(1024, 128),
        "query_grad": wide(1024, 128),
        "key_acc": wide(128, 1024),
        "value_acc": wide(128, 1024),
        "three": low(1024, 384),
        "qkv_grads": low(8, 128, 384),
        "qkv_out": low(8, 128, 384),
        "packed_out": low(8, 128, 768),
        "output_grad": low(128, 1024),
        "gain_own": wide(8, 8, 128),
        "gain_in": wide(8, 8, 128),
        "gain_part": wide(8, 128),
        "gain_rep": wide(4, 8, 128),
        "value_blocks": low(8, 128, 128),
        "keep": DMA((6,)),
        "w_send": DMA((3, 7)),
        "w_recv": DMA((3, 8)),
        "p_send": DMA((7,)),
        "p_recv": DMA((8,)),
        "s_send": DMA((7,)),
        "s_recv": DMA((8,)),
        "f_send": DMA((7,)),
        "f_recv": DMA((8,)),
        "m_send": DMA((7,)),
        "m_recv": DMA((8,)),
        "mp_send": DMA((7,)),
        "mp_recv": DMA((8,)),
        "g_send": DMA((7,)),
        "g_recv": DMA((8,)),
        "gr_send": DMA((3,)),
        "gr_recv": DMA((4,)),
        "v_send": DMA((7,)),
        "v_recv": DMA((8,)),
        "d_send": DMA((2,)),
        "d_recv": DMA((2,)),
    }
    groups = {
        "sums_one": sums_scratch(),
        "sums_two": cube_sums_scratch(),
        "sums_out": cube_sums_scratch(),
        "sums_three": sums_scratch(),
        "row_flow": rows_sems(),
        "grad_flow": cube_rows_sems(),
        "hidden_flow": cube_rows_sems(),
        "branch_flow": rows_sems(),
        "packed_flow": cube_collect_scratch(128, 768),
        "qkv_flow": collect_scratch(128, 384),
        "down_flow": cube_collect_rows_scratch(hidden),
        "output_flow": collect_rows_scratch(128),
    }
    return single, groups


def layer_kernel(
    hidden,
    rows,
    firsts,
    prefix,
    positions,
    first_gain,
    query_weight,
    key_weight,
    value_weight,
    output_weight,
    second_gain,
    gate_weight,
    up_weight,
    down,
    cotangent,
    layer_output,
    input_grad,
    firsts_grad,
    query_out,
    key_out,
    value_out,
    output_out,
    gate_out,
    up_out,
    down_out,
    gains,
    *refs,
):
    single, groups = scratch_of(hidden)
    s = types.SimpleNamespace(**dict(zip(single, refs)))
    refs = list(refs[len(single) :])
    for name, shapes in groups.items():
        setattr(s, name, refs[: len(shapes)])
        refs = refs[len(shapes) :]
    rep, fsdp, z, x = plane_place()
    core, level = lax.rem(rep, 2), rep // 2
    partner = rep + 1 - 2 * core
    above = rep + 2 - 4 * level
    slant = 3 - rep
    others = [lax.rem(fsdp + k, 8) for k in range(1, 8)]
    cube = Cube()
    greet(
        [(rep, other) for other in others]
        + [(partner, fsdp), (above, fsdp), (slant, fsdp)]
        + [cube.device("y", "x"), cube.device("y", "z"), cube.device("y", "z", "x")]
    )
    mine = piece(core, 64)
    theirs = piece(1 - core, 64)
    started, kept = [], []
    row_flow = Rows(rows, s.rows_full, *s.row_flow)
    grad_flow = CubeRows(cube, cotangent, s.grad_full, *s.grad_flow)
    hidden_flow = CubeRows(cube, s.hidden_two, s.hidden_full, *s.hidden_flow)
    branch_flow = Rows(s.branch, s.branch_full, *s.branch_flow)
    sums_one, sums_three = Sums(*s.sums_one), Sums(*s.sums_three)
    sums_two = CubeSums(cube, s.part, s.total, *s.sums_two)
    sums_out = CubeSums(cube, s.out_part, s.total, *s.sums_out)
    packed_flow = CubeCollect(cube, s.packed, s.packed_out, *s.packed_flow)
    qkv_flow = Collect(s.qkv_grads, s.qkv_out, *s.qkv_flow)
    down_flow = CubeCollectRows(cube, s.down_grad, down_out, *s.down_flow)
    output_flow = CollectRows(s.output_grad, output_out, *s.output_flow)

    def go(copy):
        copy.start()
        started.append(copy)

    def here(src, dst):
        copy = pltpu.make_async_copy(src, dst, s.keep.at[len(kept)])
        copy.start()
        kept.append(copy)

    sources = (query_weight, key_weight, value_weight)
    for k, other in enumerate(others):
        for i, source in enumerate(sources):
            go(
                remote(
                    source.at[mine, piece(other, 128)],
                    s.weights.at[fsdp, mine, pl.ds(128 * i, 128)],
                    s.w_send.at[i, k],
                    s.w_recv.at[i, fsdp],
                    rep,
                    other,
                )
            )
    row_flow.start()
    rates = turn_rates()
    place_row = positions[...].astype(WIDE)
    lane = lax.broadcasted_iota(jnp.int32, (1, 128), 1)
    s.small[0:1, :] = place_row
    s.small[1:2, :] = first_gain[...].astype(WIDE)
    s.small[2:3, :] = second_gain[...].astype(WIDE)
    for run in range(2):
        begin = jnp.sum(jnp.where(lane == 64 * run, place_row, 0.0), axis=1, keepdims=True)
        s.small[3 + 2 * run : 4 + 2 * run, :] = jnp.cos(begin * rates)
        s.small[4 + 2 * run : 5 + 2 * run, :] = jnp.sin(begin * rates)
    s.small[7:8, :] = jnp.zeros((1, 128), WIDE)
    for k, other in enumerate(others):
        go(
            remote(
                s.small, s.marks.at[:, piece(fsdp, 128)], s.s_send.at[k], s.s_recv.at[fsdp], rep, other
            )
        )
    for k, other in enumerate(others):
        go(
            remote(
                firsts.at[:, piece(other, 128)],
                s.firsts_full.at[fsdp],
                s.f_send.at[k],
                s.f_recv.at[fsdp],
                rep,
                other,
            )
        )
    grad_flow.start()
    for i, source in enumerate(sources):
        here(source.at[:, piece(fsdp, 128)], s.weights.at[fsdp, :, pl.ds(128 * i, 128)])
    here(s.small, s.marks.at[:, piece(fsdp, 128)])
    here(firsts.at[:, piece(fsdp, 128)], s.firsts_full.at[fsdp])
    angles = lax.broadcasted_iota(jnp.int32, (64, 128), 0).astype(WIDE) * rates
    s.cosine_step[...] = jnp.cos(angles)
    s.sine_step[...] = jnp.sin(angles)
    pad = jnp.zeros((128, 384 - hidden), LOW)
    for i in range(8):
        s.packed[i, :, 0:hidden] = gate_weight[:, hidden * i : hidden * (i + 1)]
        s.packed[i, :, hidden:384] = pad
        s.packed[i, :, 384 : 384 + hidden] = up_weight[:, hidden * i : hidden * (i + 1)]
        s.packed[i, :, 384 + hidden : 768] = pad
    here(s.packed.at[cube.own], s.packed_full.at[fsdp])

    row_flow.pass_on(0)
    for k, other in enumerate(others):
        for i in range(3):
            arrived(s.weights.at[other, mine, pl.ds(128 * i, 128)], s.w_recv.at[i, other])
        place = s.weights.at[other, mine]
        go(remote(place, place, s.p_send.at[k], s.p_recv.at[other], partner, fsdp))
    row_flow.pass_on(1)
    grad_flow.relay_one()
    for other in others:
        arrived(s.marks.at[:, piece(other, 128)], s.s_recv.at[other])
    for copy in kept:
        copy.wait()
    row_flow.kept()
    for other in others:
        arrived(s.weights.at[other, theirs], s.p_recv.at[other])
        arrived(s.firsts_full.at[other], s.f_recv.at[other])

    def project(block):
        entry = s.rows_full[block].astype(WIDE)
        scale = lax.rsqrt(jnp.mean(entry * entry, axis=-1, keepdims=True) + epsilon)
        low = (entry * scale * s.marks[1:2, :]).astype(LOW)
        s.hidden_one[block] = low
        pre = matmul(low, s.weights[...].reshape(8 * 128, 384))
        cosine, sine = turn_tables(s.marks, block, s.cosine_step, s.sine_step)
        at = piece(block, 128)
        s.queries[at, :] = turn(pre[:, :128], cosine, sine).astype(LOW)
        key = turn(pre[:, 128:256], cosine, sine)
        s.keys[at, :] = key.astype(LOW)
        s.keys_turned[:, at] = key.T.astype(LOW)
        value = 0.5 * pre[:, 256:] + 0.5 * s.firsts_full[block].astype(WIDE)
        s.values[at, :] = value.astype(LOW)
        s.values_turned[:, at] = value.T.astype(LOW)

    def project_column(k, carry):
        @pl.when(k == 2)
        def hand_on():
            row_flow.pass_on(2)

        project(2 * row_flow.line(k) + x)
        return carry

    def project_across(k, carry):
        project(row_flow.across(lax.rem(z + k, 4)))
        return carry

    project(fsdp)
    lax.fori_loop(0, 3, project_column, 0)
    grad_flow.relay_two()
    for k, other in enumerate(others):
        go(
            remote(
                s.packed.at[other % 4 + 4 * cube.y, mine],
                s.packed_full.at[fsdp, mine],
                s.m_send.at[k],
                s.m_recv.at[fsdp],
                rep,
                other,
            )
        )
    used = hidden // 2
    down_half = piece(core, used)
    s.down_pad[hidden:384, :] = jnp.zeros((384 - hidden, D), LOW)

    @pl.when(cube.lends)
    def lend():
        s.down_pad[0:hidden, :] = down[...]
        remote(
            down.at[down_half], s.down_pad.at[down_half], s.d_send.at[0], s.d_recv.at[0], rep, cube.far
        ).start()

    lax.fori_loop(0, 4, project_across, 0)
    prefix_last = (prefix[rep] - 1).astype(WIDE)
    masks = [head_lanes(head) for head in range(2)]

    def attend(block):
        at = piece(block, 128)
        query = s.queries[at, :]
        allowed = s.marks[0:1, :] <= limit_column(s.marks, block, prefix_last)
        result = total = None
        for head in range(2):
            scores = matmul(only(masks[head], query), s.keys_turned[...]) * E ** (-0.5)
            scores = jnp.where(allowed, scores, masked_score)
            top = jnp.max(scores, axis=-1, keepdims=True)
            weight = jnp.exp(scores - top)
            below = jnp.sum(weight, axis=-1, keepdims=True)
            probabilities = (weight * (1.0 / below)).astype(LOW)
            out = matmul(probabilities, s.values[...])
            log_total = jnp.broadcast_to(top + jnp.log(below), out.shape)
            result = out if head == 0 else jnp.where(masks[0], result, out)
            total = log_total if head == 0 else jnp.where(masks[0], total, log_total)
        s.totals[at, :] = total
        low = result.astype(LOW)
        s.attended[at, :] = low
        return matmul(low, output_weight[...])

    def attend_across(k, carry):
        other = sums_one.other(k)
        s.part[other] = attend(2 * other + 1 - x).astype(LOW)
        sums_one.give(k, s.part.at[other])

        return carry

    lax.fori_loop(0, 4, attend_across, 0)
    for k, other in enumerate(others):
        place = s.packed_full.at[other, mine]
        arrived(place, s.m_recv.at[other])
        go(remote(place, place, s.mp_send.at[k], s.mp_recv.at[other], partner, fsdp))

    @pl.when(jnp.logical_not(cube.lends))
    def borrow():
        place = s.down_pad.at[down_half]
        arrived(place, s.d_recv.at[0])
        remote(place, place, s.d_send.at[1], s.d_recv.at[1], partner, fsdp).start()

    def attend_column(k, carry):
        sums_one.forward(k, attend(2 * sums_one.other(k) + x))
        return carry

    lax.fori_loop(0, 3, attend_column, 0)
    total = rows[...].astype(WIDE) + sums_one.total(attend(fsdp))
    s.middle[...] = total
    scale = lax.rsqrt(jnp.mean(total * total, axis=-1, keepdims=True) + epsilon)
    s.hidden_two[...] = (total * scale * s.marks[2:3, :]).astype(LOW)

    hidden_flow.start()
    grad_flow.close_by()
    grad_flow.further()
    grad_flow.last()
    grad_flow.kept()

    @pl.when(jnp.logical_not(cube.lends))
    def borrowed():
        arrived(s.down_pad.at[piece(1 - core, used)], s.d_recv.at[1])

    for other in others:
        arrived(s.packed_full.at[other, theirs], s.mp_recv.at[other])

    def feed(block):
        at = piece(block, 128)
        packed = s.packed_full[...].reshape(8 * 128, 768)
        pre = matmul(s.hidden_full[block], packed)
        gate, up = pre[:, :384], pre[:, 384:]
        sigmoid = 1.0 / (1.0 + jnp.exp(-gate))
        swish = gate * sigmoid
        act = (swish * up).astype(LOW)
        s.active[at, :] = act
        act_grad = times_transposed(s.grad_full[block], s.down_pad[...])
        gate_grad = act_grad * up * sigmoid * (1.0 + gate * (1.0 - sigmoid))
        s.both[at, 0:384] = gate_grad.astype(LOW)
        s.both[at, 384:768] = (act_grad * swish).astype(LOW)
        s.part[block] = times_transposed(s.both[at, :], packed).astype(LOW)
        s.out_part[block] = matmul(act, s.down_pad[...]).astype(LOW)

    sums_one.sent()
    hidden_flow.kept()

    def feed_near(i, carry):
        @pl.when(i == 1)
        def first_wait():
            hidden_flow.relay_one()
            hidden_flow.close_by()

        pl.when(i == 2)(hidden_flow.relay_two)
        step = i + i // 3
        block = cube.own + step - 2 * step * (cube.own // (step + (3 - i) // 3) % 2)
        feed(block)
        for i_now, t in ((1, 1), (2, 0), (3, 2)):
            pl.when(i == i_now)(functools.partial(sums_two.give, t, block))
        return carry

    def feed_far(j, carry):
        pl.when(j == 0)(hidden_flow.further)
        pl.when(j == 3)(hidden_flow.last)
        i = (j + 1) % 4
        step = i + i // 3
        base = 7 - cube.own
        block = base + step - 2 * step * (base // (step + (3 - i) // 3) % 2)
        feed(block)
        for j_not, t in ((1, 0), (0, 1), (2, 2)):
            pl.when(j != j_not)(functools.partial(sums_two.give, t, block))
        return carry

    lax.fori_loop(0, 4, feed_near, 0)
    lax.fori_loop(0, 4, feed_far, 0)

    def feed_grads(i, carry):
        turned = s.hidden_full[:, :, piece(i, 128)].reshape(8 * 128, 128)
        s.packed[i] = transposed_times(turned, s.both[...]).astype(LOW)
        return carry

    for copy in started:
        copy.wait_send()

    lax.fori_loop(0, 3, feed_grads, 0)
    sums_two.fold_one()
    lax.fori_loop(3, 6, feed_grads, 0)
    sums_two.fold_two()
    lax.fori_loop(6, 8, feed_grads, 0)
    sums_two.finish()
    hidden_grad = s.total[...]
    entry = s.middle[...]
    scale = lax.rsqrt(jnp.mean(entry * entry, axis=-1, keepdims=True) + epsilon)
    normed = entry * scale
    normed_grad = hidden_grad * s.marks[2:3, :]
    back = scale * (normed_grad - normed * jnp.mean(normed_grad * normed, axis=-1, keepdims=True))
    grad = cotangent[...].astype(WIDE) + back
    s.branch[...] = grad.astype(LOW)
    branch_flow.start()
    s.middle_grad[...] = grad
    s.gain_two_term[...] = jnp.sum(hidden_grad * normed, axis=0, keepdims=True)

    def pull(block):
        s.out_grad[piece(block, 128), :] = times_transposed(
            s.branch_full[block], output_weight[...]
        ).astype(LOW)

    packed_flow.start()
    down_sum = transposed_times(s.active[...], s.grad_full[...].reshape(8 * 128, D))
    s.down_grad[...] = down_sum[0:hidden].astype(LOW)
    down_flow.start()
    branch_flow.kept()
    pull(fsdp)

    def pull_column(k, carry):
        pull(branch_flow.pass_on(k))
        return carry

    def pull_across(k, carry):
        pull(branch_flow.across(lax.rem(z + k, 4)))
        return carry

    lax.fori_loop(0, 3, pull_column, 0)
    lax.fori_loop(0, 4, pull_across, 0)
    sums_out.give_all()
    packed_flow.fold_pair()
    down_flow.fold_pair()
    s.output_grad[...] = transposed_times(
        s.attended[...], s.branch_full[...].reshape(8 * 128, D)
    ).astype(LOW)
    output_flow.start()
    s.key_acc[...] = jnp.zeros_like(s.key_acc)
    s.value_acc[...] = jnp.zeros_like(s.value_acc)

    def attend_back(block, carry):
        at = piece(block, 128)
        query, grad = s.queries[at, :], s.out_grad[at, :]
        log_total = s.totals[at, :]
        allowed = s.marks[0:1, :] <= limit_column(s.marks, block, prefix_last)
        result = None
        lows, score_grads, turned_queries, turned_grads = [], [], [], []
        for head in range(2):
            query_here, grad_here = only(masks[head], query), only(masks[head], grad)
            scores = matmul(query_here, s.keys_turned[...]) * E ** (-0.5)
            column = log_total[:, head * E : head * E + 1]
            probabilities = jnp.where(allowed, jnp.exp(scores - column), 0.0)
            prob_grad = matmul(grad_here, s.values_turned[...])
            delta = jnp.sum(probabilities * prob_grad, axis=-1, keepdims=True)
            score_grad = (probabilities * (prob_grad - delta)).astype(LOW)
            out = matmul(score_grad, s.keys[...])
            result = out if head == 0 else jnp.where(masks[0], result, out)
            lows.append(probabilities.astype(LOW))
            score_grads.append(score_grad)
            turned_queries.append(query_here.astype(WIDE).T)
            turned_grads.append(grad_here.astype(WIDE).T)
        s.query_grad[at, :] = result
        s.key_acc[...] += matmul(
            jnp.concatenate(turned_queries, axis=1).astype(LOW),
            jnp.concatenate(score_grads, axis=0),
        )
        s.value_acc[...] += matmul(
            jnp.concatenate(turned_grads, axis=1).astype(LOW), jnp.concatenate(lows, axis=0)
        )

        return carry

    lax.fori_loop(0, 8, attend_back, 0)

    def close(block):
        at = piece(block, 128)
        cosine, sine = turn_tables(s.marks, block, s.cosine_step, s.sine_step)
        s.three[at, 0:128] = turn(s.query_grad[at, :] * E ** (-0.5), cosine, -sine).astype(LOW)
        s.three[at, 128:256] = turn(s.key_acc[:, at].T * E ** (-0.5), cosine, -sine).astype(LOW)
        value_grad = (0.5 * s.value_acc[:, at].T).astype(LOW)
        s.three[at, 256:384] = value_grad
        s.value_blocks[block] = value_grad
        return times_transposed(s.three[at, :], s.weights[...].reshape(8 * 128, 384))

    def close_across(k, carry):
        other = sums_three.other(k)
        block = 2 * other + 1 - x
        s.part[block] = close(block).astype(LOW)
        sums_three.give(k, s.part.at[block])
        return carry

    def close_column(k, carry):
        block = 2 * sums_three.other(k) + x
        s.part[block] = close(block).astype(LOW)
        return carry

    sums_two.sent()
    lax.fori_loop(0, 4, close_across, 0)
    lax.fori_loop(0, 4, close_column, 0)
    for k, other in enumerate(others):
        remote(
            s.value_blocks.at[other],
            firsts_grad.at[:, piece(fsdp, 128)],
            s.v_send.at[k],
            s.v_recv.at[fsdp],
            rep,
            other,
        ).start()
    firsts_grad[:, piece(fsdp, 128)] = s.value_blocks[fsdp]

    def qkv_grads(i, carry):
        turned = s.hidden_one[:, :, piece(i, 128)].reshape(8 * 128, 128)
        s.qkv_grads[i] = transposed_times(turned, s.three[...]).astype(LOW)
        return carry

    lax.fori_loop(0, 8, qkv_grads, 0)
    qkv_flow.start()
    sums_out.fold_one()
    output_flow.fold_pair()
    packed_flow.fold_level()
    down_flow.fold_level()

    def onward(k):
        sums_three.forward(k, s.part[2 * sums_three.other(k) + x].astype(WIDE))

    onward(0)
    qkv_flow.fold_pair()
    sums_out.fold_two()
    onward(1)
    output_flow.fold_level()
    down_flow.relay()
    qkv_flow.fold_level()
    onward(2)
    packed_flow.land()
    sums_out.finish()
    layer_output[...] = (s.middle[...] + s.total[...]).astype(LOW)
    output_flow.relay()
    qkv_flow.land()
    hidden_grad = sums_three.total(s.part[fsdp].astype(WIDE))
    entry = rows[...].astype(WIDE)
    scale = lax.rsqrt(jnp.mean(entry * entry, axis=-1, keepdims=True) + epsilon)
    normed = entry * scale
    normed_grad = hidden_grad * s.marks[1:2, :]
    gain_term = jnp.sum(hidden_grad * normed, axis=0, keepdims=True)
    for i in range(8):
        lanes = slice(128 * i, 128 * i + 128)
        s.gain_own[i, 0:1, :] = gain_term[:, lanes]
        s.gain_own[i, 1:2, :] = s.gain_two_term[:, lanes]
        s.gain_own[i, 2:8, :] = jnp.zeros((6, 128), WIDE)
    for k, other in enumerate(others):
        remote(
            s.gain_own.at[other], s.gain_in.at[fsdp], s.g_send.at[k], s.g_recv.at[fsdp], rep, other
        ).start()
    back = scale * (normed_grad - normed * jnp.mean(normed_grad * normed, axis=-1, keepdims=True))
    input_grad[...] = s.middle_grad[...] + back
    packed_flow.finish()
    for i in range(8):
        wide = slice(hidden * i, hidden * (i + 1))
        gate_out[:, wide] = s.packed_out[i, :, 0:hidden]
        up_out[:, wide] = s.packed_out[i, :, 384 : 384 + hidden]
    qkv_flow.relay()
    s.gain_in[fsdp] = s.gain_own[fsdp]
    for other in others:
        arrived(s.gain_in.at[other], s.g_recv.at[other])
    s.gain_part[...] = jnp.sum(s.gain_in[...], axis=0)
    for k, target in enumerate((partner, above, slant)):
        remote(
            s.gain_part, s.gain_rep.at[rep], s.gr_send.at[k], s.gr_recv.at[rep], target, fsdp
        ).start()
    s.gain_rep[rep] = s.gain_part[...]
    for k, other in enumerate(others):
        arrived(firsts_grad.at[:, piece(other, 128)], s.v_recv.at[other])
        arrived(s.value_blocks.at[0], s.v_send.at[k])
        arrived(s.gain_own.at[0], s.g_send.at[k])
    for k, source in enumerate((partner, above, slant)):
        arrived(s.gain_rep.at[source], s.gr_recv.at[source])
        arrived(s.gain_part, s.gr_send.at[k])
    gains[...] = jnp.sum(s.gain_rep[...], axis=0)
    down_flow.finish()
    output_flow.finish()
    qkv_flow.finish()
    for i in range(8):
        lanes = slice(128 * i, 128 * i + 128)
        query_out[:, lanes] = s.qkv_out[i, :, 0:128]
        key_out[:, lanes] = s.qkv_out[i, :, 128:256]
        value_out[:, lanes] = s.qkv_out[i, :, 256:384]
    pl.when(cube.lends)(lambda: arrived(s.down_pad.at[down_half], s.d_send.at[0]))
    pl.when(jnp.logical_not(cube.lends))(lambda: arrived(s.down_pad.at[down_half], s.d_send.at[1]))
    for flow in (row_flow, grad_flow, hidden_flow, branch_flow):
        flow.sent()
    for sums in (sums_out, sums_three):
        sums.sent()


def shards_plane(
    inputs,
    first_values,
    prefix,
    positions,
    first_gain,
    query_weight,
    key_weight,
    value_weight,
    output_weight,
    second_gain,
    gate_weight,
    up_weight,
    down_weight,
    cotangent,
):
    hidden = down_weight.shape[0]
    single, groups = scratch_of(hidden)
    outs = pl.pallas_call(
        functools.partial(layer_kernel, hidden),
        out_shape=[
            low_shape(128, D),
            wide_shape(128, D),
            low_shape(128, D),
            low_shape(128, D),
            low_shape(128, D),
            low_shape(128, D),
            low_shape(128, D),
            low_shape(128, 8 * hidden),
            low_shape(128, 8 * hidden),
            low_shape(hidden, D),
            wide_shape(8, 128),
        ],
        in_specs=[VM, VM, SM] + [VM] * 11,
        out_specs=[VM] * 11,
        scratch_shapes=list(single.values()) + [shape for group in groups.values() for shape in group],
        compiler_params=pltpu.CompilerParams(
            collective_id=1, has_side_effects=True, vmem_limit_bytes=LIMIT
        ),
    )(
        inputs,
        first_values,
        prefix,
        positions[None],
        first_gain[None],
        query_weight,
        key_weight,
        value_weight,
        output_weight,
        second_gain[None],
        gate_weight,
        up_weight,
        down_weight,
        cotangent,
    )
    layer_output, input_grad = outs[:2]
    firsts, query, key, value, output, gate, up, down = [a.astype(WIDE) for a in outs[2:10]]
    gains = outs[10]
    return (
        layer_output,
        input_grad,
        firsts,
        gains[0],
        query,
        key,
        value,
        output,
        gains[1],
        gate,
        up,
        down,
    )


def pick_body(mesh):
    if mesh.shape["fsdp"] == 8 and mesh.shape["rep"] == 4:
        return shards_plane
    return shards_general


def solution(mesh):
    placed = (
        P(("rep", "fsdp"), None),
        P(("rep", "fsdp"), None),
        P(),
        P(("rep", "fsdp")),
        P("fsdp"),
        P("fsdp", None),
        P("fsdp", None),
        P("fsdp", None),
        P("fsdp", None),
        P("fsdp"),
        P("fsdp", None),
        P("fsdp", None),
        P("fsdp", None),
        P(("rep", "fsdp"), None),
    )
    return jax.shard_map(
        pick_body(mesh),
        mesh=mesh,
        in_specs=placed,
        out_specs=(
            P(("rep", "fsdp"), None),
            P(("rep", "fsdp"), None),
            P(("rep", "fsdp"), None),
            P("fsdp"),
            P("fsdp", None),
            P("fsdp", None),
            P("fsdp", None),
            P("fsdp", None),
            P("fsdp"),
            P("fsdp", None),
            P("fsdp", None),
            P("fsdp", None),
        ),
        check_vma=False,
    )
```

```python
import functools
import math
import types

import jax
import jax.numpy as jnp
from jax import lax
from jax.experimental import pallas as pl
from jax.experimental.pallas import tpu as pltpu
from jax.sharding import PartitionSpec as P

D = 1024
H = 16
E = 64


epsilon = 1e-06
masked_score = -1e30


def rms_scale(values):
    return lax.rsqrt(jnp.mean(values * values, axis=-1, keepdims=True) + epsilon)


def rope_tables(places):
    half_width = E // 2
    frequency = jnp.exp(
        jnp.arange(half_width, dtype=jnp.float32) * (-math.log(10000.0) / half_width)
    )
    angles = places.astype(jnp.float32)[:, None] * frequency[None, :]
    return (jnp.cos(angles)[:, None, :], jnp.sin(angles)[:, None, :])


def rope_apply(shaped, cosine, sine_table):
    half_width = shaped.shape[-1] // 2
    first_half = shaped[..., :half_width]
    second_half = shaped[..., half_width:]
    return jnp.concatenate(
        [
            first_half * cosine - second_half * sine_table,
            second_half * cosine + first_half * sine_table,
        ],
        axis=-1,
    )


def rope_undo(shaped, cosine, sine_table):
    half_width = shaped.shape[-1] // 2
    first_half = shaped[..., :half_width]
    second_half = shaped[..., half_width:]
    return jnp.concatenate(
        [
            first_half * cosine + second_half * sine_table,
            second_half * cosine - first_half * sine_table,
        ],
        axis=-1,
    )


def times_transposed(left, right):
    return lax.dot_general(
        left, right, (((1,), (1,)), ((), ())), preferred_element_type=jnp.float32
    )


def transposed_times(left, right):
    return lax.dot_general(
        left, right, (((0,), (0,)), ((), ())), preferred_element_type=jnp.float32
    )


def block_rows(count):
    size_now = count
    while size_now > 1024 and size_now % 2 == 0:
        size_now = size_now // 2
    return size_now


def split_blocks(array, size_now):
    return array.reshape((array.shape[0] // size_now, size_now) + array.shape[1:])


def masked_scores(queries, key_rows, limits, key_places):
    scores = jnp.einsum(
        "qhe,khe->hqk", queries, key_rows, preferred_element_type=jnp.float32
    ) * E ** (-0.5)
    allowed = key_places[None, None, :] <= limits[None, :, None]
    return (scores, allowed)


def grad_block(queries, key_rows, value_rows, limits, key_places, out_low, log_total, delta_rows):
    scores, allowed = masked_scores(queries, key_rows, limits, key_places)
    probabilities = jnp.where(allowed, jnp.exp(scores - log_total[:, :, None]), 0.0)
    prob_grad = jnp.einsum("qhe,khe->hqk", out_low, value_rows, preferred_element_type=jnp.float32)
    score_grad = (probabilities * (prob_grad - delta_rows[:, :, None])).astype(jnp.bfloat16)
    return (probabilities.astype(jnp.bfloat16), score_grad)


def norm_back(hidden_grad, normed, gain_float, scale_rows):
    normed_grad = hidden_grad * gain_float
    gain_term = jnp.sum(hidden_grad * normed, axis=0)
    rows_grad = scale_rows * (
        normed_grad - normed * jnp.mean(normed_grad * normed, axis=-1, keepdims=True)
    )
    return (gain_term, rows_grad)


def shards_general(
    inputs,
    first_values,
    prefix,
    positions,
    first_gain,
    query_weight,
    key_weight,
    value_weight,
    output_weight,
    second_gain,
    gate_weight,
    up_weight,
    down_weight,
    cotangent,
):
    token_count = inputs.shape[0]
    gain_one, query_full, key_full, value_full, output_full = (
        lax.all_gather(first_gain, "fsdp", axis=0, tiled=True),
        lax.all_gather(query_weight, "fsdp", axis=0, tiled=True),
        lax.all_gather(key_weight, "fsdp", axis=0, tiled=True),
        lax.all_gather(value_weight, "fsdp", axis=0, tiled=True),
        lax.all_gather(output_weight, "fsdp", axis=0, tiled=True),
    )
    all_places = lax.all_gather(positions, "fsdp", axis=0, tiled=True)
    prefix_here = lax.dynamic_index_in_dim(prefix, lax.axis_index("rep"), keepdims=False)
    own_limits = jnp.maximum(positions, prefix_here - 1)
    cosine, sine_table = rope_tables(positions)
    rows_float = inputs.astype(jnp.float32)
    scale_one = rms_scale(rows_float)
    normed_one = rows_float * scale_one
    gain_one_float = gain_one.astype(jnp.float32)
    hidden_one = (normed_one * gain_one_float).astype(jnp.bfloat16)
    query_pre = jnp.dot(hidden_one, query_full, preferred_element_type=jnp.float32)
    key_pre = jnp.dot(hidden_one, key_full, preferred_element_type=jnp.float32)
    value_pre = jnp.dot(hidden_one, value_full, preferred_element_type=jnp.float32)
    queries = rope_apply(query_pre.reshape(token_count, H, E), cosine, sine_table).astype(
        jnp.bfloat16
    )
    key_rows = (
        rope_apply(key_pre.reshape(token_count, H, E), cosine, sine_table)
        .astype(jnp.bfloat16)
        .reshape(token_count, D)
    )
    mixed_values = (0.5 * value_pre + 0.5 * first_values.astype(jnp.float32)).astype(jnp.bfloat16)
    start_state = (
        jnp.full((H, token_count), masked_score, jnp.float32),
        jnp.zeros((H, token_count), jnp.float32),
        jnp.zeros((token_count, H, E), jnp.float32),
    )
    running = start_state
    key_piece = lax.all_gather(key_rows, "fsdp", axis=0, tiled=True)
    value_piece = lax.all_gather(mixed_values, "fsdp", axis=0, tiled=True)
    count = key_piece.shape[0]
    size_now = block_rows(count)

    def forward_step(state_now, blocks):
        row_max, row_sum, accum = state_now
        key_block, value_block, place_block = blocks
        scores, allowed = masked_scores(
            queries, key_block.reshape(-1, H, E), own_limits, place_block
        )
        new_max = jnp.maximum(row_max, jnp.max(jnp.where(allowed, scores, masked_score), axis=-1))
        rescale = jnp.exp(row_max - new_max)
        weights = jnp.where(allowed, jnp.exp(scores - new_max[:, :, None]), 0.0)
        row_sum = row_sum * rescale + jnp.sum(weights, axis=-1)
        accum = accum * rescale.T[:, :, None] + jnp.einsum(
            "hqk,khe->qhe",
            weights.astype(jnp.bfloat16),
            value_block.reshape(-1, H, E),
            preferred_element_type=jnp.float32,
        )
        return ((new_max, row_sum, accum), None)

    running, unused = lax.scan(
        forward_step,
        running,
        (
            split_blocks(key_piece, size_now),
            split_blocks(value_piece, size_now),
            split_blocks(all_places, size_now),
        ),
    )
    row_max, row_sum, accum = running
    log_total = row_max + jnp.log(row_sum)
    attended = accum / row_sum.T[:, :, None]
    attended_low = attended.reshape(token_count, D).astype(jnp.bfloat16)
    middle = rows_float + jnp.dot(attended_low, output_full, preferred_element_type=jnp.float32)
    mlp_forward = (
        lax.all_gather(second_gain, "fsdp", axis=0, tiled=True),
        lax.all_gather(gate_weight, "fsdp", axis=0, tiled=True),
        lax.all_gather(up_weight, "fsdp", axis=0, tiled=True),
        lax.all_gather(down_weight, "fsdp", axis=0, tiled=True),
    )
    gain_two, gate_full, up_full, down_full = mlp_forward
    scale_two = rms_scale(middle)
    normed_two = middle * scale_two
    hidden_two = (normed_two * gain_two.astype(jnp.float32)).astype(jnp.bfloat16)
    gate_pre = jnp.dot(hidden_two, gate_full, preferred_element_type=jnp.float32)
    up_pre = jnp.dot(hidden_two, up_full, preferred_element_type=jnp.float32)
    sigmoid_gate = jax.nn.sigmoid(gate_pre)
    activated = (gate_pre * sigmoid_gate * up_pre).astype(jnp.bfloat16)
    layer_output = (
        middle + jnp.dot(activated, down_full, preferred_element_type=jnp.float32)
    ).astype(jnp.bfloat16)
    gain_two_back, gate_back, up_back, down_back = (
        lax.all_gather(second_gain, "fsdp", axis=0, tiled=True),
        lax.all_gather(gate_weight, "fsdp", axis=0, tiled=True),
        lax.all_gather(up_weight, "fsdp", axis=0, tiled=True),
        lax.all_gather(down_weight, "fsdp", axis=0, tiled=True),
    )
    act_grad = times_transposed(cotangent, down_back)
    down_term = transposed_times(activated, cotangent)
    gate_grad = (act_grad * up_pre * sigmoid_gate * (1.0 + gate_pre * (1.0 - sigmoid_gate))).astype(
        jnp.bfloat16
    )
    up_grad = (act_grad * gate_pre * sigmoid_gate).astype(jnp.bfloat16)
    hidden_two_grad = times_transposed(gate_grad, gate_back) + times_transposed(up_grad, up_back)
    gate_term = transposed_times(hidden_two, gate_grad)
    up_term = transposed_times(hidden_two, up_grad)
    gain_two_term, middle_part = norm_back(
        hidden_two_grad, normed_two, gain_two_back.astype(jnp.float32), scale_two
    )
    middle_grad = cotangent.astype(jnp.float32) + middle_part
    gain_two_sum, gate_sum, up_sum, down_sum = (
        lax.psum_scatter(gain_two_term, "fsdp", scatter_dimension=0, tiled=True),
        lax.psum_scatter(gate_term, "fsdp", scatter_dimension=0, tiled=True),
        lax.psum_scatter(up_term, "fsdp", scatter_dimension=0, tiled=True),
        lax.psum_scatter(down_term, "fsdp", scatter_dimension=0, tiled=True),
    )
    gain_one_back, query_back, key_back, value_back, output_back = (
        lax.all_gather(first_gain, "fsdp", axis=0, tiled=True),
        lax.all_gather(query_weight, "fsdp", axis=0, tiled=True),
        lax.all_gather(key_weight, "fsdp", axis=0, tiled=True),
        lax.all_gather(value_weight, "fsdp", axis=0, tiled=True),
        lax.all_gather(output_weight, "fsdp", axis=0, tiled=True),
    )
    branch_low = middle_grad.astype(jnp.bfloat16)
    output_term = transposed_times(attended_low, branch_low)
    out_flat = times_transposed(branch_low, output_back).astype(jnp.bfloat16)
    out_low = out_flat.reshape(token_count, H, E)
    delta_rows = jnp.sum(out_low.astype(jnp.float32) * attended, axis=-1).T
    zero_rows = jnp.zeros((token_count, H, E), jnp.float32)
    gathered_keys, gathered_values = (
        lax.all_gather(key_rows, "fsdp", axis=0, tiled=True),
        lax.all_gather(mixed_values, "fsdp", axis=0, tiled=True),
    )
    length = gathered_keys.shape[0]
    size_now = block_rows(length)

    def back_step(query_acc, blocks):
        key_block, value_block, place_block = blocks
        key_shaped = key_block.reshape(-1, H, E)
        value_shaped = value_block.reshape(-1, H, E)
        prob_low, score_grad = grad_block(
            queries,
            key_shaped,
            value_shaped,
            own_limits,
            place_block,
            out_low,
            log_total,
            delta_rows,
        )
        query_acc = query_acc + jnp.einsum(
            "hqk,khe->qhe", score_grad, key_shaped, preferred_element_type=jnp.float32
        )
        key_part = jnp.einsum(
            "hqk,qhe->khe", score_grad, queries, preferred_element_type=jnp.float32
        ).reshape(-1, D)
        value_part = jnp.einsum(
            "hqk,qhe->khe", prob_low, out_low, preferred_element_type=jnp.float32
        ).reshape(-1, D)
        return (query_acc, jnp.concatenate([key_part, value_part], axis=1))

    query_acc, parts = lax.scan(
        back_step,
        zero_rows,
        (
            split_blocks(gathered_keys, size_now),
            split_blocks(gathered_values, size_now),
            split_blocks(all_places, size_now),
        ),
    )
    summed = lax.psum_scatter(parts.reshape(length, 2 * D), "fsdp", scatter_dimension=0, tiled=True)
    key_acc = summed[:, :D]
    value_acc = summed[:, D:]
    query_grad = (
        rope_undo(query_acc * E ** (-0.5), cosine, sine_table)
        .reshape(token_count, D)
        .astype(jnp.bfloat16)
    )
    key_grad = (
        rope_undo(key_acc.reshape(token_count, H, E) * E ** (-0.5), cosine, sine_table)
        .reshape(token_count, D)
        .astype(jnp.bfloat16)
    )
    first_values_grad = 0.5 * value_acc
    value_grad = first_values_grad.astype(jnp.bfloat16)
    hidden_one_grad = (
        times_transposed(query_grad, query_back)
        + times_transposed(key_grad, key_back)
        + times_transposed(value_grad, value_back)
    )
    query_term = transposed_times(hidden_one, query_grad)
    key_term = transposed_times(hidden_one, key_grad)
    value_term = transposed_times(hidden_one, value_grad)
    gain_one_term, input_part = norm_back(
        hidden_one_grad, normed_one, gain_one_back.astype(jnp.float32), scale_one
    )
    input_grad = middle_grad + input_part
    gain_one_sum, query_sum, key_sum, value_sum, output_sum = (
        lax.psum_scatter(gain_one_term, "fsdp", scatter_dimension=0, tiled=True),
        lax.psum_scatter(query_term, "fsdp", scatter_dimension=0, tiled=True),
        lax.psum_scatter(key_term, "fsdp", scatter_dimension=0, tiled=True),
        lax.psum_scatter(value_term, "fsdp", scatter_dimension=0, tiled=True),
        lax.psum_scatter(output_term, "fsdp", scatter_dimension=0, tiled=True),
    )
    totals = (
        lax.psum(gain_one_sum.astype(jnp.bfloat16), "rep").astype(jnp.float32),
        lax.psum(query_sum.astype(jnp.bfloat16), "rep").astype(jnp.float32),
        lax.psum(key_sum.astype(jnp.bfloat16), "rep").astype(jnp.float32),
        lax.psum(value_sum.astype(jnp.bfloat16), "rep").astype(jnp.float32),
        lax.psum(output_sum.astype(jnp.bfloat16), "rep").astype(jnp.float32),
        lax.psum(gain_two_sum.astype(jnp.bfloat16), "rep").astype(jnp.float32),
        lax.psum(gate_sum.astype(jnp.bfloat16), "rep").astype(jnp.float32),
        lax.psum(up_sum.astype(jnp.bfloat16), "rep").astype(jnp.float32),
        lax.psum(down_sum.astype(jnp.bfloat16), "rep").astype(jnp.float32),
    )
    return (
        layer_output,
        input_grad,
        first_values_grad,
        totals[0],
        totals[1],
        totals[2],
        totals[3],
        totals[4],
        totals[5],
        totals[6],
        totals[7],
        totals[8],
    )


MESH = pl.DeviceIdType.MESH
LOW = jnp.bfloat16
WIDE = jnp.float32
VM = pl.BlockSpec(memory_space=pltpu.VMEM)
FAR = pl.BlockSpec(memory_space=pl.ANY)
SM = pl.BlockSpec(memory_space=pltpu.SMEM)
DMA = pltpu.SemaphoreType.DMA
LIMIT = 63 * 1024 * 1024


def remote(src, dst, send_sem, recv_sem, rep, fsdp):
    return pltpu.make_async_remote_copy(
        src_ref=src,
        dst_ref=dst,
        send_sem=send_sem,
        recv_sem=recv_sem,
        device_id={"rep": rep, "fsdp": fsdp},
        device_id_type=MESH,
    )


def arrived(place, sem):
    pltpu.make_async_copy(place, place, sem).wait()


def greet(peers):
    barrier = pltpu.get_barrier_semaphore()
    for rep, fsdp in peers:
        pl.semaphore_signal(
            barrier, inc=1, device_id={"rep": rep, "fsdp": fsdp}, device_id_type=MESH
        )
    pl.semaphore_wait(barrier, len(peers))


def plane_place():
    rep, fsdp = lax.axis_index("rep"), lax.axis_index("fsdp")
    return rep, fsdp, fsdp // 2, fsdp % 2


def piece(index, size):
    return pl.ds(pl.multiple_of(index * size, size), size)


def matmul(left, right):
    return jnp.dot(left, right, preferred_element_type=WIDE)


class Rows:
    def __init__(self, own, full, keep, send, recv):
        self.own, self.full, self.keep, self.send, self.recv = own, full, keep, send, recv
        self.rep, self.fsdp, self.z, self.x = plane_place()
        self.side = 2 * self.z + 1 - self.x

    def push(self, src, block, sem, target):
        return remote(
            src, self.full.at[block], self.send.at[sem], self.recv.at[block], self.rep, target
        )

    def start(self):
        z, x = self.z, self.x

        @pl.when(z < 3)
        def up():
            self.push(self.own, self.fsdp, 0, 2 * (z + 1) + x).start()

        @pl.when(z > 0)
        def down():
            self.push(self.own, self.fsdp, 1, 2 * (z - 1) + x).start()

        self.push(self.own, self.fsdp, 2, self.side).start()
        pltpu.make_async_copy(self.own, self.full.at[self.fsdp], self.keep).start()

    def kept(self):
        pltpu.make_async_copy(self.own, self.full.at[self.fsdp], self.keep).wait()

    def line(self, k):
        high, odd = self.z // 2, self.z % 2
        first = 1 - (k + 1) // 2
        low_side = k + 1 - odd * first
        high_side = 2 - k + first * (1 - odd)
        return low_side + high * (high_side - low_side)

    def pass_on(self, k):
        z, x = self.z, self.x
        other = self.line(k)
        block = 2 * other + x
        place = self.full.at[block]
        arrived(place, self.recv.at[block])

        @pl.when((other < z) & (z < 3))
        def up():
            self.push(place, block, 3 + k, 2 * (z + 1) + x).start()

        @pl.when((other > z) & (z > 0))
        def down():
            self.push(place, block, 3 + k, 2 * (z - 1) + x).start()

        self.push(place, block, 6 + k, self.side).start()
        return block

    def across(self, other):
        block = 2 * other + 1 - self.x
        arrived(self.full.at[block], self.recv.at[block])
        return block

    def sent(self):
        z = self.z
        place = self.full.at[0]

        def done(sem):
            arrived(place, self.send.at[sem])

        pl.when(z < 3)(lambda: done(0))
        pl.when(z > 0)(lambda: done(1))
        done(2)
        for k in range(3):
            done(6 + k)

            @pl.when((z > 0) & (z < 3))
            def relayed():
                done(3 + k)


def rows_sems():
    return [DMA(()), DMA((9,)), DMA((8,))]


class Sums:
    def __init__(self, acc, side_in, summed, relay_in, send, side_recv, relay_recv):
        self.acc = acc
        self.side_in, self.summed, self.relay_in = side_in, summed, relay_in
        self.send, self.side_recv, self.relay_recv = send, side_recv, relay_recv
        self.rep, self.fsdp, self.z, self.x = plane_place()
        self.side = 2 * self.z + 1 - self.x

    def other(self, k):
        far = line_of(self.z, 2 - k % 3)
        return far + (k // 3) * (self.z - far)

    def give(self, k, ref):
        other = self.other(k)
        remote(
            ref, self.side_in.at[other], self.send.at[k], self.side_recv.at[other], self.rep, self.side
        ).start()

    def hop(self, k, other, slot, z):
        remote(
            self.summed.at[other],
            self.relay_in.at[slot],
            self.send.at[4 + k],
            self.relay_recv.at[slot],
            self.rep,
            2 * z + self.x,
        ).start()

    def forward(self, k, value):
        other, z = self.other(k), self.z
        arrived(self.side_in.at[other], self.side_recv.at[other])
        value = value + self.side_in[other].astype(WIDE)
        joins = ((other > z) & (z > 0)) | ((other < z) & (z < 3))

        @pl.when(joins)
        def join():
            arrived(self.relay_in.at[other], self.relay_recv.at[other])
            self.summed[other] = (value + self.relay_in[other].astype(WIDE)).astype(LOW)

        @pl.when(jnp.logical_not(joins))
        def begin():
            self.summed[other] = value.astype(LOW)

        @pl.when(other > z)
        def up():
            self.hop(k, other, other, z + 1)

        @pl.when(other < z)
        def down():
            ends = 1 - (z - other) // 2
            self.hop(k, other, other + ends * (4 - other), z - 1)

    def total(self, value):
        z = self.z
        arrived(self.side_in.at[z], self.side_recv.at[z])
        self.acc[...] = value + self.side_in[z].astype(WIDE)

        @pl.when(z > 0)
        def below():
            arrived(self.relay_in.at[z], self.relay_recv.at[z])
            self.acc[...] += self.relay_in[z].astype(WIDE)

        @pl.when(z < 3)
        def above():
            arrived(self.relay_in.at[4], self.relay_recv.at[4])
            self.acc[...] += self.relay_in[4].astype(WIDE)

        return self.acc[...]

    def sent(self):
        for k in range(7):
            arrived(self.side_in.at[0], self.send.at[k])


def line_of(z, k):
    high, odd = z // 2, z % 2
    first = 1 - (k + 1) // 2
    low_side = k + 1 - odd * first
    high_side = 2 - k + first * (1 - odd)
    return low_side + high * (high_side - low_side)


def sums_scratch():
    return [
        pltpu.VMEM((4, 128, D), LOW),
        pltpu.VMEM((4, 128, D), LOW),
        pltpu.VMEM((5, 128, D), LOW),
        DMA((7,)),
        DMA((4,)),
        DMA((5,)),
    ]


class Collect:
    def __init__(self, grads, out, pair_in, pair_sum, level_in, level_sum, landed, send, recv, cross_send, cross_recv):
        self.grads, self.out = grads, out
        self.pair_in, self.pair_sum = pair_in, pair_sum
        self.level_in, self.level_sum, self.landed = level_in, level_sum, landed
        self.send, self.recv, self.cross_send, self.cross_recv = send, recv, cross_send, cross_recv
        self.rep, self.fsdp, _, _ = plane_place()
        self.core, self.level = lax.rem(self.rep, 2), self.rep // 2
        self.partner = self.rep + 1 - 2 * self.core
        self.above = self.rep + 2 - 4 * self.level
        self.half = grads.shape[1] // 2
        self.fourth = self.half // 2

    def to(self, src, dst, index, rep):
        return remote(src, dst, self.send.at[index], self.recv.at[index], rep, self.fsdp)

    def start(self):
        src = self.grads.at[:, piece(1 - self.core, self.half)]
        self.to(src, self.pair_in, 0, self.partner).start()

    def fold_pair(self):
        arrived(self.pair_in, self.recv.at[0])
        mine = piece(self.core, self.half)

        def add(i, carry):
            self.pair_sum[i] = (
                self.grads[i, mine].astype(WIDE) + self.pair_in[i].astype(WIDE)
            ).astype(LOW)
            return carry

        lax.fori_loop(0, 8, add, 0)
        src = self.pair_sum.at[:, piece(1 - self.level, self.fourth)]
        self.to(src, self.level_in, 1, self.above).start()

    def fold_level(self):
        arrived(self.level_in, self.recv.at[1])
        mine = piece(self.level, self.fourth)

        def add(i, carry):
            self.level_sum[i] = (
                self.pair_sum[i, mine].astype(WIDE) + self.level_in[i].astype(WIDE)
            ).astype(LOW)
            return carry

        lax.fori_loop(0, 8, add, 0)
        for k in range(7):
            other = lax.rem(self.fsdp + k + 1, 8)
            remote(
                self.level_sum.at[other],
                self.landed.at[self.fsdp],
                self.cross_send.at[k],
                self.cross_recv.at[self.fsdp],
                self.rep,
                other,
            ).start()

    def quarter(self, core, level):
        return self.out.at[:, piece(2 * core + level, self.fourth)]

    def land(self):
        for k in range(7):
            other = lax.rem(self.fsdp + k + 1, 8)
            arrived(self.landed.at[other], self.cross_recv.at[other])
        self.landed[self.fsdp] = self.level_sum[self.fsdp]
        mine = piece(2 * self.core + self.level, self.fourth)
        place = self.quarter(self.core, self.level)
        self.to(self.landed, place, 2, self.above).start()
        self.to(self.landed, place, 3, self.partner).start()
        for i in range(8):
            self.out[i, mine] = self.landed[i]

    def relay(self):
        place = self.quarter(self.core, 1 - self.level)
        arrived(place, self.recv.at[2])
        self.to(place, place, 4, self.partner).start()

    def finish(self):
        arrived(self.quarter(1 - self.core, self.level), self.recv.at[3])
        arrived(self.quarter(1 - self.core, 1 - self.level), self.recv.at[4])
        arrived(self.pair_in, self.send.at[0])
        arrived(self.level_in, self.send.at[1])
        for k in range(3):
            arrived(self.landed, self.send.at[2 + k])
        for k in range(7):
            arrived(self.landed.at[0], self.cross_send.at[k])


def collect_scratch(high, wide):
    return [
        pltpu.VMEM((8, high // 2, wide), LOW),
        pltpu.VMEM((8, high // 2, wide), LOW),
        pltpu.VMEM((8, high // 4, wide), LOW),
        pltpu.VMEM((8, high // 4, wide), LOW),
        pltpu.VMEM((8, high // 4, wide), LOW),
        DMA((5,)),
        DMA((5,)),
        DMA((7,)),
        DMA((8,)),
    ]


class CollectRows:
    def __init__(self, rows, out, pair_in, pair_sum, level_in, send, recv):
        self.rows, self.out = rows, out
        self.pair_in, self.pair_sum, self.level_in = pair_in, pair_sum, level_in
        self.send, self.recv = send, recv
        self.rep, self.fsdp, _, _ = plane_place()
        self.core, self.level = lax.rem(self.rep, 2), self.rep // 2
        self.partner = self.rep + 1 - 2 * self.core
        self.above = self.rep + 2 - 4 * self.level
        self.half = rows.shape[1] // 2
        self.fourth = self.half // 2

    def to(self, src, dst, index, rep):
        return remote(src, dst, self.send.at[index], self.recv.at[index], rep, self.fsdp)

    def start(self):
        src = self.rows.at[:, piece(1 - self.core, self.half)]
        self.to(src, self.pair_in, 0, self.partner).start()

    def fold_pair(self):
        arrived(self.pair_in, self.recv.at[0])
        self.pair_sum[...] = (
            self.rows[:, piece(self.core, self.half)].astype(WIDE) + self.pair_in[...].astype(WIDE)
        ).astype(LOW)
        src = self.pair_sum.at[:, piece(1 - self.level, self.fourth)]
        self.to(src, self.level_in, 1, self.above).start()

    def quarter(self, core, level):
        return self.out.at[:, piece(2 * core + level, self.fourth)]

    def fold_level(self):
        arrived(self.level_in, self.recv.at[1])
        mine = piece(2 * self.core + self.level, self.fourth)
        self.out[:, mine] = (
            self.pair_sum[:, piece(self.level, self.fourth)].astype(WIDE)
            + self.level_in[...].astype(WIDE)
        ).astype(LOW)
        place = self.quarter(self.core, self.level)
        self.to(place, place, 2, self.above).start()
        self.to(place, place, 3, self.partner).start()

    def relay(self):
        place = self.quarter(self.core, 1 - self.level)
        arrived(place, self.recv.at[2])
        self.to(place, place, 4, self.partner).start()

    def finish(self):
        arrived(self.quarter(1 - self.core, self.level), self.recv.at[3])
        arrived(self.quarter(1 - self.core, 1 - self.level), self.recv.at[4])
        arrived(self.pair_in, self.send.at[0])
        for k in range(4):
            arrived(self.level_in, self.send.at[1 + k])


def collect_rows_scratch(tall):
    return [
        pltpu.VMEM((tall, D // 2), LOW),
        pltpu.VMEM((tall, D // 2), LOW),
        pltpu.VMEM((tall, D // 4), LOW),
        DMA((5,)),
        DMA((5,)),
    ]


def turn_rates():
    lane = lax.broadcasted_iota(jnp.int32, (1, 128), 1) % (E // 2)
    return jnp.exp(lane.astype(WIDE) * (-math.log(10000.0) / (E // 2)))


def turn_tables(marks, block, cosine_step, sine_step):
    lanes = piece(block, 128)
    cosines, sines = [], []
    for run in range(2):
        c = marks[3 + 2 * run : 4 + 2 * run, lanes]
        s = marks[4 + 2 * run : 5 + 2 * run, lanes]
        cosines.append(c * cosine_step[...] - s * sine_step[...])
        sines.append(s * cosine_step[...] + c * sine_step[...])
    lane = lax.broadcasted_iota(jnp.int32, (1, 128), 1)
    sign = jnp.where(lane % E < E // 2, -1.0, 1.0)
    return jnp.concatenate(cosines, axis=0), jnp.concatenate(sines, axis=0) * sign


def turn(array, cosine, sine):
    lane = lax.broadcasted_iota(jnp.int32, (1, 128), 1)
    swapped = jnp.where(lane % E < E // 2, pltpu.roll(array, 96, 1), pltpu.roll(array, 32, 1))
    return array * cosine + swapped * sine


def limit_column(marks, block, prefix_last):
    tile = marks[0:1, piece(block, 128)]
    lane = lax.broadcasted_iota(jnp.int32, (1, 128), 1)
    row = lax.broadcasted_iota(jnp.int32, (128, 1), 0)
    first = jnp.sum(jnp.where(lane == 0, tile, 0.0), axis=1, keepdims=True)
    second = jnp.sum(jnp.where(lane == 64, tile, 0.0), axis=1, keepdims=True)
    places = jnp.where(row < 64, first + row.astype(WIDE), second + (row - 64).astype(WIDE))
    return jnp.maximum(places, prefix_last)


def head_lanes(head):
    lane = lax.broadcasted_iota(jnp.int32, (1, 128), 1)
    return (lane // E) == head


def only(mask, array):
    return jnp.where(mask, array.astype(WIDE), 0.0).astype(LOW)


STEP = {"x": 1, "z": 2, "y": 4}
THIRDS = (("x", "y", "z", 0, 48), ("y", "z", "x", 48, 48), ("z", "x", "y", 96, 32))
SPARING = (("x", "z", "y", 0, 64), ("x", "z", "y", 64, 64))
LATER = (("z", "x", "y", 0, 64), ("z", "y", "x", 64, 64))


def flip(block, *dims):
    for dim in dims:
        block = block + STEP[dim] - 2 * STEP[dim] * ((block // STEP[dim]) % 2)
    return block


class Cube:
    def __init__(self):
        self.rep, self.fsdp, z, x = plane_place()
        self.core, self.y = lax.rem(self.rep, 2), self.rep // 2
        self.low, self.high = z % 2, z // 2
        self.own = x + 2 * self.low + 4 * self.y
        self.partner = self.rep + 1 - 2 * self.core
        self.far = self.fsdp + 4 - 8 * self.high
        self.lends = self.high == self.y
        self.near = {
            "x": (self.rep, self.fsdp + 1 - 2 * x),
            "z": (self.rep, self.fsdp + 2 - 4 * self.low),
            "y": (self.rep + 2 - 4 * self.y, self.fsdp),
        }

    def device(self, *dims):
        rep, fsdp = self.rep, self.fsdp
        for dim in dims:
            rep = rep + self.near[dim][0] - self.rep
            fsdp = fsdp + self.near[dim][1] - self.fsdp
        return rep, fsdp


class CubeRows:
    def __init__(self, cube, parts, own, full, keep, send, recv):
        self.cube, self.parts, self.own, self.full = cube, parts, own, full
        self.keep, self.send, self.recv = keep, send, recv

    def push(self, src, t, block, sem, dim):
        low, count = self.parts[t][3:]
        rep, fsdp = self.cube.near[dim]
        remote(
            src.at[pl.ds(low, count)],
            self.full.at[block, pl.ds(low, count)],
            self.send.at[t, sem],
            self.recv.at[t, block],
            rep,
            fsdp,
        ).start()

    def come(self, t, *dims):
        low, count = self.parts[t][3:]
        block = flip(self.cube.own, *dims)
        arrived(self.full.at[block, pl.ds(low, count)], self.recv.at[t, block])
        return block

    def start(self):
        own = self.cube.own
        for step in range(3):
            for t in range(len(self.parts)):
                self.push(self.own, t, own, (0, 1, 3)[step], self.parts[t][step])
        pltpu.make_async_copy(self.own, self.full.at[own], self.keep).start()

    def kept(self):
        pltpu.make_async_copy(self.own, self.full.at[self.cube.own], self.keep).wait()

    def relay_one(self):
        for t, (one, two, three, _, _) in enumerate(self.parts):
            block = self.come(t, one)
            self.push(self.full.at[block], t, block, 2, two)
            self.push(self.full.at[block], t, block, 4, three)
        for t, (one, two, three, _, _) in enumerate(self.parts):
            block = self.come(t, two)
            self.push(self.full.at[block], t, block, 5, three)

    def relay_two(self):
        for t, (one, two, three, _, _) in enumerate(self.parts):
            block = self.come(t, one, two)
            self.push(self.full.at[block], t, block, 6, three)

    def close_by(self):
        for t in range(len(self.parts)):
            self.come(t, self.parts[t][2])

    def further(self):
        for t, (one, two, three, _, _) in enumerate(self.parts):
            self.come(t, one, three)
            self.come(t, two, three)

    def last(self):
        for t, (one, two, three, _, _) in enumerate(self.parts):
            self.come(t, one, two, three)

    def sent(self):
        for t in range(len(self.parts)):
            low, count = self.parts[t][3:]
            for sem in range(7):
                arrived(self.full.at[0, pl.ds(low, count)], self.send.at[t, sem])


def cube_rows_sems():
    return [DMA(()), DMA((3, 7)), DMA((3, 8))]


class CubeSums:
    def __init__(self, cube, parts, part, total, in_one, out_two, in_two, out_three, in_three, send, recv):
        self.cube, self.parts, self.part, self.total = cube, parts, part, total
        self.in_one, self.out_two, self.in_two = in_one, out_two, in_two
        self.out_three, self.in_three = out_three, in_three
        self.send, self.recv = send, recv

    def slot(self, t, block):
        one, two = self.parts[t][:2]
        return (block // STEP[one]) % 2 + 2 * ((block // STEP[two]) % 2)

    def bit(self, t, block):
        return (block // STEP[self.parts[t][0]]) % 2

    def give(self, t, block):
        three, low, count = self.parts[t][2:]
        at = pl.ds(low, count)
        slot = self.slot(t, block)
        rep, fsdp = self.cube.near[three]
        remote(
            self.part.at[block, at],
            self.in_one.at[slot, at],
            self.send.at[t, slot],
            self.recv.at[t, slot],
            rep,
            fsdp,
        ).start()

    def give_all(self):
        for dims in ((), (0,), (1,), (0, 1)):
            for t in range(len(self.parts)):
                axes = [self.parts[t][2]] + [self.parts[t][d] for d in dims]
                self.give(t, flip(self.cube.own, *axes))

    def first(self, t, block):
        low, count = self.parts[t][3:]
        at = pl.ds(low, count)
        slot = self.slot(t, block)
        arrived(self.in_one.at[slot, at], self.recv.at[t, slot])
        return self.part[block, at].astype(WIDE) + self.in_one[slot, at].astype(WIDE)

    def second(self, t, block):
        low, count = self.parts[t][3:]
        at = pl.ds(low, count)
        value = self.first(t, block)
        bit = self.bit(t, block)
        arrived(self.in_two.at[bit, at], self.recv.at[t, 4 + bit])
        return value + self.in_two[bit, at].astype(WIDE)

    def fold_one(self):
        for t, (one, two, three, low, count) in enumerate(self.parts):
            at = pl.ds(low, count)
            rep, fsdp = self.cube.near[two]
            for v, dims in enumerate(((two, one), (two,))):
                block = flip(self.cube.own, *dims)
                self.out_two[v, at] = self.first(t, block).astype(LOW)
                bit = self.bit(t, block)
                remote(
                    self.out_two.at[v, at],
                    self.in_two.at[bit, at],
                    self.send.at[t, 4 + v],
                    self.recv.at[t, 4 + bit],
                    rep,
                    fsdp,
                ).start()

    def fold_two(self):
        for t, (one, two, three, low, count) in enumerate(self.parts):
            at = pl.ds(low, count)
            rep, fsdp = self.cube.near[one]
            self.out_three[at] = self.second(t, flip(self.cube.own, one)).astype(LOW)
            remote(
                self.out_three.at[at],
                self.in_three.at[at],
                self.send.at[t, 6],
                self.recv.at[t, 6],
                rep,
                fsdp,
            ).start()

    def finish(self):
        for t, (one, two, three, low, count) in enumerate(self.parts):
            at = pl.ds(low, count)
            value = self.second(t, self.cube.own)
            arrived(self.in_three.at[at], self.recv.at[t, 6])
            self.total[at] = value + self.in_three[at].astype(WIDE)

    def sent(self):
        for t in range(len(self.parts)):
            low, count = self.parts[t][3:]
            for sem in range(7):
                arrived(self.in_one.at[0, pl.ds(low, count)], self.send.at[t, sem])


def cube_sums_scratch():
    return [
        pltpu.VMEM((4, 128, D), LOW),
        pltpu.VMEM((2, 128, D), LOW),
        pltpu.VMEM((2, 128, D), LOW),
        pltpu.VMEM((128, D), LOW),
        pltpu.VMEM((128, D), LOW),
        DMA((3, 7)),
        DMA((3, 7)),
    ]


class CubeCollect:
    def __init__(self, cube, grads, out, pair_in, pair_sum, level_in, level_sum, send, recv, cross_send, cross_recv):
        self.cube, self.grads, self.out = cube, grads, out
        self.pair_in, self.pair_sum = pair_in, pair_sum
        self.level_in, self.level_sum = level_in, level_sum
        self.send, self.recv, self.cross_send, self.cross_recv = send, recv, cross_send, cross_recv
        self.half = grads.shape[1] // 2
        self.mine = piece(cube.core, self.half)
        self.theirs = piece(1 - cube.core, self.half)

    def start(self):
        cube = self.cube
        remote(
            self.grads.at[:, self.theirs],
            self.pair_in,
            self.send.at[0],
            self.recv.at[0],
            cube.partner,
            cube.fsdp,
        ).start()

    def fold_pair(self):
        cube = self.cube
        arrived(self.pair_in, self.recv.at[0])

        def add(i, carry):
            self.pair_sum[i] = (
                self.grads[i, self.mine].astype(WIDE) + self.pair_in[i].astype(WIDE)
            ).astype(LOW)
            return carry

        lax.fori_loop(0, 8, add, 0)
        remote(
            self.pair_sum.at[pl.ds(4 * (1 - cube.high), 4)],
            self.level_in,
            self.send.at[1],
            self.recv.at[1],
            cube.rep,
            cube.far,
        ).start()

    def fold_level(self):
        cube = self.cube
        arrived(self.level_in, self.recv.at[1])

        def add(i, carry):
            self.level_sum[i] = (
                self.pair_sum[4 * cube.high + i].astype(WIDE) + self.level_in[i].astype(WIDE)
            ).astype(LOW)
            return carry

        lax.fori_loop(0, 4, add, 0)
        for k, dims in enumerate(PEERS):
            rep, fsdp = cube.device(*dims)
            remote(
                self.level_sum.at[flip(cube.own, *dims) % 4],
                self.out.at[cube.own, self.mine],
                self.cross_send.at[k],
                self.cross_recv.at[cube.own],
                rep,
                fsdp,
            ).start()
        self.out[cube.own, self.mine] = self.level_sum[cube.own % 4]

    def land(self):
        cube = self.cube
        for dims in PEERS:
            block = flip(cube.own, *dims)
            arrived(self.out.at[block, self.mine], self.cross_recv.at[block])
        place = self.out.at[:, self.mine]
        remote(place, place, self.send.at[2], self.recv.at[2], cube.partner, cube.fsdp).start()

    def finish(self):
        arrived(self.out.at[:, self.theirs], self.recv.at[2])
        arrived(self.pair_in, self.send.at[0])
        arrived(self.level_in, self.send.at[1])
        arrived(self.pair_in, self.send.at[2])
        for k in range(7):
            arrived(self.level_in.at[0], self.cross_send.at[k])


PEERS = (("x",), ("z",), ("y",), ("x", "z"), ("x", "y"), ("z", "y"), ("x", "z", "y"))


def cube_collect_scratch(high, wide):
    return [
        pltpu.VMEM((8, high // 2, wide), LOW),
        pltpu.VMEM((8, high // 2, wide), LOW),
        pltpu.VMEM((4, high // 2, wide), LOW),
        pltpu.VMEM((4, high // 2, wide), LOW),
        DMA((3,)),
        DMA((3,)),
        DMA((7,)),
        DMA((8,)),
    ]


class CubeCollectRows:
    def __init__(self, cube, rows, out, pair_in, pair_sum, level_in, send, recv):
        self.cube, self.rows, self.out = cube, rows, out
        self.pair_in, self.pair_sum, self.level_in = pair_in, pair_sum, level_in
        self.send, self.recv = send, recv
        self.half = rows.shape[1] // 2
        self.mine = piece(cube.core, self.half)
        self.theirs = piece(1 - cube.core, self.half)

    def to(self, src, dst, index, rep, fsdp):
        remote(src, dst, self.send.at[index], self.recv.at[index], rep, fsdp).start()

    def start(self):
        cube = self.cube
        self.to(self.rows.at[:, self.theirs], self.pair_in, 0, cube.partner, cube.fsdp)

    def fold_pair(self):
        cube = self.cube
        arrived(self.pair_in, self.recv.at[0])
        self.pair_sum[...] = (
            self.rows[:, self.mine].astype(WIDE) + self.pair_in[...].astype(WIDE)
        ).astype(LOW)

        @pl.when(jnp.logical_not(cube.lends))
        def hand_over():
            self.to(self.pair_sum, self.level_in, 1, cube.rep, cube.far)

    def fold_level(self):
        cube = self.cube

        @pl.when(cube.lends)
        def close():
            arrived(self.level_in, self.recv.at[1])
            self.out[:, self.mine] = (
                self.pair_sum[...].astype(WIDE) + self.level_in[...].astype(WIDE)
            ).astype(LOW)
            place = self.out.at[:, self.mine]
            self.to(place, place, 2, *cube.near["y"])
            self.to(place, place, 3, cube.partner, cube.fsdp)

    def relay(self):
        cube = self.cube

        @pl.when(jnp.logical_not(cube.lends))
        def pass_on():
            place = self.out.at[:, self.mine]
            arrived(place, self.recv.at[2])
            self.to(place, place, 3, cube.partner, cube.fsdp)

    def finish(self):
        arrived(self.out.at[:, self.theirs], self.recv.at[3])
        arrived(self.pair_in, self.send.at[0])
        arrived(self.pair_in, self.send.at[3])
        pl.when(self.cube.lends)(lambda: arrived(self.pair_in, self.send.at[2]))
        pl.when(jnp.logical_not(self.cube.lends))(lambda: arrived(self.pair_in, self.send.at[1]))


def cube_collect_rows_scratch(tall):
    return [pltpu.VMEM((tall, D // 2), LOW)] * 3 + [DMA((4,)), DMA((4,))]


def low_shape(*shape):
    return jax.ShapeDtypeStruct(shape, LOW)


def wide_shape(*shape):
    return jax.ShapeDtypeStruct(shape, WIDE)


def scratch_of(hidden):
    low, wide = (lambda *shape: pltpu.VMEM(shape, LOW)), (lambda *shape: pltpu.VMEM(shape, WIDE))
    single = {
        "marks": wide(8, 1024),
        "small": wide(8, 128),
        "cosine_step": wide(64, 128),
        "sine_step": wide(64, 128),
        "rows_full": low(8, 128, 1024),
        "firsts_full": low(8, 128, 128),
        "weights": low(8, 128, 384),
        "packed": low(8, 128, 768),
        "packed_full": low(8, 128, 768),
        "grad_full": low(8, 128, 1024),
        "hidden_one": low(8, 128, 1024),
        "queries": low(1024, 128),
        "keys": low(1024, 128),
        "keys_turned": low(128, 1024),
        "values": low(1024, 128),
        "values_turned": low(128, 1024),
        "attended": low(1024, 128),
        "totals": wide(1024, 128),
        "middle": wide(128, 1024),
        "hidden_two": low(128, 1024),
        "hidden_full": low(8, 128, 1024),
        "active": low(1024, 384),
        "both": low(1024, 768),
        "down_pad": low(384, 1024),
        "part": low(8, 128, 1024),
        "out_part": low(8, 128, 1024),
        "total": wide(128, 1024),
        "middle_grad": wide(128, 1024),
        "branch": low(128, 1024),
        "gain_two_term": wide(1, 1024),
        "down_grad": low(hidden, 1024),
        "branch_full": low(8, 128, 1024),
        "out_grad": low(1024, 128),
        "query_grad": wide(1024, 128),
        "key_acc": wide(128, 1024),
        "value_acc": wide(128, 1024),
        "three": low(1024, 384),
        "qkv_grads": low(8, 128, 384),
        "qkv_out": low(8, 128, 384),
        "packed_out": low(8, 128, 768),
        "output_grad": low(128, 1024),
        "gain_own": wide(8, 8, 128),
        "gain_in": wide(8, 8, 128),
        "gain_part": wide(8, 128),
        "gain_rep": wide(4, 8, 128),
        "value_blocks": low(8, 128, 128),
        "gate_weight": low(128, 8 * hidden),
        "up_weight": low(128, 8 * hidden),
        "down": low(hidden, 1024),
        "layer_output": low(128, 1024),
        "input_grad": wide(128, 1024),
        "firsts_grad": low(128, 1024),
        "output_out": low(128, 1024),
        "two": low(2, 128, 8 * hidden),
        "down_out": low(hidden, 1024),
        "gains": wide(8, 128),
        "fetch": DMA((3,)),
        "finals": DMA((32,)),
        "keep": DMA((6,)),
        "w_send": DMA((3, 7)),
        "w_recv": DMA((3, 8)),
        "p_send": DMA((7,)),
        "p_recv": DMA((8,)),
        "s_send": DMA((7,)),
        "s_recv": DMA((8,)),
        "f_send": DMA((7,)),
        "f_recv": DMA((8,)),
        "m_send": DMA((7,)),
        "m_recv": DMA((8,)),
        "mp_send": DMA((7,)),
        "mp_recv": DMA((8,)),
        "g_send": DMA((7,)),
        "g_recv": DMA((8,)),
        "gr_send": DMA((3,)),
        "gr_recv": DMA((4,)),
        "v_send": DMA((7,)),
        "v_recv": DMA((8,)),
        "d_send": DMA((2,)),
        "d_recv": DMA((2,)),
    }
    groups = {
        "sums_one": sums_scratch(),
        "sums_two": cube_sums_scratch(),
        "sums_out": cube_sums_scratch(),
        "sums_three": sums_scratch(),
        "row_flow": rows_sems(),
        "grad_flow": cube_rows_sems(),
        "hidden_flow": cube_rows_sems(),
        "branch_flow": rows_sems(),
        "packed_flow": cube_collect_scratch(128, 768),
        "qkv_flow": collect_scratch(128, 384),
        "down_flow": cube_collect_rows_scratch(hidden),
        "output_flow": collect_rows_scratch(128),
    }
    return single, groups


def layer_kernel(
    hidden,
    rows,
    firsts,
    prefix,
    positions,
    first_gain,
    query_weight,
    key_weight,
    value_weight,
    output_weight,
    second_gain,
    gate_far,
    up_far,
    down_far,
    cotangent,
    layer_final,
    input_final,
    five_final,
    two_final,
    down_final,
    gains_final,
    *refs,
):
    single, groups = scratch_of(hidden)
    s = types.SimpleNamespace(**dict(zip(single, refs)))
    refs = list(refs[len(single) :])
    for name, shapes in groups.items():
        setattr(s, name, refs[: len(shapes)])
        refs = refs[len(shapes) :]
    rep, fsdp, z, x = plane_place()
    core, level = lax.rem(rep, 2), rep // 2
    partner = rep + 1 - 2 * core
    above = rep + 2 - 4 * level
    slant = 3 - rep
    others = [lax.rem(fsdp + k, 8) for k in range(1, 8)]
    gate_weight, up_weight, down = s.gate_weight, s.up_weight, s.down
    firsts_grad, output_out, down_out = s.firsts_grad, s.output_out, s.down_out
    fetched = []
    for k, (src, dst) in enumerate(((gate_far, gate_weight), (up_far, up_weight), (down_far, down))):
        fetched.append(pltpu.make_async_copy(src, dst, s.fetch.at[k]))
        fetched[k].start()
    saved = []

    def save(src, dst):
        copy = pltpu.make_async_copy(src, dst, s.finals.at[len(saved)])
        copy.start()
        saved.append(copy)

    cube = Cube()
    greet(
        [(rep, other) for other in others]
        + [(partner, fsdp), (above, fsdp), (slant, fsdp)]
        + [cube.device("y", "x"), cube.device("y", "z"), cube.device("y", "z", "x")]
    )
    mine = piece(core, 64)
    theirs = piece(1 - core, 64)
    started, kept = [], []
    row_flow = Rows(rows, s.rows_full, *s.row_flow)
    grad_flow = CubeRows(cube, SPARING, cotangent, s.grad_full, *s.grad_flow)
    hidden_flow = CubeRows(cube, THIRDS, s.hidden_two, s.hidden_full, *s.hidden_flow)
    branch_flow = Rows(s.branch, s.branch_full, *s.branch_flow)
    sums_one, sums_three = Sums(s.total, *s.sums_one), Sums(s.total, *s.sums_three)
    sums_two = CubeSums(cube, THIRDS, s.part, s.total, *s.sums_two)
    sums_out = CubeSums(cube, LATER, s.out_part, s.total, *s.sums_out)
    packed_flow = CubeCollect(cube, s.packed, s.packed_out, *s.packed_flow)
    qkv_flow = Collect(s.qkv_grads, s.qkv_out, *s.qkv_flow)
    down_flow = CubeCollectRows(cube, s.down_grad, down_out, *s.down_flow)
    output_flow = CollectRows(s.output_grad, output_out, *s.output_flow)

    def go(copy):
        copy.start()
        started.append(copy)

    def here(src, dst):
        copy = pltpu.make_async_copy(src, dst, s.keep.at[len(kept)])
        copy.start()
        kept.append(copy)

    sources = (query_weight, key_weight, value_weight)
    for k, other in enumerate(others):
        for i, source in enumerate(sources):
            go(
                remote(
                    source.at[mine, piece(other, 128)],
                    s.weights.at[fsdp, mine, pl.ds(128 * i, 128)],
                    s.w_send.at[i, k],
                    s.w_recv.at[i, fsdp],
                    rep,
                    other,
                )
            )
    row_flow.start()
    rates = turn_rates()
    place_row = positions[...].astype(WIDE)
    lane = lax.broadcasted_iota(jnp.int32, (1, 128), 1)
    s.small[0:1, :] = place_row
    s.small[1:2, :] = first_gain[...].astype(WIDE)
    s.small[2:3, :] = second_gain[...].astype(WIDE)
    for run in range(2):
        begin = jnp.sum(jnp.where(lane == 64 * run, place_row, 0.0), axis=1, keepdims=True)
        s.small[3 + 2 * run : 4 + 2 * run, :] = jnp.cos(begin * rates)
        s.small[4 + 2 * run : 5 + 2 * run, :] = jnp.sin(begin * rates)
    s.small[7:8, :] = jnp.zeros((1, 128), WIDE)
    for k, other in enumerate(others):
        go(
            remote(
                s.small, s.marks.at[:, piece(fsdp, 128)], s.s_send.at[k], s.s_recv.at[fsdp], rep, other
            )
        )
    for k, other in enumerate(others):
        go(
            remote(
                firsts.at[:, piece(other, 128)],
                s.firsts_full.at[fsdp],
                s.f_send.at[k],
                s.f_recv.at[fsdp],
                rep,
                other,
            )
        )
    grad_flow.start()
    for i, source in enumerate(sources):
        here(source.at[:, piece(fsdp, 128)], s.weights.at[fsdp, :, pl.ds(128 * i, 128)])
    here(s.small, s.marks.at[:, piece(fsdp, 128)])
    here(firsts.at[:, piece(fsdp, 128)], s.firsts_full.at[fsdp])
    angles = lax.broadcasted_iota(jnp.int32, (64, 128), 0).astype(WIDE) * rates
    s.cosine_step[...] = jnp.cos(angles)
    s.sine_step[...] = jnp.sin(angles)
    for copy in fetched:
        copy.wait()
    pad = jnp.zeros((128, 384 - hidden), LOW)
    for i in range(8):
        s.packed[i, :, 0:hidden] = gate_weight[:, hidden * i : hidden * (i + 1)]
        s.packed[i, :, hidden:384] = pad
        s.packed[i, :, 384 : 384 + hidden] = up_weight[:, hidden * i : hidden * (i + 1)]
        s.packed[i, :, 384 + hidden : 768] = pad
    here(s.packed.at[cube.own], s.packed_full.at[fsdp])

    row_flow.pass_on(0)
    for k, other in enumerate(others):
        for i in range(3):
            arrived(s.weights.at[other, mine, pl.ds(128 * i, 128)], s.w_recv.at[i, other])
        place = s.weights.at[other, mine]
        go(remote(place, place, s.p_send.at[k], s.p_recv.at[other], partner, fsdp))
    row_flow.pass_on(1)
    grad_flow.relay_one()
    for other in others:
        arrived(s.marks.at[:, piece(other, 128)], s.s_recv.at[other])
    for copy in kept:
        copy.wait()
    row_flow.kept()
    for other in others:
        arrived(s.weights.at[other, theirs], s.p_recv.at[other])
        arrived(s.firsts_full.at[other], s.f_recv.at[other])

    def project(block):
        entry = s.rows_full[block].astype(WIDE)
        scale = lax.rsqrt(jnp.mean(entry * entry, axis=-1, keepdims=True) + epsilon)
        low = (entry * scale * s.marks[1:2, :]).astype(LOW)
        s.hidden_one[block] = low
        pre = matmul(low, s.weights[...].reshape(8 * 128, 384))
        cosine, sine = turn_tables(s.marks, block, s.cosine_step, s.sine_step)
        at = piece(block, 128)
        s.queries[at, :] = turn(pre[:, :128], cosine, sine).astype(LOW)
        key = turn(pre[:, 128:256], cosine, sine)
        s.keys[at, :] = key.astype(LOW)
        s.keys_turned[:, at] = key.T.astype(LOW)
        value = 0.5 * pre[:, 256:] + 0.5 * s.firsts_full[block].astype(WIDE)
        s.values[at, :] = value.astype(LOW)
        s.values_turned[:, at] = value.T.astype(LOW)

    def project_column(k, carry):
        @pl.when(k == 2)
        def hand_on():
            row_flow.pass_on(2)

        project(2 * row_flow.line(k) + x)
        return carry

    def project_across(k, carry):
        project(row_flow.across(lax.rem(z + k, 4)))
        return carry

    project(fsdp)
    lax.fori_loop(0, 3, project_column, 0)
    grad_flow.relay_two()
    for k, other in enumerate(others):
        go(
            remote(
                s.packed.at[other % 4 + 4 * cube.y, mine],
                s.packed_full.at[fsdp, mine],
                s.m_send.at[k],
                s.m_recv.at[fsdp],
                rep,
                other,
            )
        )
    used = hidden // 2
    down_half = piece(core, used)
    s.down_pad[hidden:384, :] = jnp.zeros((384 - hidden, D), LOW)

    @pl.when(cube.lends)
    def lend():
        s.down_pad[0:hidden, :] = down[...]
        remote(
            down.at[down_half], s.down_pad.at[down_half], s.d_send.at[0], s.d_recv.at[0], rep, cube.far
        ).start()

    lax.fori_loop(0, 4, project_across, 0)
    prefix_last = (prefix[rep] - 1).astype(WIDE)
    masks = [head_lanes(head) for head in range(2)]

    def attend(block):
        at = piece(block, 128)
        query = s.queries[at, :]
        allowed = s.marks[0:1, :] <= limit_column(s.marks, block, prefix_last)
        result = total = None
        for head in range(2):
            scores = matmul(only(masks[head], query), s.keys_turned[...]) * E ** (-0.5)
            scores = jnp.where(allowed, scores, masked_score)
            top = jnp.max(scores, axis=-1, keepdims=True)
            weight = jnp.exp(scores - top)
            below = jnp.sum(weight, axis=-1, keepdims=True)
            probabilities = (weight * (1.0 / below)).astype(LOW)
            out = matmul(probabilities, s.values[...])
            log_total = jnp.broadcast_to(top + jnp.log(below), out.shape)
            result = out if head == 0 else jnp.where(masks[0], result, out)
            total = log_total if head == 0 else jnp.where(masks[0], total, log_total)
        s.totals[at, :] = total
        low = result.astype(LOW)
        s.attended[at, :] = low
        return matmul(low, output_weight[...])

    def attend_across(k, carry):
        other = sums_one.other(k)
        s.part[other] = attend(2 * other + 1 - x).astype(LOW)
        sums_one.give(k, s.part.at[other])

        return carry

    lax.fori_loop(0, 4, attend_across, 0)
    for k, other in enumerate(others):
        place = s.packed_full.at[other, mine]
        arrived(place, s.m_recv.at[other])
        go(remote(place, place, s.mp_send.at[k], s.mp_recv.at[other], partner, fsdp))

    @pl.when(jnp.logical_not(cube.lends))
    def borrow():
        place = s.down_pad.at[down_half]
        arrived(place, s.d_recv.at[0])
        remote(place, place, s.d_send.at[1], s.d_recv.at[1], partner, fsdp).start()

    def attend_column(k, carry):
        sums_one.forward(k, attend(2 * sums_one.other(k) + x))
        return carry

    lax.fori_loop(0, 3, attend_column, 0)
    total = rows[...].astype(WIDE) + sums_one.total(attend(fsdp))
    s.middle[...] = total
    scale = lax.rsqrt(jnp.mean(total * total, axis=-1, keepdims=True) + epsilon)
    s.hidden_two[...] = (total * scale * s.marks[2:3, :]).astype(LOW)

    hidden_flow.start()
    grad_flow.close_by()
    grad_flow.further()
    grad_flow.last()
    grad_flow.kept()

    @pl.when(jnp.logical_not(cube.lends))
    def borrowed():
        arrived(s.down_pad.at[piece(1 - core, used)], s.d_recv.at[1])

    for other in others:
        arrived(s.packed_full.at[other, theirs], s.mp_recv.at[other])

    def feed(block):
        at = piece(block, 128)
        packed = s.packed_full[...].reshape(8 * 128, 768)
        pre = matmul(s.hidden_full[block], packed)
        gate, up = pre[:, :384], pre[:, 384:]
        sigmoid = 1.0 / (1.0 + jnp.exp(-gate))
        swish = gate * sigmoid
        act = (swish * up).astype(LOW)
        s.active[at, :] = act
        act_grad = times_transposed(s.grad_full[block], s.down_pad[...])
        gate_grad = act_grad * up * sigmoid * (1.0 + gate * (1.0 - sigmoid))
        s.both[at, 0:384] = gate_grad.astype(LOW)
        s.both[at, 384:768] = (act_grad * swish).astype(LOW)
        s.part[block] = times_transposed(s.both[at, :], packed).astype(LOW)
        s.out_part[block] = matmul(act, s.down_pad[...]).astype(LOW)

    sums_one.sent()
    hidden_flow.kept()

    def feed_near(i, carry):
        @pl.when(i == 1)
        def first_wait():
            hidden_flow.relay_one()
            hidden_flow.close_by()

        pl.when(i == 2)(hidden_flow.relay_two)
        step = i + i // 3
        block = cube.own + step - 2 * step * (cube.own // (step + (3 - i) // 3) % 2)
        feed(block)
        for i_now, t in ((1, 1), (2, 0), (3, 2)):
            pl.when(i == i_now)(functools.partial(sums_two.give, t, block))
        return carry

    def feed_far(j, carry):
        pl.when(j == 0)(hidden_flow.further)
        pl.when(j == 3)(hidden_flow.last)
        i = (j + 1) % 4
        step = i + i // 3
        base = 7 - cube.own
        block = base + step - 2 * step * (base // (step + (3 - i) // 3) % 2)
        feed(block)
        for j_not, t in ((1, 0), (0, 1), (2, 2)):
            pl.when(j != j_not)(functools.partial(sums_two.give, t, block))
        return carry

    lax.fori_loop(0, 4, feed_near, 0)
    lax.fori_loop(0, 4, feed_far, 0)

    def feed_grads(i, carry):
        turned = s.hidden_full[:, :, piece(i, 128)].reshape(8 * 128, 128)
        s.packed[i] = transposed_times(turned, s.both[...]).astype(LOW)
        return carry

    for copy in started:
        copy.wait_send()

    lax.fori_loop(0, 3, feed_grads, 0)
    sums_two.fold_one()
    lax.fori_loop(3, 6, feed_grads, 0)
    sums_two.fold_two()
    lax.fori_loop(6, 8, feed_grads, 0)
    sums_two.finish()
    hidden_grad = s.total[...]
    entry = s.middle[...]
    scale = lax.rsqrt(jnp.mean(entry * entry, axis=-1, keepdims=True) + epsilon)
    normed = entry * scale
    normed_grad = hidden_grad * s.marks[2:3, :]
    back = scale * (normed_grad - normed * jnp.mean(normed_grad * normed, axis=-1, keepdims=True))
    grad = cotangent[...].astype(WIDE) + back
    s.branch[...] = grad.astype(LOW)
    branch_flow.start()
    s.middle_grad[...] = grad
    s.gain_two_term[...] = jnp.sum(hidden_grad * normed, axis=0, keepdims=True)

    def pull(block):
        s.out_grad[piece(block, 128), :] = times_transposed(
            s.branch_full[block], output_weight[...]
        ).astype(LOW)

    packed_flow.start()
    down_sum = transposed_times(s.active[...], s.grad_full[...].reshape(8 * 128, D))
    s.down_grad[...] = down_sum[0:hidden].astype(LOW)
    down_flow.start()
    branch_flow.kept()
    pull(fsdp)

    def pull_column(k, carry):
        pull(branch_flow.pass_on(k))
        return carry

    def pull_across(k, carry):
        pull(branch_flow.across(lax.rem(z + k, 4)))
        return carry

    lax.fori_loop(0, 3, pull_column, 0)
    lax.fori_loop(0, 4, pull_across, 0)
    sums_out.give_all()
    packed_flow.fold_pair()
    down_flow.fold_pair()
    s.output_grad[...] = transposed_times(
        s.attended[...], s.branch_full[...].reshape(8 * 128, D)
    ).astype(LOW)
    output_flow.start()
    s.key_acc[...] = jnp.zeros_like(s.key_acc)
    s.value_acc[...] = jnp.zeros_like(s.value_acc)

    def attend_back(block, carry):
        at = piece(block, 128)
        query, grad = s.queries[at, :], s.out_grad[at, :]
        log_total = s.totals[at, :]
        allowed = s.marks[0:1, :] <= limit_column(s.marks, block, prefix_last)
        result = None
        lows, score_grads, turned_queries, turned_grads = [], [], [], []
        for head in range(2):
            query_here, grad_here = only(masks[head], query), only(masks[head], grad)
            scores = matmul(query_here, s.keys_turned[...]) * E ** (-0.5)
            column = log_total[:, head * E : head * E + 1]
            probabilities = jnp.where(allowed, jnp.exp(scores - column), 0.0)
            prob_grad = matmul(grad_here, s.values_turned[...])
            delta = jnp.sum(probabilities * prob_grad, axis=-1, keepdims=True)
            score_grad = (probabilities * (prob_grad - delta)).astype(LOW)
            out = matmul(score_grad, s.keys[...])
            result = out if head == 0 else jnp.where(masks[0], result, out)
            lows.append(probabilities.astype(LOW))
            score_grads.append(score_grad)
            turned_queries.append(query_here.astype(WIDE).T)
            turned_grads.append(grad_here.astype(WIDE).T)
        s.query_grad[at, :] = result
        s.key_acc[...] += matmul(
            jnp.concatenate(turned_queries, axis=1).astype(LOW),
            jnp.concatenate(score_grads, axis=0),
        )
        s.value_acc[...] += matmul(
            jnp.concatenate(turned_grads, axis=1).astype(LOW), jnp.concatenate(lows, axis=0)
        )

        return carry

    lax.fori_loop(0, 8, attend_back, 0)

    def close(block):
        at = piece(block, 128)
        cosine, sine = turn_tables(s.marks, block, s.cosine_step, s.sine_step)
        s.three[at, 0:128] = turn(s.query_grad[at, :] * E ** (-0.5), cosine, -sine).astype(LOW)
        s.three[at, 128:256] = turn(s.key_acc[:, at].T * E ** (-0.5), cosine, -sine).astype(LOW)
        value_grad = (0.5 * s.value_acc[:, at].T).astype(LOW)
        s.three[at, 256:384] = value_grad
        s.value_blocks[block] = value_grad
        return times_transposed(s.three[at, :], s.weights[...].reshape(8 * 128, 384))

    def close_across(k, carry):
        other = sums_three.other(k)
        block = 2 * other + 1 - x
        s.part[block] = close(block).astype(LOW)
        sums_three.give(k, s.part.at[block])
        return carry

    def close_column(k, carry):
        block = 2 * sums_three.other(k) + x
        s.part[block] = close(block).astype(LOW)
        return carry

    sums_two.sent()
    lax.fori_loop(0, 4, close_across, 0)
    lax.fori_loop(0, 4, close_column, 0)
    for k, other in enumerate(others):
        remote(
            s.value_blocks.at[other],
            firsts_grad.at[:, piece(fsdp, 128)],
            s.v_send.at[k],
            s.v_recv.at[fsdp],
            rep,
            other,
        ).start()
    firsts_grad[:, piece(fsdp, 128)] = s.value_blocks[fsdp]

    def qkv_grads(i, carry):
        turned = s.hidden_one[:, :, piece(i, 128)].reshape(8 * 128, 128)
        s.qkv_grads[i] = transposed_times(turned, s.three[...]).astype(LOW)
        return carry

    lax.fori_loop(0, 8, qkv_grads, 0)
    qkv_flow.start()
    def onward(k):
        sums_three.forward(k, s.part[2 * sums_three.other(k) + x].astype(WIDE))

    onward(0)
    qkv_flow.fold_pair()
    sums_out.fold_one()
    packed_flow.fold_level()
    onward(1)
    output_flow.fold_pair()
    onward(2)
    down_flow.fold_level()
    qkv_flow.fold_level()
    sums_out.fold_two()
    output_flow.fold_level()
    packed_flow.land()
    down_flow.relay()
    packed_flow.finish()
    for i in range(8):
        wide = slice(hidden * i, hidden * (i + 1))
        s.two[0, :, wide] = s.packed_out[i, :, 0:hidden]
        s.two[1, :, wide] = s.packed_out[i, :, 384 : 384 + hidden]
    save(s.two, two_final)
    sums_out.finish()
    s.layer_output[...] = (s.middle[...] + s.total[...]).astype(LOW)
    save(s.layer_output, layer_final)
    output_flow.relay()
    qkv_flow.land()
    hidden_grad = sums_three.total(s.part[fsdp].astype(WIDE))
    entry = rows[...].astype(WIDE)
    scale = lax.rsqrt(jnp.mean(entry * entry, axis=-1, keepdims=True) + epsilon)
    normed = entry * scale
    normed_grad = hidden_grad * s.marks[1:2, :]
    gain_term = jnp.sum(hidden_grad * normed, axis=0, keepdims=True)
    for i in range(8):
        lanes = slice(128 * i, 128 * i + 128)
        s.gain_own[i, 0:1, :] = gain_term[:, lanes]
        s.gain_own[i, 1:2, :] = s.gain_two_term[:, lanes]
        s.gain_own[i, 2:8, :] = jnp.zeros((6, 128), WIDE)
    for k, other in enumerate(others):
        remote(
            s.gain_own.at[other], s.gain_in.at[fsdp], s.g_send.at[k], s.g_recv.at[fsdp], rep, other
        ).start()
    back = scale * (normed_grad - normed * jnp.mean(normed_grad * normed, axis=-1, keepdims=True))
    s.input_grad[...] = s.middle_grad[...] + back
    save(s.input_grad, input_final)
    qkv_flow.relay()
    s.gain_in[fsdp] = s.gain_own[fsdp]
    with jax.named_scope("gain_wait"):
        for other in others:
            arrived(s.gain_in.at[other], s.g_recv.at[other])
    s.gain_part[...] = jnp.sum(s.gain_in[...], axis=0)
    for k, target in enumerate((partner, above, slant)):
        remote(
            s.gain_part, s.gain_rep.at[rep], s.gr_send.at[k], s.gr_recv.at[rep], target, fsdp
        ).start()
    s.gain_rep[rep] = s.gain_part[...]
    with jax.named_scope("first_wait"):
        for k, other in enumerate(others):
            arrived(firsts_grad.at[:, piece(other, 128)], s.v_recv.at[other])
            arrived(s.value_blocks.at[0], s.v_send.at[k])
            arrived(s.gain_own.at[0], s.g_send.at[k])
    with jax.named_scope("rep_wait"):
        for k, source in enumerate((partner, above, slant)):
            arrived(s.gain_rep.at[source], s.gr_recv.at[source])
            arrived(s.gain_part, s.gr_send.at[k])
    s.gains[...] = jnp.sum(s.gain_rep[...], axis=0)
    save(s.gains, gains_final)
    save(firsts_grad, five_final.at[0])
    down_flow.finish()
    save(down_out, down_final)
    output_flow.finish()
    save(output_out, five_final.at[4])
    qkv_flow.finish()
    for i in range(8):
        for k in range(3):
            save(
                s.qkv_out.at[i, :, pl.ds(128 * k, 128)],
                five_final.at[1 + k, :, pl.ds(128 * i, 128)],
            )
    pl.when(cube.lends)(lambda: arrived(s.down_pad.at[down_half], s.d_send.at[0]))
    pl.when(jnp.logical_not(cube.lends))(lambda: arrived(s.down_pad.at[down_half], s.d_send.at[1]))
    for flow in (row_flow, grad_flow, hidden_flow, branch_flow):
        flow.sent()
    for sums in (sums_out, sums_three):
        sums.sent()
    for copy in saved:
        copy.wait()


def shards_plane(
    inputs,
    first_values,
    prefix,
    positions,
    first_gain,
    query_weight,
    key_weight,
    value_weight,
    output_weight,
    second_gain,
    gate_weight,
    up_weight,
    down_weight,
    cotangent,
):
    hidden = down_weight.shape[0]
    single, groups = scratch_of(hidden)
    outs = pl.pallas_call(
        functools.partial(layer_kernel, hidden),
        out_shape=[
            low_shape(128, D),
            wide_shape(128, D),
            low_shape(5, 128, D),
            low_shape(2, 128, 8 * hidden),
            low_shape(hidden, D),
            wide_shape(8, 128),
        ],
        in_specs=[VM, VM, SM] + [VM] * 7 + [FAR] * 3 + [VM],
        out_specs=[FAR] * 6,
        scratch_shapes=list(single.values()) + [shape for group in groups.values() for shape in group],
        compiler_params=pltpu.CompilerParams(
            collective_id=1, has_side_effects=True, vmem_limit_bytes=LIMIT
        ),
    )(
        inputs,
        first_values,
        prefix,
        positions[None],
        first_gain[None],
        query_weight,
        key_weight,
        value_weight,
        output_weight,
        second_gain[None],
        gate_weight,
        up_weight,
        down_weight,
        cotangent,
    )
    layer_output, input_grad, five, two, down, gains = outs
    firsts, query, key, value, output = [five[i].astype(WIDE) for i in range(5)]
    gate, up = [two[i].astype(WIDE) for i in range(2)]
    down = down.astype(WIDE)
    return (
        layer_output,
        input_grad,
        firsts,
        gains[0],
        query,
        key,
        value,
        output,
        gains[1],
        gate,
        up,
        down,
    )


def pick_body(mesh):
    if mesh.shape["fsdp"] == 8 and mesh.shape["rep"] == 4:
        return shards_plane
    return shards_general


def solution(mesh):
    placed = (
        P(("rep", "fsdp"), None),
        P(("rep", "fsdp"), None),
        P(),
        P(("rep", "fsdp")),
        P("fsdp"),
        P("fsdp", None),
        P("fsdp", None),
        P("fsdp", None),
        P("fsdp", None),
        P("fsdp"),
        P("fsdp", None),
        P("fsdp", None),
        P("fsdp", None),
        P(("rep", "fsdp"), None),
    )
    return jax.shard_map(
        pick_body(mesh),
        mesh=mesh,
        in_specs=placed,
        out_specs=(
            P(("rep", "fsdp"), None),
            P(("rep", "fsdp"), None),
            P(("rep", "fsdp"), None),
            P("fsdp"),
            P("fsdp", None),
            P("fsdp", None),
            P("fsdp", None),
            P("fsdp", None),
            P("fsdp"),
            P("fsdp", None),
            P("fsdp", None),
            P("fsdp", None),
        ),
        check_vma=False,
    )
```

```python
import functools
import math
import types

import jax
import jax.numpy as jnp
from jax import lax
from jax.experimental import pallas as pl
from jax.experimental.pallas import tpu as pltpu
from jax.sharding import PartitionSpec as P

D = 1024
H = 16
E = 64


epsilon = 1e-06
masked_score = -1e30


def rms_scale(values):
    return lax.rsqrt(jnp.mean(values * values, axis=-1, keepdims=True) + epsilon)


def rope_tables(places):
    half_width = E // 2
    frequency = jnp.exp(
        jnp.arange(half_width, dtype=jnp.float32) * (-math.log(10000.0) / half_width)
    )
    angles = places.astype(jnp.float32)[:, None] * frequency[None, :]
    return (jnp.cos(angles)[:, None, :], jnp.sin(angles)[:, None, :])


def rope_apply(shaped, cosine, sine_table):
    half_width = shaped.shape[-1] // 2
    first_half = shaped[..., :half_width]
    second_half = shaped[..., half_width:]
    return jnp.concatenate(
        [
            first_half * cosine - second_half * sine_table,
            second_half * cosine + first_half * sine_table,
        ],
        axis=-1,
    )


def rope_undo(shaped, cosine, sine_table):
    half_width = shaped.shape[-1] // 2
    first_half = shaped[..., :half_width]
    second_half = shaped[..., half_width:]
    return jnp.concatenate(
        [
            first_half * cosine + second_half * sine_table,
            second_half * cosine - first_half * sine_table,
        ],
        axis=-1,
    )


def times_transposed(left, right):
    return lax.dot_general(
        left, right, (((1,), (1,)), ((), ())), preferred_element_type=jnp.float32
    )


def transposed_times(left, right):
    return lax.dot_general(
        left, right, (((0,), (0,)), ((), ())), preferred_element_type=jnp.float32
    )


def block_rows(count):
    size_now = count
    while size_now > 1024 and size_now % 2 == 0:
        size_now = size_now // 2
    return size_now


def split_blocks(array, size_now):
    return array.reshape((array.shape[0] // size_now, size_now) + array.shape[1:])


def masked_scores(queries, key_rows, limits, key_places):
    scores = jnp.einsum(
        "qhe,khe->hqk", queries, key_rows, preferred_element_type=jnp.float32
    ) * E ** (-0.5)
    allowed = key_places[None, None, :] <= limits[None, :, None]
    return (scores, allowed)


def grad_block(queries, key_rows, value_rows, limits, key_places, out_low, log_total, delta_rows):
    scores, allowed = masked_scores(queries, key_rows, limits, key_places)
    probabilities = jnp.where(allowed, jnp.exp(scores - log_total[:, :, None]), 0.0)
    prob_grad = jnp.einsum("qhe,khe->hqk", out_low, value_rows, preferred_element_type=jnp.float32)
    score_grad = (probabilities * (prob_grad - delta_rows[:, :, None])).astype(jnp.bfloat16)
    return (probabilities.astype(jnp.bfloat16), score_grad)


def norm_back(hidden_grad, normed, gain_float, scale_rows):
    normed_grad = hidden_grad * gain_float
    gain_term = jnp.sum(hidden_grad * normed, axis=0)
    rows_grad = scale_rows * (
        normed_grad - normed * jnp.mean(normed_grad * normed, axis=-1, keepdims=True)
    )
    return (gain_term, rows_grad)


def shards_general(
    inputs,
    first_values,
    prefix,
    positions,
    first_gain,
    query_weight,
    key_weight,
    value_weight,
    output_weight,
    second_gain,
    gate_weight,
    up_weight,
    down_weight,
    cotangent,
):
    token_count = inputs.shape[0]
    gain_one, query_full, key_full, value_full, output_full = (
        lax.all_gather(first_gain, "fsdp", axis=0, tiled=True),
        lax.all_gather(query_weight, "fsdp", axis=0, tiled=True),
        lax.all_gather(key_weight, "fsdp", axis=0, tiled=True),
        lax.all_gather(value_weight, "fsdp", axis=0, tiled=True),
        lax.all_gather(output_weight, "fsdp", axis=0, tiled=True),
    )
    all_places = lax.all_gather(positions, "fsdp", axis=0, tiled=True)
    prefix_here = lax.dynamic_index_in_dim(prefix, lax.axis_index("rep"), keepdims=False)
    own_limits = jnp.maximum(positions, prefix_here - 1)
    cosine, sine_table = rope_tables(positions)
    rows_float = inputs.astype(jnp.float32)
    scale_one = rms_scale(rows_float)
    normed_one = rows_float * scale_one
    gain_one_float = gain_one.astype(jnp.float32)
    hidden_one = (normed_one * gain_one_float).astype(jnp.bfloat16)
    query_pre = jnp.dot(hidden_one, query_full, preferred_element_type=jnp.float32)
    key_pre = jnp.dot(hidden_one, key_full, preferred_element_type=jnp.float32)
    value_pre = jnp.dot(hidden_one, value_full, preferred_element_type=jnp.float32)
    queries = rope_apply(query_pre.reshape(token_count, H, E), cosine, sine_table).astype(
        jnp.bfloat16
    )
    key_rows = (
        rope_apply(key_pre.reshape(token_count, H, E), cosine, sine_table)
        .astype(jnp.bfloat16)
        .reshape(token_count, D)
    )
    mixed_values = (0.5 * value_pre + 0.5 * first_values.astype(jnp.float32)).astype(jnp.bfloat16)
    start_state = (
        jnp.full((H, token_count), masked_score, jnp.float32),
        jnp.zeros((H, token_count), jnp.float32),
        jnp.zeros((token_count, H, E), jnp.float32),
    )
    running = start_state
    key_piece = lax.all_gather(key_rows, "fsdp", axis=0, tiled=True)
    value_piece = lax.all_gather(mixed_values, "fsdp", axis=0, tiled=True)
    count = key_piece.shape[0]
    size_now = block_rows(count)

    def forward_step(state_now, blocks):
        row_max, row_sum, accum = state_now
        key_block, value_block, place_block = blocks
        scores, allowed = masked_scores(
            queries, key_block.reshape(-1, H, E), own_limits, place_block
        )
        new_max = jnp.maximum(row_max, jnp.max(jnp.where(allowed, scores, masked_score), axis=-1))
        rescale = jnp.exp(row_max - new_max)
        weights = jnp.where(allowed, jnp.exp(scores - new_max[:, :, None]), 0.0)
        row_sum = row_sum * rescale + jnp.sum(weights, axis=-1)
        accum = accum * rescale.T[:, :, None] + jnp.einsum(
            "hqk,khe->qhe",
            weights.astype(jnp.bfloat16),
            value_block.reshape(-1, H, E),
            preferred_element_type=jnp.float32,
        )
        return ((new_max, row_sum, accum), None)

    running, unused = lax.scan(
        forward_step,
        running,
        (
            split_blocks(key_piece, size_now),
            split_blocks(value_piece, size_now),
            split_blocks(all_places, size_now),
        ),
    )
    row_max, row_sum, accum = running
    log_total = row_max + jnp.log(row_sum)
    attended = accum / row_sum.T[:, :, None]
    attended_low = attended.reshape(token_count, D).astype(jnp.bfloat16)
    middle = rows_float + jnp.dot(attended_low, output_full, preferred_element_type=jnp.float32)
    mlp_forward = (
        lax.all_gather(second_gain, "fsdp", axis=0, tiled=True),
        lax.all_gather(gate_weight, "fsdp", axis=0, tiled=True),
        lax.all_gather(up_weight, "fsdp", axis=0, tiled=True),
        lax.all_gather(down_weight, "fsdp", axis=0, tiled=True),
    )
    gain_two, gate_full, up_full, down_full = mlp_forward
    scale_two = rms_scale(middle)
    normed_two = middle * scale_two
    hidden_two = (normed_two * gain_two.astype(jnp.float32)).astype(jnp.bfloat16)
    gate_pre = jnp.dot(hidden_two, gate_full, preferred_element_type=jnp.float32)
    up_pre = jnp.dot(hidden_two, up_full, preferred_element_type=jnp.float32)
    sigmoid_gate = jax.nn.sigmoid(gate_pre)
    activated = (gate_pre * sigmoid_gate * up_pre).astype(jnp.bfloat16)
    layer_output = (
        middle + jnp.dot(activated, down_full, preferred_element_type=jnp.float32)
    ).astype(jnp.bfloat16)
    gain_two_back, gate_back, up_back, down_back = (
        lax.all_gather(second_gain, "fsdp", axis=0, tiled=True),
        lax.all_gather(gate_weight, "fsdp", axis=0, tiled=True),
        lax.all_gather(up_weight, "fsdp", axis=0, tiled=True),
        lax.all_gather(down_weight, "fsdp", axis=0, tiled=True),
    )
    act_grad = times_transposed(cotangent, down_back)
    down_term = transposed_times(activated, cotangent)
    gate_grad = (act_grad * up_pre * sigmoid_gate * (1.0 + gate_pre * (1.0 - sigmoid_gate))).astype(
        jnp.bfloat16
    )
    up_grad = (act_grad * gate_pre * sigmoid_gate).astype(jnp.bfloat16)
    hidden_two_grad = times_transposed(gate_grad, gate_back) + times_transposed(up_grad, up_back)
    gate_term = transposed_times(hidden_two, gate_grad)
    up_term = transposed_times(hidden_two, up_grad)
    gain_two_term, middle_part = norm_back(
        hidden_two_grad, normed_two, gain_two_back.astype(jnp.float32), scale_two
    )
    middle_grad = cotangent.astype(jnp.float32) + middle_part
    gain_two_sum, gate_sum, up_sum, down_sum = (
        lax.psum_scatter(gain_two_term, "fsdp", scatter_dimension=0, tiled=True),
        lax.psum_scatter(gate_term, "fsdp", scatter_dimension=0, tiled=True),
        lax.psum_scatter(up_term, "fsdp", scatter_dimension=0, tiled=True),
        lax.psum_scatter(down_term, "fsdp", scatter_dimension=0, tiled=True),
    )
    gain_one_back, query_back, key_back, value_back, output_back = (
        lax.all_gather(first_gain, "fsdp", axis=0, tiled=True),
        lax.all_gather(query_weight, "fsdp", axis=0, tiled=True),
        lax.all_gather(key_weight, "fsdp", axis=0, tiled=True),
        lax.all_gather(value_weight, "fsdp", axis=0, tiled=True),
        lax.all_gather(output_weight, "fsdp", axis=0, tiled=True),
    )
    branch_low = middle_grad.astype(jnp.bfloat16)
    output_term = transposed_times(attended_low, branch_low)
    out_flat = times_transposed(branch_low, output_back).astype(jnp.bfloat16)
    out_low = out_flat.reshape(token_count, H, E)
    delta_rows = jnp.sum(out_low.astype(jnp.float32) * attended, axis=-1).T
    zero_rows = jnp.zeros((token_count, H, E), jnp.float32)
    gathered_keys, gathered_values = (
        lax.all_gather(key_rows, "fsdp", axis=0, tiled=True),
        lax.all_gather(mixed_values, "fsdp", axis=0, tiled=True),
    )
    length = gathered_keys.shape[0]
    size_now = block_rows(length)

    def back_step(query_acc, blocks):
        key_block, value_block, place_block = blocks
        key_shaped = key_block.reshape(-1, H, E)
        value_shaped = value_block.reshape(-1, H, E)
        prob_low, score_grad = grad_block(
            queries,
            key_shaped,
            value_shaped,
            own_limits,
            place_block,
            out_low,
            log_total,
            delta_rows,
        )
        query_acc = query_acc + jnp.einsum(
            "hqk,khe->qhe", score_grad, key_shaped, preferred_element_type=jnp.float32
        )
        key_part = jnp.einsum(
            "hqk,qhe->khe", score_grad, queries, preferred_element_type=jnp.float32
        ).reshape(-1, D)
        value_part = jnp.einsum(
            "hqk,qhe->khe", prob_low, out_low, preferred_element_type=jnp.float32
        ).reshape(-1, D)
        return (query_acc, jnp.concatenate([key_part, value_part], axis=1))

    query_acc, parts = lax.scan(
        back_step,
        zero_rows,
        (
            split_blocks(gathered_keys, size_now),
            split_blocks(gathered_values, size_now),
            split_blocks(all_places, size_now),
        ),
    )
    summed = lax.psum_scatter(parts.reshape(length, 2 * D), "fsdp", scatter_dimension=0, tiled=True)
    key_acc = summed[:, :D]
    value_acc = summed[:, D:]
    query_grad = (
        rope_undo(query_acc * E ** (-0.5), cosine, sine_table)
        .reshape(token_count, D)
        .astype(jnp.bfloat16)
    )
    key_grad = (
        rope_undo(key_acc.reshape(token_count, H, E) * E ** (-0.5), cosine, sine_table)
        .reshape(token_count, D)
        .astype(jnp.bfloat16)
    )
    first_values_grad = 0.5 * value_acc
    value_grad = first_values_grad.astype(jnp.bfloat16)
    hidden_one_grad = (
        times_transposed(query_grad, query_back)
        + times_transposed(key_grad, key_back)
        + times_transposed(value_grad, value_back)
    )
    query_term = transposed_times(hidden_one, query_grad)
    key_term = transposed_times(hidden_one, key_grad)
    value_term = transposed_times(hidden_one, value_grad)
    gain_one_term, input_part = norm_back(
        hidden_one_grad, normed_one, gain_one_back.astype(jnp.float32), scale_one
    )
    input_grad = middle_grad + input_part
    gain_one_sum, query_sum, key_sum, value_sum, output_sum = (
        lax.psum_scatter(gain_one_term, "fsdp", scatter_dimension=0, tiled=True),
        lax.psum_scatter(query_term, "fsdp", scatter_dimension=0, tiled=True),
        lax.psum_scatter(key_term, "fsdp", scatter_dimension=0, tiled=True),
        lax.psum_scatter(value_term, "fsdp", scatter_dimension=0, tiled=True),
        lax.psum_scatter(output_term, "fsdp", scatter_dimension=0, tiled=True),
    )
    totals = (
        lax.psum(gain_one_sum.astype(jnp.bfloat16), "rep").astype(jnp.float32),
        lax.psum(query_sum.astype(jnp.bfloat16), "rep").astype(jnp.float32),
        lax.psum(key_sum.astype(jnp.bfloat16), "rep").astype(jnp.float32),
        lax.psum(value_sum.astype(jnp.bfloat16), "rep").astype(jnp.float32),
        lax.psum(output_sum.astype(jnp.bfloat16), "rep").astype(jnp.float32),
        lax.psum(gain_two_sum.astype(jnp.bfloat16), "rep").astype(jnp.float32),
        lax.psum(gate_sum.astype(jnp.bfloat16), "rep").astype(jnp.float32),
        lax.psum(up_sum.astype(jnp.bfloat16), "rep").astype(jnp.float32),
        lax.psum(down_sum.astype(jnp.bfloat16), "rep").astype(jnp.float32),
    )
    return (
        layer_output,
        input_grad,
        first_values_grad,
        totals[0],
        totals[1],
        totals[2],
        totals[3],
        totals[4],
        totals[5],
        totals[6],
        totals[7],
        totals[8],
    )


MESH = pl.DeviceIdType.MESH
LOW = jnp.bfloat16
WIDE = jnp.float32
VM = pl.BlockSpec(memory_space=pltpu.VMEM)
FAR = pl.BlockSpec(memory_space=pl.ANY)
SM = pl.BlockSpec(memory_space=pltpu.SMEM)
DMA = pltpu.SemaphoreType.DMA
LIMIT = 63 * 1024 * 1024


def remote(src, dst, send_sem, recv_sem, rep, fsdp):
    return pltpu.make_async_remote_copy(
        src_ref=src,
        dst_ref=dst,
        send_sem=send_sem,
        recv_sem=recv_sem,
        device_id={"rep": rep, "fsdp": fsdp},
        device_id_type=MESH,
    )


def arrived(place, sem):
    pltpu.make_async_copy(place, place, sem).wait()


def greet(peers):
    barrier = pltpu.get_barrier_semaphore()
    for rep, fsdp in peers:
        pl.semaphore_signal(
            barrier, inc=1, device_id={"rep": rep, "fsdp": fsdp}, device_id_type=MESH
        )
    pl.semaphore_wait(barrier, len(peers))


def plane_place():
    rep, fsdp = lax.axis_index("rep"), lax.axis_index("fsdp")
    return rep, fsdp, fsdp // 2, fsdp % 2


def piece(index, size):
    return pl.ds(pl.multiple_of(index * size, size), size)


def matmul(left, right):
    return jnp.dot(left, right, preferred_element_type=WIDE)


class Rows:
    def __init__(self, own, full, keep, send, recv):
        self.own, self.full, self.keep, self.send, self.recv = own, full, keep, send, recv
        self.rep, self.fsdp, self.z, self.x = plane_place()
        self.side = 2 * self.z + 1 - self.x

    def push(self, src, block, sem, target):
        return remote(
            src, self.full.at[block], self.send.at[sem], self.recv.at[block], self.rep, target
        )

    def start(self):
        z, x = self.z, self.x

        @pl.when(z < 3)
        def up():
            self.push(self.own, self.fsdp, 0, 2 * (z + 1) + x).start()

        @pl.when(z > 0)
        def down():
            self.push(self.own, self.fsdp, 1, 2 * (z - 1) + x).start()

        self.push(self.own, self.fsdp, 2, self.side).start()
        pltpu.make_async_copy(self.own, self.full.at[self.fsdp], self.keep).start()

    def kept(self):
        pltpu.make_async_copy(self.own, self.full.at[self.fsdp], self.keep).wait()

    def line(self, k):
        high, odd = self.z // 2, self.z % 2
        first = 1 - (k + 1) // 2
        low_side = k + 1 - odd * first
        high_side = 2 - k + first * (1 - odd)
        return low_side + high * (high_side - low_side)

    def pass_on(self, k):
        z, x = self.z, self.x
        other = self.line(k)
        block = 2 * other + x
        place = self.full.at[block]
        arrived(place, self.recv.at[block])

        @pl.when((other < z) & (z < 3))
        def up():
            self.push(place, block, 3 + k, 2 * (z + 1) + x).start()

        @pl.when((other > z) & (z > 0))
        def down():
            self.push(place, block, 3 + k, 2 * (z - 1) + x).start()

        self.push(place, block, 6 + k, self.side).start()
        return block

    def across(self, other):
        block = 2 * other + 1 - self.x
        arrived(self.full.at[block], self.recv.at[block])
        return block

    def sent(self):
        z = self.z
        place = self.full.at[0]

        def done(sem):
            arrived(place, self.send.at[sem])

        pl.when(z < 3)(lambda: done(0))
        pl.when(z > 0)(lambda: done(1))
        done(2)
        for k in range(3):
            done(6 + k)

            @pl.when((z > 0) & (z < 3))
            def relayed():
                done(3 + k)


def rows_sems():
    return [DMA(()), DMA((9,)), DMA((8,))]


class Sums:
    def __init__(self, acc, side_in, summed, relay_in, send, side_recv, relay_recv):
        self.acc = acc
        self.side_in, self.summed, self.relay_in = side_in, summed, relay_in
        self.send, self.side_recv, self.relay_recv = send, side_recv, relay_recv
        self.rep, self.fsdp, self.z, self.x = plane_place()
        self.side = 2 * self.z + 1 - self.x

    def other(self, k):
        far = line_of(self.z, 2 - k % 3)
        return far + (k // 3) * (self.z - far)

    def give(self, k, ref):
        other = self.other(k)
        remote(
            ref, self.side_in.at[other], self.send.at[k], self.side_recv.at[other], self.rep, self.side
        ).start()

    def hop(self, k, other, slot, z):
        remote(
            self.summed.at[other],
            self.relay_in.at[slot],
            self.send.at[4 + k],
            self.relay_recv.at[slot],
            self.rep,
            2 * z + self.x,
        ).start()

    def forward(self, k, value):
        other, z = self.other(k), self.z
        arrived(self.side_in.at[other], self.side_recv.at[other])
        value = value + self.side_in[other].astype(WIDE)
        joins = ((other > z) & (z > 0)) | ((other < z) & (z < 3))

        @pl.when(joins)
        def join():
            arrived(self.relay_in.at[other], self.relay_recv.at[other])
            self.summed[other] = (value + self.relay_in[other].astype(WIDE)).astype(LOW)

        @pl.when(jnp.logical_not(joins))
        def begin():
            self.summed[other] = value.astype(LOW)

        @pl.when(other > z)
        def up():
            self.hop(k, other, other, z + 1)

        @pl.when(other < z)
        def down():
            ends = 1 - (z - other) // 2
            self.hop(k, other, other + ends * (4 - other), z - 1)

    def total(self, value):
        z = self.z
        arrived(self.side_in.at[z], self.side_recv.at[z])
        self.acc[...] = value + self.side_in[z].astype(WIDE)

        @pl.when(z > 0)
        def below():
            arrived(self.relay_in.at[z], self.relay_recv.at[z])
            self.acc[...] += self.relay_in[z].astype(WIDE)

        @pl.when(z < 3)
        def above():
            arrived(self.relay_in.at[4], self.relay_recv.at[4])
            self.acc[...] += self.relay_in[4].astype(WIDE)

        return self.acc[...]

    def sent(self):
        for k in range(7):
            arrived(self.side_in.at[0], self.send.at[k])


def line_of(z, k):
    high, odd = z // 2, z % 2
    first = 1 - (k + 1) // 2
    low_side = k + 1 - odd * first
    high_side = 2 - k + first * (1 - odd)
    return low_side + high * (high_side - low_side)


def sums_scratch():
    return [
        pltpu.VMEM((4, 128, D), LOW),
        pltpu.VMEM((4, 128, D), LOW),
        pltpu.VMEM((5, 128, D), LOW),
        DMA((7,)),
        DMA((4,)),
        DMA((5,)),
    ]


class Collect:
    def __init__(self, grads, out, pair_in, pair_sum, level_in, level_sum, landed, send, recv, cross_send, cross_recv):
        self.grads, self.out = grads, out
        self.pair_in, self.pair_sum = pair_in, pair_sum
        self.level_in, self.level_sum, self.landed = level_in, level_sum, landed
        self.send, self.recv, self.cross_send, self.cross_recv = send, recv, cross_send, cross_recv
        self.rep, self.fsdp, _, _ = plane_place()
        self.core, self.level = lax.rem(self.rep, 2), self.rep // 2
        self.partner = self.rep + 1 - 2 * self.core
        self.above = self.rep + 2 - 4 * self.level
        self.half = grads.shape[1] // 2
        self.fourth = self.half // 2

    def to(self, src, dst, index, rep):
        return remote(src, dst, self.send.at[index], self.recv.at[index], rep, self.fsdp)

    def start(self):
        src = self.grads.at[:, piece(1 - self.core, self.half)]
        self.to(src, self.pair_in, 0, self.partner).start()

    def fold_pair(self):
        arrived(self.pair_in, self.recv.at[0])
        mine = piece(self.core, self.half)

        def add(i, carry):
            self.pair_sum[i] = (
                self.grads[i, mine].astype(WIDE) + self.pair_in[i].astype(WIDE)
            ).astype(LOW)
            return carry

        lax.fori_loop(0, 8, add, 0)
        src = self.pair_sum.at[:, piece(1 - self.level, self.fourth)]
        self.to(src, self.level_in, 1, self.above).start()

    def fold_level(self):
        arrived(self.level_in, self.recv.at[1])
        mine = piece(self.level, self.fourth)

        def add(i, carry):
            self.level_sum[i] = (
                self.pair_sum[i, mine].astype(WIDE) + self.level_in[i].astype(WIDE)
            ).astype(LOW)
            return carry

        lax.fori_loop(0, 8, add, 0)
        for k in range(7):
            other = lax.rem(self.fsdp + k + 1, 8)
            remote(
                self.level_sum.at[other],
                self.landed.at[self.fsdp],
                self.cross_send.at[k],
                self.cross_recv.at[self.fsdp],
                self.rep,
                other,
            ).start()

    def quarter(self, core, level):
        return self.out.at[:, piece(2 * core + level, self.fourth)]

    def land(self):
        for k in range(7):
            other = lax.rem(self.fsdp + k + 1, 8)
            arrived(self.landed.at[other], self.cross_recv.at[other])
        self.landed[self.fsdp] = self.level_sum[self.fsdp]
        mine = piece(2 * self.core + self.level, self.fourth)
        place = self.quarter(self.core, self.level)
        self.to(self.landed, place, 2, self.above).start()
        self.to(self.landed, place, 3, self.partner).start()
        for i in range(8):
            self.out[i, mine] = self.landed[i]

    def relay(self):
        place = self.quarter(self.core, 1 - self.level)
        arrived(place, self.recv.at[2])
        self.to(place, place, 4, self.partner).start()

    def finish(self):
        arrived(self.quarter(1 - self.core, self.level), self.recv.at[3])
        arrived(self.quarter(1 - self.core, 1 - self.level), self.recv.at[4])
        arrived(self.pair_in, self.send.at[0])
        arrived(self.level_in, self.send.at[1])
        for k in range(3):
            arrived(self.landed, self.send.at[2 + k])
        for k in range(7):
            arrived(self.landed.at[0], self.cross_send.at[k])


def collect_scratch(high, wide):
    return [
        pltpu.VMEM((8, high // 2, wide), LOW),
        pltpu.VMEM((8, high // 2, wide), LOW),
        pltpu.VMEM((8, high // 4, wide), LOW),
        pltpu.VMEM((8, high // 4, wide), LOW),
        pltpu.VMEM((8, high // 4, wide), LOW),
        DMA((5,)),
        DMA((5,)),
        DMA((7,)),
        DMA((8,)),
    ]


class CollectRows:
    def __init__(self, rows, out, pair_in, pair_sum, level_in, send, recv):
        self.rows, self.out = rows, out
        self.pair_in, self.pair_sum, self.level_in = pair_in, pair_sum, level_in
        self.send, self.recv = send, recv
        self.rep, self.fsdp, _, _ = plane_place()
        self.core, self.level = lax.rem(self.rep, 2), self.rep // 2
        self.partner = self.rep + 1 - 2 * self.core
        self.above = self.rep + 2 - 4 * self.level
        self.half = rows.shape[1] // 2
        self.fourth = self.half // 2

    def to(self, src, dst, index, rep):
        return remote(src, dst, self.send.at[index], self.recv.at[index], rep, self.fsdp)

    def start(self):
        src = self.rows.at[:, piece(1 - self.core, self.half)]
        self.to(src, self.pair_in, 0, self.partner).start()

    def fold_pair(self):
        arrived(self.pair_in, self.recv.at[0])
        self.pair_sum[...] = (
            self.rows[:, piece(self.core, self.half)].astype(WIDE) + self.pair_in[...].astype(WIDE)
        ).astype(LOW)
        src = self.pair_sum.at[:, piece(1 - self.level, self.fourth)]
        self.to(src, self.level_in, 1, self.above).start()

    def quarter(self, core, level):
        return self.out.at[:, piece(2 * core + level, self.fourth)]

    def fold_level(self):
        arrived(self.level_in, self.recv.at[1])
        mine = piece(2 * self.core + self.level, self.fourth)
        self.out[:, mine] = (
            self.pair_sum[:, piece(self.level, self.fourth)].astype(WIDE)
            + self.level_in[...].astype(WIDE)
        ).astype(LOW)
        place = self.quarter(self.core, self.level)
        self.to(place, place, 2, self.above).start()
        self.to(place, place, 3, self.partner).start()

    def relay(self):
        place = self.quarter(self.core, 1 - self.level)
        arrived(place, self.recv.at[2])
        self.to(place, place, 4, self.partner).start()

    def finish(self):
        arrived(self.quarter(1 - self.core, self.level), self.recv.at[3])
        arrived(self.quarter(1 - self.core, 1 - self.level), self.recv.at[4])
        arrived(self.pair_in, self.send.at[0])
        for k in range(4):
            arrived(self.level_in, self.send.at[1 + k])


def collect_rows_scratch(tall):
    return [
        pltpu.VMEM((tall, D // 2), LOW),
        pltpu.VMEM((tall, D // 2), LOW),
        pltpu.VMEM((tall, D // 4), LOW),
        DMA((5,)),
        DMA((5,)),
    ]


def turn_rates():
    lane = lax.broadcasted_iota(jnp.int32, (1, 128), 1) % (E // 2)
    return jnp.exp(lane.astype(WIDE) * (-math.log(10000.0) / (E // 2)))


def turn_tables(marks, block, cosine_step, sine_step):
    lanes = piece(block, 128)
    cosines, sines = [], []
    for run in range(2):
        c = marks[3 + 2 * run : 4 + 2 * run, lanes]
        s = marks[4 + 2 * run : 5 + 2 * run, lanes]
        cosines.append(c * cosine_step[...] - s * sine_step[...])
        sines.append(s * cosine_step[...] + c * sine_step[...])
    lane = lax.broadcasted_iota(jnp.int32, (1, 128), 1)
    sign = jnp.where(lane % E < E // 2, -1.0, 1.0)
    return jnp.concatenate(cosines, axis=0), jnp.concatenate(sines, axis=0) * sign


def turn(array, cosine, sine):
    lane = lax.broadcasted_iota(jnp.int32, (1, 128), 1)
    swapped = jnp.where(lane % E < E // 2, pltpu.roll(array, 96, 1), pltpu.roll(array, 32, 1))
    return array * cosine + swapped * sine


def limit_column(marks, block, prefix_last):
    tile = marks[0:1, piece(block, 128)]
    lane = lax.broadcasted_iota(jnp.int32, (1, 128), 1)
    row = lax.broadcasted_iota(jnp.int32, (128, 1), 0)
    first = jnp.sum(jnp.where(lane == 0, tile, 0.0), axis=1, keepdims=True)
    second = jnp.sum(jnp.where(lane == 64, tile, 0.0), axis=1, keepdims=True)
    places = jnp.where(row < 64, first + row.astype(WIDE), second + (row - 64).astype(WIDE))
    return jnp.maximum(places, prefix_last)


def head_lanes(head):
    lane = lax.broadcasted_iota(jnp.int32, (1, 128), 1)
    return (lane // E) == head


def only(mask, array):
    return jnp.where(mask, array.astype(WIDE), 0.0).astype(LOW)


STEP = {"x": 1, "z": 2, "y": 4}
THIRDS = (("x", "y", "z", 0, 48), ("y", "z", "x", 48, 48), ("z", "x", "y", 96, 32))
SPARING = (("x", "z", "y", 0, 64), ("x", "z", "y", 64, 64))
LATER = (("z", "x", "y", 0, 64), ("z", "y", "x", 64, 64))


def flip(block, *dims):
    for dim in dims:
        block = block + STEP[dim] - 2 * STEP[dim] * ((block // STEP[dim]) % 2)
    return block


class Cube:
    def __init__(self):
        self.rep, self.fsdp, z, x = plane_place()
        self.core, self.y = lax.rem(self.rep, 2), self.rep // 2
        self.low, self.high = z % 2, z // 2
        self.own = x + 2 * self.low + 4 * self.y
        self.partner = self.rep + 1 - 2 * self.core
        self.far = self.fsdp + 4 - 8 * self.high
        self.lends = self.high == self.y
        self.near = {
            "x": (self.rep, self.fsdp + 1 - 2 * x),
            "z": (self.rep, self.fsdp + 2 - 4 * self.low),
            "y": (self.rep + 2 - 4 * self.y, self.fsdp),
        }

    def device(self, *dims):
        rep, fsdp = self.rep, self.fsdp
        for dim in dims:
            rep = rep + self.near[dim][0] - self.rep
            fsdp = fsdp + self.near[dim][1] - self.fsdp
        return rep, fsdp


class CubeRows:
    def __init__(self, cube, parts, own, full, keep, send, recv):
        self.cube, self.parts, self.own, self.full = cube, parts, own, full
        self.keep, self.send, self.recv = keep, send, recv

    def push(self, src, t, block, sem, dim):
        low, count = self.parts[t][3:]
        rep, fsdp = self.cube.near[dim]
        remote(
            src.at[pl.ds(low, count)],
            self.full.at[block, pl.ds(low, count)],
            self.send.at[t, sem],
            self.recv.at[t, block],
            rep,
            fsdp,
        ).start()

    def come(self, t, *dims):
        low, count = self.parts[t][3:]
        block = flip(self.cube.own, *dims)
        arrived(self.full.at[block, pl.ds(low, count)], self.recv.at[t, block])
        return block

    def start(self):
        own = self.cube.own
        for step in range(3):
            for t in range(len(self.parts)):
                self.push(self.own, t, own, (0, 1, 3)[step], self.parts[t][step])
        pltpu.make_async_copy(self.own, self.full.at[own], self.keep).start()

    def kept(self):
        pltpu.make_async_copy(self.own, self.full.at[self.cube.own], self.keep).wait()

    def relay_one(self):
        for t, (one, two, three, _, _) in enumerate(self.parts):
            block = self.come(t, one)
            self.push(self.full.at[block], t, block, 2, two)
            self.push(self.full.at[block], t, block, 4, three)
        for t, (one, two, three, _, _) in enumerate(self.parts):
            block = self.come(t, two)
            self.push(self.full.at[block], t, block, 5, three)

    def relay_two(self):
        for t, (one, two, three, _, _) in enumerate(self.parts):
            block = self.come(t, one, two)
            self.push(self.full.at[block], t, block, 6, three)

    def close_by(self):
        for t in range(len(self.parts)):
            self.come(t, self.parts[t][2])

    def further(self):
        for t, (one, two, three, _, _) in enumerate(self.parts):
            self.come(t, one, three)
            self.come(t, two, three)

    def last(self):
        for t, (one, two, three, _, _) in enumerate(self.parts):
            self.come(t, one, two, three)

    def sent(self):
        for t in range(len(self.parts)):
            low, count = self.parts[t][3:]
            for sem in range(7):
                arrived(self.full.at[0, pl.ds(low, count)], self.send.at[t, sem])


def cube_rows_sems():
    return [DMA(()), DMA((3, 7)), DMA((3, 8))]


class CubeSums:
    def __init__(self, cube, parts, part, total, in_one, out_two, in_two, out_three, in_three, send, recv):
        self.cube, self.parts, self.part, self.total = cube, parts, part, total
        self.in_one, self.out_two, self.in_two = in_one, out_two, in_two
        self.out_three, self.in_three = out_three, in_three
        self.send, self.recv = send, recv

    def slot(self, t, block):
        one, two = self.parts[t][:2]
        return (block // STEP[one]) % 2 + 2 * ((block // STEP[two]) % 2)

    def bit(self, t, block):
        return (block // STEP[self.parts[t][0]]) % 2

    def give(self, t, block):
        three, low, count = self.parts[t][2:]
        at = pl.ds(low, count)
        slot = self.slot(t, block)
        rep, fsdp = self.cube.near[three]
        remote(
            self.part.at[block, at],
            self.in_one.at[slot, at],
            self.send.at[t, slot],
            self.recv.at[t, slot],
            rep,
            fsdp,
        ).start()

    def give_all(self):
        for dims in ((), (0,), (1,), (0, 1)):
            for t in range(len(self.parts)):
                axes = [self.parts[t][2]] + [self.parts[t][d] for d in dims]
                self.give(t, flip(self.cube.own, *axes))

    def first(self, t, block):
        low, count = self.parts[t][3:]
        at = pl.ds(low, count)
        slot = self.slot(t, block)
        arrived(self.in_one.at[slot, at], self.recv.at[t, slot])
        return self.part[block, at].astype(WIDE) + self.in_one[slot, at].astype(WIDE)

    def second(self, t, block):
        low, count = self.parts[t][3:]
        at = pl.ds(low, count)
        value = self.first(t, block)
        bit = self.bit(t, block)
        arrived(self.in_two.at[bit, at], self.recv.at[t, 4 + bit])
        return value + self.in_two[bit, at].astype(WIDE)

    def fold_one(self):
        for t, (one, two, three, low, count) in enumerate(self.parts):
            at = pl.ds(low, count)
            rep, fsdp = self.cube.near[two]
            for v, dims in enumerate(((two, one), (two,))):
                block = flip(self.cube.own, *dims)
                self.out_two[v, at] = self.first(t, block).astype(LOW)
                bit = self.bit(t, block)
                remote(
                    self.out_two.at[v, at],
                    self.in_two.at[bit, at],
                    self.send.at[t, 4 + v],
                    self.recv.at[t, 4 + bit],
                    rep,
                    fsdp,
                ).start()

    def fold_two(self):
        for t, (one, two, three, low, count) in enumerate(self.parts):
            at = pl.ds(low, count)
            rep, fsdp = self.cube.near[one]
            self.out_three[at] = self.second(t, flip(self.cube.own, one)).astype(LOW)
            remote(
                self.out_three.at[at],
                self.in_three.at[at],
                self.send.at[t, 6],
                self.recv.at[t, 6],
                rep,
                fsdp,
            ).start()

    def finish(self):
        for t, (one, two, three, low, count) in enumerate(self.parts):
            at = pl.ds(low, count)
            value = self.second(t, self.cube.own)
            arrived(self.in_three.at[at], self.recv.at[t, 6])
            self.total[at] = value + self.in_three[at].astype(WIDE)

    def sent(self):
        for t in range(len(self.parts)):
            low, count = self.parts[t][3:]
            for sem in range(7):
                arrived(self.in_one.at[0, pl.ds(low, count)], self.send.at[t, sem])


def cube_sums_scratch():
    return [
        pltpu.VMEM((4, 128, D), LOW),
        pltpu.VMEM((2, 128, D), LOW),
        pltpu.VMEM((2, 128, D), LOW),
        pltpu.VMEM((128, D), LOW),
        pltpu.VMEM((128, D), LOW),
        DMA((3, 7)),
        DMA((3, 7)),
    ]


class CubeCollect:
    def __init__(self, cube, grads, out, pair_in, pair_sum, level_in, level_sum, send, recv, cross_send, cross_recv):
        self.cube, self.grads, self.out = cube, grads, out
        self.pair_in, self.pair_sum = pair_in, pair_sum
        self.level_in, self.level_sum = level_in, level_sum
        self.send, self.recv, self.cross_send, self.cross_recv = send, recv, cross_send, cross_recv
        self.half = grads.shape[1] // 2
        self.mine = piece(cube.core, self.half)
        self.theirs = piece(1 - cube.core, self.half)

    def start(self):
        cube = self.cube
        remote(
            self.grads.at[:, self.theirs],
            self.pair_in,
            self.send.at[0],
            self.recv.at[0],
            cube.partner,
            cube.fsdp,
        ).start()

    def fold_pair(self):
        cube = self.cube
        arrived(self.pair_in, self.recv.at[0])

        def add(i, carry):
            self.pair_sum[i] = (
                self.grads[i, self.mine].astype(WIDE) + self.pair_in[i].astype(WIDE)
            ).astype(LOW)
            return carry

        lax.fori_loop(0, 8, add, 0)
        remote(
            self.pair_sum.at[pl.ds(4 * (1 - cube.high), 4)],
            self.level_in,
            self.send.at[1],
            self.recv.at[1],
            cube.rep,
            cube.far,
        ).start()

    def fold_level(self):
        cube = self.cube
        arrived(self.level_in, self.recv.at[1])

        def add(i, carry):
            self.level_sum[i] = (
                self.pair_sum[4 * cube.high + i].astype(WIDE) + self.level_in[i].astype(WIDE)
            ).astype(LOW)
            return carry

        lax.fori_loop(0, 4, add, 0)
        for k, dims in enumerate(PEERS):
            rep, fsdp = cube.device(*dims)
            remote(
                self.level_sum.at[flip(cube.own, *dims) % 4],
                self.out.at[cube.own, self.mine],
                self.cross_send.at[k],
                self.cross_recv.at[cube.own],
                rep,
                fsdp,
            ).start()
        self.out[cube.own, self.mine] = self.level_sum[cube.own % 4]

    def land(self):
        cube = self.cube
        for dims in PEERS:
            block = flip(cube.own, *dims)
            arrived(self.out.at[block, self.mine], self.cross_recv.at[block])
        place = self.out.at[:, self.mine]
        remote(place, place, self.send.at[2], self.recv.at[2], cube.partner, cube.fsdp).start()

    def finish(self):
        arrived(self.out.at[:, self.theirs], self.recv.at[2])
        arrived(self.pair_in, self.send.at[0])
        arrived(self.level_in, self.send.at[1])
        arrived(self.pair_in, self.send.at[2])
        for k in range(7):
            arrived(self.level_in.at[0], self.cross_send.at[k])


PEERS = (("x",), ("z",), ("y",), ("x", "z"), ("x", "y"), ("z", "y"), ("x", "z", "y"))


def cube_collect_scratch(high, wide):
    return [
        pltpu.VMEM((8, high // 2, wide), LOW),
        pltpu.VMEM((8, high // 2, wide), LOW),
        pltpu.VMEM((4, high // 2, wide), LOW),
        pltpu.VMEM((4, high // 2, wide), LOW),
        DMA((3,)),
        DMA((3,)),
        DMA((7,)),
        DMA((8,)),
    ]


class CubeCollectRows:
    def __init__(self, cube, rows, out, pair_in, pair_sum, level_in, send, recv):
        self.cube, self.rows, self.out = cube, rows, out
        self.pair_in, self.pair_sum, self.level_in = pair_in, pair_sum, level_in
        self.send, self.recv = send, recv
        self.half = rows.shape[1] // 2
        self.mine = piece(cube.core, self.half)
        self.theirs = piece(1 - cube.core, self.half)

    def to(self, src, dst, index, rep, fsdp):
        remote(src, dst, self.send.at[index], self.recv.at[index], rep, fsdp).start()

    def start(self):
        cube = self.cube
        self.to(self.rows.at[:, self.theirs], self.pair_in, 0, cube.partner, cube.fsdp)

    def fold_pair(self):
        cube = self.cube
        arrived(self.pair_in, self.recv.at[0])
        self.pair_sum[...] = (
            self.rows[:, self.mine].astype(WIDE) + self.pair_in[...].astype(WIDE)
        ).astype(LOW)

        @pl.when(jnp.logical_not(cube.lends))
        def hand_over():
            self.to(self.pair_sum, self.level_in, 1, cube.rep, cube.far)

    def fold_level(self):
        cube = self.cube

        @pl.when(cube.lends)
        def close():
            arrived(self.level_in, self.recv.at[1])
            self.out[:, self.mine] = (
                self.pair_sum[...].astype(WIDE) + self.level_in[...].astype(WIDE)
            ).astype(LOW)
            place = self.out.at[:, self.mine]
            self.to(place, place, 2, *cube.near["y"])
            self.to(place, place, 3, cube.partner, cube.fsdp)

    def relay(self):
        cube = self.cube

        @pl.when(jnp.logical_not(cube.lends))
        def pass_on():
            place = self.out.at[:, self.mine]
            arrived(place, self.recv.at[2])
            self.to(place, place, 3, cube.partner, cube.fsdp)

    def finish(self):
        arrived(self.out.at[:, self.theirs], self.recv.at[3])
        arrived(self.pair_in, self.send.at[0])
        arrived(self.pair_in, self.send.at[3])
        pl.when(self.cube.lends)(lambda: arrived(self.pair_in, self.send.at[2]))
        pl.when(jnp.logical_not(self.cube.lends))(lambda: arrived(self.pair_in, self.send.at[1]))


def cube_collect_rows_scratch(tall):
    return [pltpu.VMEM((tall, D // 2), LOW)] * 3 + [DMA((4,)), DMA((4,))]


def low_shape(*shape):
    return jax.ShapeDtypeStruct(shape, LOW)


def wide_shape(*shape):
    return jax.ShapeDtypeStruct(shape, WIDE)


def scratch_of(hidden):
    low, wide = (lambda *shape: pltpu.VMEM(shape, LOW)), (lambda *shape: pltpu.VMEM(shape, WIDE))
    single = {
        "marks": wide(8, 1024),
        "small": wide(8, 128),
        "cosine_step": wide(64, 128),
        "sine_step": wide(64, 128),
        "rows_full": low(8, 128, 1024),
        "firsts_full": low(8, 128, 128),
        "weights": low(8, 128, 384),
        "packed": low(8, 128, 768),
        "packed_full": low(8, 128, 768),
        "grad_full": low(8, 128, 1024),
        "hidden_one": low(8, 128, 1024),
        "queries": low(1024, 128),
        "keys": low(1024, 128),
        "keys_turned": low(128, 1024),
        "values": low(1024, 128),
        "values_turned": low(128, 1024),
        "attended": low(1024, 128),
        "totals": wide(1024, 128),
        "middle": wide(128, 1024),
        "hidden_two": low(128, 1024),
        "hidden_full": low(8, 128, 1024),
        "active": low(1024, 384),
        "both": low(1024, 768),
        "down_pad": low(384, 1024),
        "part": low(8, 128, 1024),
        "out_part": low(8, 128, 1024),
        "total": wide(128, 1024),
        "middle_grad": wide(128, 1024),
        "branch": low(128, 1024),
        "gain_two_term": wide(1, 1024),
        "down_grad": low(hidden, 1024),
        "branch_full": low(8, 128, 1024),
        "out_grad": low(1024, 128),
        "query_grad": wide(1024, 128),
        "key_acc": wide(128, 1024),
        "value_acc": wide(128, 1024),
        "three": low(1024, 384),
        "qkv_grads": low(8, 128, 384),
        "qkv_out": low(8, 128, 384),
        "packed_out": low(8, 128, 768),
        "output_grad": low(128, 1024),
        "gain_own": wide(8, 8, 128),
        "gain_in": wide(8, 8, 128),
        "gain_part": wide(8, 128),
        "gain_rep": wide(4, 8, 128),
        "value_blocks": low(8, 128, 128),
        "gate_weight": low(128, 8 * hidden),
        "up_weight": low(128, 8 * hidden),
        "down": low(hidden, 1024),
        "layer_output": low(128, 1024),
        "input_grad": wide(128, 1024),
        "firsts_grad": low(128, 1024),
        "output_out": low(128, 1024),
        "two": low(2, 128, 8 * hidden),
        "down_out": low(hidden, 1024),
        "gains": wide(8, 128),
        "fetch": DMA((3,)),
        "finals": DMA((32,)),
        "keep": DMA((6,)),
        "w_send": DMA((3, 7)),
        "w_recv": DMA((3, 8)),
        "p_send": DMA((7,)),
        "p_recv": DMA((8,)),
        "s_send": DMA((7,)),
        "s_recv": DMA((8,)),
        "f_send": DMA((7,)),
        "f_recv": DMA((8,)),
        "m_send": DMA((7,)),
        "m_recv": DMA((8,)),
        "mp_send": DMA((7,)),
        "mp_recv": DMA((8,)),
        "g_send": DMA((7,)),
        "g_recv": DMA((8,)),
        "gr_send": DMA((3,)),
        "gr_recv": DMA((4,)),
        "v_send": DMA((7,)),
        "v_recv": DMA((8,)),
        "d_send": DMA((2,)),
        "d_recv": DMA((2,)),
    }
    groups = {
        "sums_one": sums_scratch(),
        "sums_two": cube_sums_scratch(),
        "sums_out": cube_sums_scratch(),
        "sums_three": sums_scratch(),
        "row_flow": rows_sems(),
        "grad_flow": cube_rows_sems(),
        "hidden_flow": cube_rows_sems(),
        "branch_flow": rows_sems(),
        "packed_flow": cube_collect_scratch(128, 768),
        "qkv_flow": collect_scratch(128, 384),
        "down_flow": cube_collect_rows_scratch(hidden),
        "output_flow": collect_rows_scratch(128),
    }
    return single, groups


def layer_kernel(
    hidden,
    rows,
    firsts,
    prefix,
    positions,
    first_gain,
    query_weight,
    key_weight,
    value_weight,
    output_weight,
    second_gain,
    gate_far,
    up_far,
    down_far,
    cotangent,
    layer_final,
    input_final,
    five_final,
    two_final,
    down_final,
    gains_final,
    *refs,
):
    single, groups = scratch_of(hidden)
    s = types.SimpleNamespace(**dict(zip(single, refs)))
    refs = list(refs[len(single) :])
    for name, shapes in groups.items():
        setattr(s, name, refs[: len(shapes)])
        refs = refs[len(shapes) :]
    rep, fsdp, z, x = plane_place()
    core, level = lax.rem(rep, 2), rep // 2
    partner = rep + 1 - 2 * core
    above = rep + 2 - 4 * level
    slant = 3 - rep
    others = [lax.rem(fsdp + k, 8) for k in range(1, 8)]
    gate_weight, up_weight, down = s.gate_weight, s.up_weight, s.down
    firsts_grad, output_out, down_out = s.firsts_grad, s.output_out, s.down_out
    fetched = []
    for k, (src, dst) in enumerate(((gate_far, gate_weight), (up_far, up_weight), (down_far, down))):
        fetched.append(pltpu.make_async_copy(src, dst, s.fetch.at[k]))
        fetched[k].start()
    saved = []

    def save(src, dst):
        copy = pltpu.make_async_copy(src, dst, s.finals.at[len(saved)])
        copy.start()
        saved.append(copy)

    cube = Cube()
    greet(
        [(rep, other) for other in others]
        + [(partner, fsdp), (above, fsdp), (slant, fsdp)]
        + [cube.device("y", "x"), cube.device("y", "z"), cube.device("y", "z", "x")]
        + [(above, cube.far)]
    )
    mine = piece(core, 64)
    theirs = piece(1 - core, 64)
    started, kept = [], []
    row_flow = Rows(rows, s.rows_full, *s.row_flow)
    grad_flow = CubeRows(cube, SPARING, cotangent, s.grad_full, *s.grad_flow)
    hidden_flow = CubeRows(cube, THIRDS, s.hidden_two, s.hidden_full, *s.hidden_flow)
    branch_flow = Rows(s.branch, s.branch_full, *s.branch_flow)
    sums_one, sums_three = Sums(s.total, *s.sums_one), Sums(s.total, *s.sums_three)
    sums_two = CubeSums(cube, THIRDS, s.part, s.total, *s.sums_two)
    sums_out = CubeSums(cube, LATER, s.out_part, s.total, *s.sums_out)
    packed_flow = CubeCollect(cube, s.packed, s.packed_out, *s.packed_flow)
    qkv_flow = Collect(s.qkv_grads, s.qkv_out, *s.qkv_flow)
    down_flow = CubeCollectRows(cube, s.down_grad, down_out, *s.down_flow)
    output_flow = CollectRows(s.output_grad, output_out, *s.output_flow)

    def go(copy):
        copy.start()
        started.append(copy)

    def here(src, dst):
        copy = pltpu.make_async_copy(src, dst, s.keep.at[len(kept)])
        copy.start()
        kept.append(copy)

    sources = (query_weight, key_weight, value_weight)
    for k, other in enumerate(others):
        for i, source in enumerate(sources):
            go(
                remote(
                    source.at[mine, piece(other, 128)],
                    s.weights.at[fsdp, mine, pl.ds(128 * i, 128)],
                    s.w_send.at[i, k],
                    s.w_recv.at[i, fsdp],
                    rep,
                    other,
                )
            )
    row_flow.start()
    rates = turn_rates()
    place_row = positions[...].astype(WIDE)
    lane = lax.broadcasted_iota(jnp.int32, (1, 128), 1)
    s.small[0:1, :] = place_row
    s.small[1:2, :] = first_gain[...].astype(WIDE)
    s.small[2:3, :] = second_gain[...].astype(WIDE)
    for run in range(2):
        begin = jnp.sum(jnp.where(lane == 64 * run, place_row, 0.0), axis=1, keepdims=True)
        s.small[3 + 2 * run : 4 + 2 * run, :] = jnp.cos(begin * rates)
        s.small[4 + 2 * run : 5 + 2 * run, :] = jnp.sin(begin * rates)
    s.small[7:8, :] = jnp.zeros((1, 128), WIDE)
    for k, other in enumerate(others):
        go(
            remote(
                s.small, s.marks.at[:, piece(fsdp, 128)], s.s_send.at[k], s.s_recv.at[fsdp], rep, other
            )
        )
    for k, other in enumerate(others):
        go(
            remote(
                firsts.at[:, piece(other, 128)],
                s.firsts_full.at[fsdp],
                s.f_send.at[k],
                s.f_recv.at[fsdp],
                rep,
                other,
            )
        )
    grad_flow.start()
    for i, source in enumerate(sources):
        here(source.at[:, piece(fsdp, 128)], s.weights.at[fsdp, :, pl.ds(128 * i, 128)])
    here(s.small, s.marks.at[:, piece(fsdp, 128)])
    here(firsts.at[:, piece(fsdp, 128)], s.firsts_full.at[fsdp])
    angles = lax.broadcasted_iota(jnp.int32, (64, 128), 0).astype(WIDE) * rates
    s.cosine_step[...] = jnp.cos(angles)
    s.sine_step[...] = jnp.sin(angles)
    for copy in fetched:
        copy.wait()
    pad = jnp.zeros((128, 384 - hidden), LOW)
    for i in range(8):
        s.packed[i, :, 0:hidden] = gate_weight[:, hidden * i : hidden * (i + 1)]
        s.packed[i, :, hidden:384] = pad
        s.packed[i, :, 384 : 384 + hidden] = up_weight[:, hidden * i : hidden * (i + 1)]
        s.packed[i, :, 384 + hidden : 768] = pad
    here(s.packed.at[cube.own], s.packed_full.at[fsdp])

    row_flow.pass_on(0)
    for k, other in enumerate(others):
        for i in range(3):
            arrived(s.weights.at[other, mine, pl.ds(128 * i, 128)], s.w_recv.at[i, other])
        place = s.weights.at[other, mine]
        go(remote(place, place, s.p_send.at[k], s.p_recv.at[other], partner, fsdp))
    row_flow.pass_on(1)
    grad_flow.relay_one()
    for other in others:
        arrived(s.marks.at[:, piece(other, 128)], s.s_recv.at[other])
    for copy in kept:
        copy.wait()
    row_flow.kept()
    for other in others:
        arrived(s.weights.at[other, theirs], s.p_recv.at[other])
        arrived(s.firsts_full.at[other], s.f_recv.at[other])

    def project(block):
        entry = s.rows_full[block].astype(WIDE)
        scale = lax.rsqrt(jnp.mean(entry * entry, axis=-1, keepdims=True) + epsilon)
        low = (entry * scale * s.marks[1:2, :]).astype(LOW)
        s.hidden_one[block] = low
        pre = matmul(low, s.weights[...].reshape(8 * 128, 384))
        cosine, sine = turn_tables(s.marks, block, s.cosine_step, s.sine_step)
        at = piece(block, 128)
        s.queries[at, :] = turn(pre[:, :128], cosine, sine).astype(LOW)
        key = turn(pre[:, 128:256], cosine, sine)
        s.keys[at, :] = key.astype(LOW)
        s.keys_turned[:, at] = key.T.astype(LOW)
        value = 0.5 * pre[:, 256:] + 0.5 * s.firsts_full[block].astype(WIDE)
        s.values[at, :] = value.astype(LOW)
        s.values_turned[:, at] = value.T.astype(LOW)

    def project_column(k, carry):
        @pl.when(k == 2)
        def hand_on():
            row_flow.pass_on(2)

        project(2 * row_flow.line(k) + x)
        return carry

    def project_across(k, carry):
        project(row_flow.across(lax.rem(z + k, 4)))
        return carry

    project(fsdp)
    lax.fori_loop(0, 3, project_column, 0)
    grad_flow.relay_two()
    for k, other in enumerate(others):
        go(
            remote(
                s.packed.at[other % 4 + 4 * cube.y, mine],
                s.packed_full.at[fsdp, mine],
                s.m_send.at[k],
                s.m_recv.at[fsdp],
                rep,
                other,
            )
        )
    used = hidden // 2
    down_half = piece(core, used)
    s.down_pad[hidden:384, :] = jnp.zeros((384 - hidden, D), LOW)

    @pl.when(cube.lends)
    def lend():
        s.down_pad[0:hidden, :] = down[...]

    gives_down = (cube.lends & (core == 0)) | (jnp.logical_not(cube.lends) & (core == 1))

    @pl.when(gives_down)
    def give_down():
        remote(
            down.at[down_half],
            s.down_pad.at[down_half],
            s.d_send.at[0],
            s.d_recv.at[0],
            rep + core * (above - rep),
            cube.far,
        ).start()

    lax.fori_loop(0, 4, project_across, 0)
    prefix_last = (prefix[rep] - 1).astype(WIDE)
    masks = [head_lanes(head) for head in range(2)]

    def attend(block):
        at = piece(block, 128)
        query = s.queries[at, :]
        allowed = s.marks[0:1, :] <= limit_column(s.marks, block, prefix_last)
        result = total = None
        for head in range(2):
            scores = matmul(only(masks[head], query), s.keys_turned[...]) * E ** (-0.5)
            scores = jnp.where(allowed, scores, masked_score)
            top = jnp.max(scores, axis=-1, keepdims=True)
            weight = jnp.exp(scores - top)
            below = jnp.sum(weight, axis=-1, keepdims=True)
            probabilities = (weight * (1.0 / below)).astype(LOW)
            out = matmul(probabilities, s.values[...])
            log_total = jnp.broadcast_to(top + jnp.log(below), out.shape)
            result = out if head == 0 else jnp.where(masks[0], result, out)
            total = log_total if head == 0 else jnp.where(masks[0], total, log_total)
        s.totals[at, :] = total
        low = result.astype(LOW)
        s.attended[at, :] = low
        return matmul(low, output_weight[...])

    def attend_across(k, carry):
        other = sums_one.other(k)
        s.part[other] = attend(2 * other + 1 - x).astype(LOW)
        sums_one.give(k, s.part.at[other])

        return carry

    lax.fori_loop(0, 4, attend_across, 0)
    for k, other in enumerate(others):
        place = s.packed_full.at[other, mine]
        arrived(place, s.m_recv.at[other])
        go(remote(place, place, s.mp_send.at[k], s.mp_recv.at[other], partner, fsdp))

    @pl.when(jnp.logical_not(cube.lends))
    def borrow():
        place = s.down_pad.at[down_half]
        arrived(place, s.d_recv.at[0])
        remote(place, place, s.d_send.at[1], s.d_recv.at[1], partner, fsdp).start()

    def attend_column(k, carry):
        sums_one.forward(k, attend(2 * sums_one.other(k) + x))
        return carry

    lax.fori_loop(0, 3, attend_column, 0)
    total = rows[...].astype(WIDE) + sums_one.total(attend(fsdp))
    s.middle[...] = total
    scale = lax.rsqrt(jnp.mean(total * total, axis=-1, keepdims=True) + epsilon)
    s.hidden_two[...] = (total * scale * s.marks[2:3, :]).astype(LOW)

    hidden_flow.start()
    grad_flow.close_by()
    grad_flow.further()
    grad_flow.last()
    grad_flow.kept()

    @pl.when(jnp.logical_not(cube.lends))
    def borrowed():
        arrived(s.down_pad.at[piece(1 - core, used)], s.d_recv.at[1])

    for other in others:
        arrived(s.packed_full.at[other, theirs], s.mp_recv.at[other])

    def feed(block):
        at = piece(block, 128)
        packed = s.packed_full[...].reshape(8 * 128, 768)
        pre = matmul(s.hidden_full[block], packed)
        gate, up = pre[:, :384], pre[:, 384:]
        sigmoid = 1.0 / (1.0 + jnp.exp(-gate))
        swish = gate * sigmoid
        act = (swish * up).astype(LOW)
        s.active[at, :] = act
        act_grad = times_transposed(s.grad_full[block], s.down_pad[...])
        gate_grad = act_grad * up * sigmoid * (1.0 + gate * (1.0 - sigmoid))
        s.both[at, 0:384] = gate_grad.astype(LOW)
        s.both[at, 384:768] = (act_grad * swish).astype(LOW)
        s.part[block] = times_transposed(s.both[at, :], packed).astype(LOW)
        s.out_part[block] = matmul(act, s.down_pad[...]).astype(LOW)

    sums_one.sent()
    hidden_flow.kept()

    def feed_near(i, carry):
        @pl.when(i == 1)
        def first_wait():
            hidden_flow.relay_one()
            hidden_flow.close_by()

        pl.when(i == 2)(hidden_flow.relay_two)
        step = i + i // 3
        block = cube.own + step - 2 * step * (cube.own // (step + (3 - i) // 3) % 2)
        feed(block)
        for i_now, t in ((1, 1), (2, 0), (3, 2)):
            pl.when(i == i_now)(functools.partial(sums_two.give, t, block))
        return carry

    def feed_far(j, carry):
        pl.when(j == 0)(hidden_flow.further)
        pl.when(j == 3)(hidden_flow.last)
        i = (j + 1) % 4
        step = i + i // 3
        base = 7 - cube.own
        block = base + step - 2 * step * (base // (step + (3 - i) // 3) % 2)
        feed(block)
        for j_not, t in ((1, 0), (0, 1), (2, 2)):
            pl.when(j != j_not)(functools.partial(sums_two.give, t, block))
        return carry

    lax.fori_loop(0, 4, feed_near, 0)
    lax.fori_loop(0, 4, feed_far, 0)

    def feed_grads(i, carry):
        turned = s.hidden_full[:, :, piece(i, 128)].reshape(8 * 128, 128)
        s.packed[i] = transposed_times(turned, s.both[...]).astype(LOW)
        return carry

    for copy in started:
        copy.wait_send()

    lax.fori_loop(0, 3, feed_grads, 0)
    sums_two.fold_one()
    lax.fori_loop(3, 6, feed_grads, 0)
    sums_two.fold_two()
    lax.fori_loop(6, 8, feed_grads, 0)
    sums_two.finish()
    hidden_grad = s.total[...]
    entry = s.middle[...]
    scale = lax.rsqrt(jnp.mean(entry * entry, axis=-1, keepdims=True) + epsilon)
    normed = entry * scale
    normed_grad = hidden_grad * s.marks[2:3, :]
    back = scale * (normed_grad - normed * jnp.mean(normed_grad * normed, axis=-1, keepdims=True))
    grad = cotangent[...].astype(WIDE) + back
    s.branch[...] = grad.astype(LOW)
    branch_flow.start()
    s.middle_grad[...] = grad
    s.gain_two_term[...] = jnp.sum(hidden_grad * normed, axis=0, keepdims=True)

    def pull(block):
        s.out_grad[piece(block, 128), :] = times_transposed(
            s.branch_full[block], output_weight[...]
        ).astype(LOW)

    packed_flow.start()
    down_sum = transposed_times(s.active[...], s.grad_full[...].reshape(8 * 128, D))
    s.down_grad[...] = down_sum[0:hidden].astype(LOW)
    down_flow.start()
    branch_flow.kept()
    s.key_acc[...] = jnp.zeros_like(s.key_acc)
    s.value_acc[...] = jnp.zeros_like(s.value_acc)

    def attend_back(block):
        at = piece(block, 128)
        pull(block)
        query, grad = s.queries[at, :], s.out_grad[at, :]
        log_total = s.totals[at, :]
        allowed = s.marks[0:1, :] <= limit_column(s.marks, block, prefix_last)
        result = None
        lows, score_grads, turned_queries, turned_grads = [], [], [], []
        for head in range(2):
            query_here, grad_here = only(masks[head], query), only(masks[head], grad)
            scores = matmul(query_here, s.keys_turned[...]) * E ** (-0.5)
            column = log_total[:, head * E : head * E + 1]
            probabilities = jnp.where(allowed, jnp.exp(scores - column), 0.0)
            prob_grad = matmul(grad_here, s.values_turned[...])
            delta = jnp.sum(probabilities * prob_grad, axis=-1, keepdims=True)
            score_grad = (probabilities * (prob_grad - delta)).astype(LOW)
            out = matmul(score_grad, s.keys[...])
            result = out if head == 0 else jnp.where(masks[0], result, out)
            lows.append(probabilities.astype(LOW))
            score_grads.append(score_grad)
            turned_queries.append(query_here.astype(WIDE).T)
            turned_grads.append(grad_here.astype(WIDE).T)
        s.query_grad[at, :] = result
        s.key_acc[...] += matmul(
            jnp.concatenate(turned_queries, axis=1).astype(LOW),
            jnp.concatenate(score_grads, axis=0),
        )
        s.value_acc[...] += matmul(
            jnp.concatenate(turned_grads, axis=1).astype(LOW), jnp.concatenate(lows, axis=0)
        )


    def back_column(k, carry):
        @pl.when(k > 0)
        def hand_on():
            branch_flow.pass_on(k - 1)

        first = 1 - (k + 2) // 3
        other = branch_flow.line(k - 1 + first)
        attend_back(2 * (other + first * (z - other)) + x)
        return carry

    def back_across(k, carry):
        attend_back(branch_flow.across(lax.rem(z + k, 4)))
        return carry

    lax.fori_loop(0, 4, back_column, 0)
    sums_out.give_all()
    lax.fori_loop(0, 4, back_across, 0)
    packed_flow.fold_pair()
    down_flow.fold_pair()

    def close(block):
        at = piece(block, 128)
        cosine, sine = turn_tables(s.marks, block, s.cosine_step, s.sine_step)
        s.three[at, 0:128] = turn(s.query_grad[at, :] * E ** (-0.5), cosine, -sine).astype(LOW)
        s.three[at, 128:256] = turn(s.key_acc[:, at].T * E ** (-0.5), cosine, -sine).astype(LOW)
        value_grad = (0.5 * s.value_acc[:, at].T).astype(LOW)
        s.three[at, 256:384] = value_grad
        s.value_blocks[block] = value_grad
        return times_transposed(s.three[at, :], s.weights[...].reshape(8 * 128, 384))

    def close_across(k, carry):
        other = sums_three.other(k)
        block = 2 * other + 1 - x
        s.part[block] = close(block).astype(LOW)
        sums_three.give(k, s.part.at[block])
        return carry

    def close_column(k, carry):
        block = 2 * sums_three.other(k) + x
        s.part[block] = close(block).astype(LOW)
        return carry

    sums_two.sent()
    lax.fori_loop(0, 4, close_across, 0)
    lax.fori_loop(0, 4, close_column, 0)
    for k, other in enumerate(others):
        remote(
            s.value_blocks.at[other],
            firsts_grad.at[:, piece(fsdp, 128)],
            s.v_send.at[k],
            s.v_recv.at[fsdp],
            rep,
            other,
        ).start()
    firsts_grad[:, piece(fsdp, 128)] = s.value_blocks[fsdp]

    def qkv_grads(i, carry):
        turned = s.hidden_one[:, :, piece(i, 128)].reshape(8 * 128, 128)
        s.qkv_grads[i] = transposed_times(turned, s.three[...]).astype(LOW)
        return carry

    lax.fori_loop(0, 8, qkv_grads, 0)
    qkv_flow.start()
    s.output_grad[...] = transposed_times(
        s.attended[...], s.branch_full[...].reshape(8 * 128, D)
    ).astype(LOW)
    output_flow.start()
    def onward(k):
        sums_three.forward(k, s.part[2 * sums_three.other(k) + x].astype(WIDE))

    onward(0)
    qkv_flow.fold_pair()
    sums_out.fold_one()
    packed_flow.fold_level()
    onward(1)
    output_flow.fold_pair()
    onward(2)
    down_flow.fold_level()
    qkv_flow.fold_level()
    sums_out.fold_two()
    output_flow.fold_level()
    packed_flow.land()
    down_flow.relay()
    packed_flow.finish()
    for i in range(8):
        wide = slice(hidden * i, hidden * (i + 1))
        s.two[0, :, wide] = s.packed_out[i, :, 0:hidden]
        s.two[1, :, wide] = s.packed_out[i, :, 384 : 384 + hidden]
    save(s.two, two_final)
    sums_out.finish()
    s.layer_output[...] = (s.middle[...] + s.total[...]).astype(LOW)
    save(s.layer_output, layer_final)
    output_flow.relay()
    qkv_flow.land()
    hidden_grad = sums_three.total(s.part[fsdp].astype(WIDE))
    entry = rows[...].astype(WIDE)
    scale = lax.rsqrt(jnp.mean(entry * entry, axis=-1, keepdims=True) + epsilon)
    normed = entry * scale
    normed_grad = hidden_grad * s.marks[1:2, :]
    gain_term = jnp.sum(hidden_grad * normed, axis=0, keepdims=True)
    for i in range(8):
        lanes = slice(128 * i, 128 * i + 128)
        s.gain_own[i, 0:1, :] = gain_term[:, lanes]
        s.gain_own[i, 1:2, :] = s.gain_two_term[:, lanes]
        s.gain_own[i, 2:8, :] = jnp.zeros((6, 128), WIDE)
    for k, other in enumerate(others):
        remote(
            s.gain_own.at[other], s.gain_in.at[fsdp], s.g_send.at[k], s.g_recv.at[fsdp], rep, other
        ).start()
    back = scale * (normed_grad - normed * jnp.mean(normed_grad * normed, axis=-1, keepdims=True))
    s.input_grad[...] = s.middle_grad[...] + back
    save(s.input_grad, input_final)
    qkv_flow.relay()
    s.gain_in[fsdp] = s.gain_own[fsdp]
    for other in others:
        arrived(s.gain_in.at[other], s.g_recv.at[other])
    s.gain_part[...] = jnp.sum(s.gain_in[...], axis=0)
    for k, target in enumerate((partner, above, slant)):
        remote(
            s.gain_part, s.gain_rep.at[rep], s.gr_send.at[k], s.gr_recv.at[rep], target, fsdp
        ).start()
    s.gain_rep[rep] = s.gain_part[...]
    for k, other in enumerate(others):
        arrived(firsts_grad.at[:, piece(other, 128)], s.v_recv.at[other])
    save(firsts_grad, five_final.at[0])
    down_flow.finish()
    save(down_out, down_final)
    output_flow.finish()
    save(output_out, five_final.at[4])
    qkv_flow.finish()
    for i in range(8):
        for k in range(3):
            save(
                s.qkv_out.at[i, :, pl.ds(128 * k, 128)],
                five_final.at[1 + k, :, pl.ds(128 * i, 128)],
            )
    for k in range(7):
        arrived(s.value_blocks.at[0], s.v_send.at[k])
        arrived(s.gain_own.at[0], s.g_send.at[k])
    for k, source in enumerate((partner, above, slant)):
        arrived(s.gain_rep.at[source], s.gr_recv.at[source])
        arrived(s.gain_part, s.gr_send.at[k])
    s.gains[...] = jnp.sum(s.gain_rep[...], axis=0)
    save(s.gains, gains_final)
    pl.when(gives_down)(lambda: arrived(s.down_pad.at[down_half], s.d_send.at[0]))
    pl.when(jnp.logical_not(cube.lends))(lambda: arrived(s.down_pad.at[down_half], s.d_send.at[1]))
    for flow in (row_flow, grad_flow, hidden_flow, branch_flow):
        flow.sent()
    for sums in (sums_out, sums_three):
        sums.sent()
    for copy in saved:
        copy.wait()


def shards_plane(
    inputs,
    first_values,
    prefix,
    positions,
    first_gain,
    query_weight,
    key_weight,
    value_weight,
    output_weight,
    second_gain,
    gate_weight,
    up_weight,
    down_weight,
    cotangent,
):
    hidden = down_weight.shape[0]
    single, groups = scratch_of(hidden)
    outs = pl.pallas_call(
        functools.partial(layer_kernel, hidden),
        out_shape=[
            low_shape(128, D),
            wide_shape(128, D),
            low_shape(5, 128, D),
            low_shape(2, 128, 8 * hidden),
            low_shape(hidden, D),
            wide_shape(8, 128),
        ],
        in_specs=[VM, VM, SM] + [VM] * 7 + [FAR] * 3 + [VM],
        out_specs=[FAR] * 6,
        scratch_shapes=list(single.values()) + [shape for group in groups.values() for shape in group],
        compiler_params=pltpu.CompilerParams(
            collective_id=1, has_side_effects=True, vmem_limit_bytes=LIMIT
        ),
    )(
        inputs,
        first_values,
        prefix,
        positions[None],
        first_gain[None],
        query_weight,
        key_weight,
        value_weight,
        output_weight,
        second_gain[None],
        gate_weight,
        up_weight,
        down_weight,
        cotangent,
    )
    layer_output, input_grad, five, two, down, gains = outs
    firsts, query, key, value, output = [five[i].astype(WIDE) for i in range(5)]
    gate, up = [two[i].astype(WIDE) for i in range(2)]
    down = down.astype(WIDE)
    return (
        layer_output,
        input_grad,
        firsts,
        gains[0],
        query,
        key,
        value,
        output,
        gains[1],
        gate,
        up,
        down,
    )


def pick_body(mesh):
    if mesh.shape["fsdp"] == 8 and mesh.shape["rep"] == 4:
        return shards_plane
    return shards_general


def solution(mesh):
    placed = (
        P(("rep", "fsdp"), None),
        P(("rep", "fsdp"), None),
        P(),
        P(("rep", "fsdp")),
        P("fsdp"),
        P("fsdp", None),
        P("fsdp", None),
        P("fsdp", None),
        P("fsdp", None),
        P("fsdp"),
        P("fsdp", None),
        P("fsdp", None),
        P("fsdp", None),
        P(("rep", "fsdp"), None),
    )
    return jax.shard_map(
        pick_body(mesh),
        mesh=mesh,
        in_specs=placed,
        out_specs=(
            P(("rep", "fsdp"), None),
            P(("rep", "fsdp"), None),
            P(("rep", "fsdp"), None),
            P("fsdp"),
            P("fsdp", None),
            P("fsdp", None),
            P("fsdp", None),
            P("fsdp", None),
            P("fsdp"),
            P("fsdp", None),
            P("fsdp", None),
            P("fsdp", None),
        ),
        check_vma=False,
    )
```
